128 devices in a mesh: batch: 4 (over y_lo, core), tensor: 8 (over x, y_hi), latent: 4 (over z).
Axes of the slice: x: 4, y: 4 (y_hi: 2, y_lo: 2; y = y_hi * 2 + y_lo), z: 4, core: 2. Of those that a mesh axis runs over, the one named last changes fastest.
Arguments:
- residual: bfloat16 [1024, 3584], P('batch', ('tensor', 'latent')), may hold values from -6 to 6
- target: bfloat16 [1024, 3584], P('batch', ('tensor', 'latent')), may hold values from -6 to 6
- encoder_weight: bfloat16 [3584, 32768], P(None, ('tensor', 'latent')), may hold values from -0.09375 to 0.09375
- encoder_bias: bfloat16 [32768], P(('tensor', 'latent')), may hold values from -0.59765625 to 0.29882812
- decoder_weight: bfloat16 [32768, 3584], P(('tensor', 'latent')), may hold values from -0.09375 to 0.09375
- decoder_bias: bfloat16 [3584], replicated, may hold values from -3 to 3
- first_gain: bfloat16 [3584], replicated, may hold values from 0.5 to 1.5
- second_gain: bfloat16 [3584], replicated, may hold values from 0.5 to 1.5
- gate_weight: bfloat16 [3584, 7168], P(None, ('tensor', 'latent')), may hold values from -0.09375 to 0.09375
- up_weight: bfloat16 [3584, 7168], P(None, ('tensor', 'latent')), may hold values from -0.09375 to 0.09375
- down_weight: bfloat16 [7168, 3584], P(('tensor', 'latent')), may hold values from -0.125 to 0.125
Outputs:
- encoder_grad: bfloat16 [3584, 32768], P('batch', ('tensor', 'latent'))
- decoder_grad: bfloat16 [32768, 3584], P(('tensor', 'latent'), 'batch')
The draws below stay inside these ranges and needn't reach their ends.
All inputs are finite; a program needn't handle non-finite values.
Results may differ from the reference program's by a relative error of at most 0.012.
The reference program's roundings to bfloat16 on the way (of `centered`, `latents`, `normed_input`, `hidden`, `grad_output`, `grad_recon` and `grad_preact`) count: a program that leaves them out, or rounds other values in their place, can miss the bound.
Values may be sent and summed in bfloat16 or wider, within the bound.
No kernel may reach another device: no remote copies, remote signals or barrier semaphores. Data moves between devices by JAX's collectives and lax.ppermute only.
A program may use at most 128 MiB of HBM per device.

```python
import jax
import jax.numpy as jnp
from jax import lax

D = 3584
FF = 7168
LAT = 32768
TOKENS = 1024


def raised(values, own_key, source, target, parts, factor):
    def block_of(axis_at):
        return (jnp.arange(values.shape[axis_at]) // (values.shape[axis_at] // parts)).reshape((-1,) + (1,) * (values.ndim - 1 - axis_at))

    first = jax.random.permutation(own_key, parts)[block_of(target)]
    far = (block_of(target) + parts // 2) % parts
    return jnp.where((block_of(source) == first) | (block_of(source) == far), factor * values, values)


def shard_levels(key, extent, split, smallest, top_value):
    level = 1.0
    for dim, parts in split:
        heights = jax.random.uniform(jax.random.fold_in(jax.random.fold_in(key, 6), dim), (parts,), jnp.float32, smallest / len(split), top_value / len(split))
        level = level * jnp.repeat(jnp.exp(heights), extent[dim] // parts).reshape((-1,) + (1,) * (len(extent) - 1 - dim))
    return level


def scatter_about(rng, extent, width, reach, cuts=(), dtype=jnp.bfloat16):
    values = width * jax.random.normal(rng, extent, jnp.float32)
    if cuts:
        values = values * shard_levels(rng, extent, cuts, -0.22, 0.18)
    return jnp.clip(values, -reach, reach).astype(dtype)


def gaussian_with(rng, shape, scale, reach, shards, heavy, kind=jnp.bfloat16):
    array = scale * jax.random.normal(rng, shape, jnp.float32)
    if shards:
        array = array * shard_levels(rng, shape, shards, -0.22, 0.18)
    return jnp.clip(raised(array, jax.random.fold_in(rng, 3), *heavy), -reach, reach).astype(kind)


def setup_inputs(seed: int = 0) -> dict:
    key_of = jax.random.split(jax.random.key(seed), 12)
    residual = scatter_about(key_of[0], (TOKENS, D), 1.0, 6.0, ((0, 4), (1, 32)))
    target = scatter_about(key_of[1], (TOKENS, D), 1.0, 6.0, ((0, 4), (1, 32)))
    encoder_weight = scatter_about(key_of[2], (D, LAT), D ** -0.5, 0.09375, ((1, 32),))
    encoder_bias = jnp.clip(-0.59765625 + 0.8964844 * jax.random.uniform(key_of[3], (LAT,), jnp.float32) ** shard_levels(key_of[3], (LAT,), ((0, 32),), -0.2, 0.2), -0.59765625, 0.29882812).astype(jnp.bfloat16)
    decoder_weight = gaussian_with(key_of[4], (LAT, D), (LAT // 2) ** -0.5, 0.09375, ((0, 32),), (0, 1, 32, 2.75))
    decoder_bias = scatter_about(key_of[5], (D,), 0.5, 3.0)
    first_gain = jnp.clip(1.0 + 0.1 * jax.random.normal(key_of[6], (D,), jnp.float32), 0.5, 1.5).astype(jnp.bfloat16)
    second_gain = jnp.clip(1.0 + 0.1 * jax.random.normal(key_of[7], (D,), jnp.float32), 0.5, 1.5).astype(jnp.bfloat16)
    gate_weight = scatter_about(key_of[8], (D, FF), D ** -0.5, 0.09375, ((1, 32),))
    up_weight = scatter_about(key_of[9], (D, FF), D ** -0.5, 0.09375, ((1, 32),))
    down_weight = gaussian_with(key_of[10], (FF, D), FF ** -0.5, 0.125, ((0, 32),), (0, 1, 32, 2.75))
    return dict(residual=residual, target=target, encoder_weight=encoder_weight, encoder_bias=encoder_bias, decoder_weight=decoder_weight, decoder_bias=decoder_bias, first_gain=first_gain, second_gain=second_gain, gate_weight=gate_weight, up_weight=up_weight, down_weight=down_weight)


epsilon = 1e-06

def reference(residual, target, encoder_weight, encoder_bias, decoder_weight, decoder_bias, first_gain, second_gain, gate_weight, up_weight, down_weight):
    f32 = jnp.float32
    bf16 = jnp.bfloat16
    contract_last = (((1,), (1,)), ((), ()))
    centered = (residual.astype(f32) - decoder_bias.astype(f32)).astype(bf16)
    preact = jnp.dot(centered, encoder_weight, preferred_element_type=f32) + encoder_bias.astype(f32)
    latents = jnp.maximum(preact, 0.0).astype(bf16)
    recon = jnp.dot(latents, decoder_weight, preferred_element_type=f32) + decoder_bias.astype(f32)
    scale_in = lax.rsqrt(lax.optimization_barrier(jnp.sum(recon * recon, axis=1, keepdims=True)) / D + epsilon)
    normed_input = (recon * scale_in * first_gain.astype(f32)).astype(bf16)
    gate_value = jnp.dot(normed_input, gate_weight, preferred_element_type=f32)
    up_value = jnp.dot(normed_input, up_weight, preferred_element_type=f32)
    gelu_value, gelu_back = jax.vjp(lambda v: jax.nn.gelu(v, approximate=True), gate_value)
    hidden = (gelu_value * up_value).astype(bf16)
    output = jnp.dot(hidden, down_weight, preferred_element_type=f32)
    scale_out = lax.rsqrt(lax.optimization_barrier(jnp.sum(output * output, axis=1, keepdims=True)) / D + epsilon)
    normed_out = output * scale_out
    result = recon + normed_out * second_gain.astype(f32)
    grad_result = 2.0 * (result - target.astype(f32)) / TOKENS
    grad_normed = grad_result * second_gain.astype(f32)
    inner_out = lax.optimization_barrier(jnp.sum(grad_normed * normed_out, axis=1, keepdims=True)) / D
    grad_output = (scale_out * (grad_normed - normed_out * inner_out)).astype(bf16)
    grad_hidden = lax.dot_general(grad_output, down_weight, contract_last, preferred_element_type=f32)
    grad_gate = gelu_back(grad_hidden * up_value)[0].astype(bf16)
    grad_up = (grad_hidden * gelu_value).astype(bf16)
    grad_normed_in = lax.dot_general(grad_gate, gate_weight, contract_last, preferred_element_type=f32)
    grad_normed_in = grad_normed_in + lax.dot_general(grad_up, up_weight, contract_last, preferred_element_type=f32)
    unit = recon * scale_in
    grad_unit = grad_normed_in * first_gain.astype(f32)
    inner_in = lax.optimization_barrier(jnp.sum(grad_unit * unit, axis=1, keepdims=True)) / D
    grad_recon = (grad_result + scale_in * (grad_unit - unit * inner_in)).astype(bf16)
    grad_latent = lax.dot_general(grad_recon, decoder_weight, contract_last, preferred_element_type=f32)
    grad_preact = jnp.where(preact > 0, grad_latent, 0.0).astype(bf16)
    contract_first = (((0,), (0,)), ((), ()))
    decoder_grad = lax.dot_general(latents, grad_recon, contract_first, preferred_element_type=f32)
    encoder_grad = lax.dot_general(centered, grad_preact, contract_first, preferred_element_type=f32)
    return (encoder_grad.astype(bf16), decoder_grad.astype(bf16))
```

```python
import jax
import jax.numpy as jnp
from jax import lax
from jax.sharding import Mesh
from jax.sharding import PartitionSpec as P

SHARDS = ("tensor_0", "tensor_1", "latent")
BATCH = ("batch_0", "batch_1")

epsilon = 1e-06


def exchange(pieces, axes):
    return lax.all_to_all(pieces, axes, split_axis=0, concat_axis=0, tiled=True)


def to_everyone(shard, axes):
    return exchange(jnp.broadcast_to(shard, (lax.axis_size(axes), *shard.shape)), axes)


def per_device(
    residual,
    target,
    encoder_weight,
    encoder_bias,
    decoder_weight,
    decoder_bias,
    first_gain,
    second_gain,
    gate_weight,
    up_weight,
    down_weight,
):
    f32 = jnp.float32
    bf16 = jnp.bfloat16
    contract_last = (((1,), (1,)), ((), ()))
    contract_first = (((0,), (0,)), ((), ()))
    tokens, share_width = residual.shape
    shards = lax.axis_size(SHARDS)
    copies = lax.axis_size(BATCH)
    width = share_width * shards
    own_tokens = tokens // shards
    token_count = tokens * copies
    offset = lax.axis_index(SHARDS) * share_width
    bias = decoder_bias.astype(f32)
    gain_in = first_gain.astype(f32)
    gain_out = second_gain.astype(f32)

    def sum_of_own_tokens(partial):
        pieces = partial.astype(bf16).reshape(shards, own_tokens, width)
        return exchange(pieces, SHARDS).astype(f32).sum(axis=0)

    def all_tokens(own):
        return to_everyone(own, SHARDS).reshape(tokens, width)

    bias_share = lax.dynamic_slice_in_dim(bias, offset, share_width)
    centered_share = (residual.astype(f32) - bias_share).astype(bf16)
    centered = to_everyone(centered_share.T, SHARDS).reshape(width, tokens)
    preact = lax.dot_general(centered, encoder_weight, contract_first, preferred_element_type=f32)
    preact = preact + encoder_bias.astype(f32)
    latents = jnp.maximum(preact, 0.0).astype(bf16)
    partial_recon = jnp.dot(latents, decoder_weight, preferred_element_type=f32)

    own_target = exchange(target.reshape(shards, own_tokens, share_width), SHARDS)
    own_target = jnp.moveaxis(own_target, 0, 1).reshape(own_tokens, width).astype(f32)
    recon = sum_of_own_tokens(partial_recon) + bias
    scale_in = lax.rsqrt(jnp.sum(recon * recon, axis=1, keepdims=True) / width + epsilon)
    unit = recon * scale_in
    normed_input = all_tokens((unit * gain_in).astype(bf16))

    latents_all = lax.all_gather(latents, BATCH, axis=0, tiled=True)
    centered_block = exchange(centered.reshape(copies, width // copies, tokens), BATCH)
    centered_block = jnp.moveaxis(centered_block, 0, 1).reshape(width // copies, token_count)

    gate_value = jnp.dot(normed_input, gate_weight, preferred_element_type=f32)
    up_value = jnp.dot(normed_input, up_weight, preferred_element_type=f32)
    gelu_value, gelu_back = jax.vjp(lambda v: jax.nn.gelu(v, approximate=True), gate_value)
    hidden = (gelu_value * up_value).astype(bf16)
    partial_out = jnp.dot(hidden, down_weight, preferred_element_type=f32)

    output = sum_of_own_tokens(partial_out)
    scale_out = lax.rsqrt(jnp.sum(output * output, axis=1, keepdims=True) / width + epsilon)
    normed_out = output * scale_out
    result = recon + normed_out * gain_out
    grad_result = 2.0 * (result - own_target) / token_count
    grad_normed = grad_result * gain_out
    inner_out = jnp.sum(grad_normed * normed_out, axis=1, keepdims=True) / width
    grad_output = all_tokens((scale_out * (grad_normed - normed_out * inner_out)).astype(bf16))

    grad_hidden = lax.dot_general(
        grad_output, down_weight, contract_last, preferred_element_type=f32
    )
    grad_gate = gelu_back(grad_hidden * up_value)[0].astype(bf16)
    grad_up = (grad_hidden * gelu_value).astype(bf16)
    partial_input = lax.dot_general(
        grad_gate, gate_weight, contract_last, preferred_element_type=f32
    )
    partial_input = partial_input + lax.dot_general(
        grad_up, up_weight, contract_last, preferred_element_type=f32
    )

    grad_unit = sum_of_own_tokens(partial_input) * gain_in
    inner_in = jnp.sum(grad_unit * unit, axis=1, keepdims=True) / width
    grad_recon = all_tokens((grad_result + scale_in * (grad_unit - unit * inner_in)).astype(bf16))

    grad_latent = lax.dot_general(
        grad_recon, decoder_weight, contract_last, preferred_element_type=f32
    )
    grad_preact = jnp.where(preact > 0, grad_latent, 0.0).astype(bf16)
    recon_block = lax.all_to_all(grad_recon, BATCH, split_axis=1, concat_axis=0, tiled=True)
    decoder_grad = lax.dot_general(
        latents_all, recon_block, contract_first, preferred_element_type=f32
    )
    preact_all = to_everyone(grad_preact, BATCH).reshape(token_count, -1)
    encoder_grad = jnp.dot(centered_block, preact_all, preferred_element_type=f32)
    return (encoder_grad.astype(bf16), decoder_grad.astype(bf16))


def solution(mesh):
    batch, latent = mesh.shape["batch"], mesh.shape["latent"]
    split = Mesh(
        mesh.devices.reshape(2, batch // 2, mesh.shape["tensor"] // 2, 2, latent),
        BATCH + SHARDS,
    )
    in_specs = (
        P(BATCH, SHARDS),
        P(BATCH, SHARDS),
        P(None, SHARDS),
        P(SHARDS),
        P(SHARDS, None),
        P(),
        P(),
        P(),
        P(None, SHARDS),
        P(None, SHARDS),
        P(SHARDS, None),
    )
    out_specs = (P(BATCH, SHARDS), P(SHARDS, BATCH))
    return jax.shard_map(
        per_device, mesh=split, in_specs=in_specs, out_specs=out_specs, check_vma=False
    )
```

```python
import functools

import jax
import jax.numpy as jnp
from jax import lax
from jax.experimental import pallas as pl
from jax.experimental.pallas import tpu as pltpu
from jax.sharding import Mesh
from jax.sharding import PartitionSpec as P

SHARDS = ("tensor_0", "tensor_1", "latent")
BATCH = ("batch_0", "batch_1")

epsilon = 1e-06

f32 = jnp.float32
bf16 = jnp.bfloat16
LAST = (((1,), (1,)), ((), ()))
WHOLE = pl.BlockSpec(memory_space=pltpu.VMEM)
LIMIT = 40 * 1024 * 1024


def exchange(pieces, axes):
    return lax.all_to_all(pieces, axes, split_axis=0, concat_axis=0, tiled=True)


def swap(block, axes):
    for_all = lax.axis_size(axes)
    return lax.ppermute(block, axes, [(i, for_all - 1 - i) for i in range(for_all)])


def copies_of_all(block):
    near = swap(block, BATCH[1])
    far = swap(block, BATCH[0])
    return [block, near, far, swap(far, BATCH[1])]


def blocks_of_all(block_at):
    own = lax.axis_index(BATCH)
    steps = ((1, BATCH[1]), (2, BATCH[0]), (3, BATCH))
    return [block_at(own)] + [swap(block_at(own ^ step), axes) for step, axes in steps]


def call(body, outs, flops, args, **more):
    moved = sum(a.size * a.dtype.itemsize for a in [*args, *jax.tree.leaves(outs)])
    cost = pl.CostEstimate(flops=flops, bytes_accessed=moved, transcendentals=0)
    return pl.pallas_call(
        body,
        out_shape=outs,
        cost_estimate=cost,
        compiler_params=pltpu.CompilerParams(vmem_limit_bytes=LIMIT),
        **more,
    )(*args)


def array(shape, dtype=bf16):
    return jax.ShapeDtypeStruct(shape, dtype)


def product(left, right):
    return jnp.dot(left, right, preferred_element_type=f32)


def product_t(left, right):
    return lax.dot_general(left, right, LAST, preferred_element_type=f32)


def encode_kernel(centered_ref, weight_ref, bias_ref, latents_ref, turned_ref, rows_ref):
    width = centered_ref.shape[0]

    @pl.when(pl.program_id(0) == 0)
    def _():
        for at in range(0, width, 256):
            rows_ref[:, at : at + 256] = centered_ref[at : at + 256, :].T

    preact = product(rows_ref[...], weight_ref[...]) + bias_ref[...].astype(f32)
    latents = jnp.maximum(preact, 0.0).astype(bf16)
    latents_ref[...] = latents
    turned_ref[...] = latents.T


def encode(centered, weight, bias, tile):
    width, tokens = centered.shape
    count = weight.shape[1]
    return call(
        encode_kernel,
        [array((tokens, count)), array((count, tokens))],
        2 * tokens * width * count,
        [centered, weight, bias.reshape(1, count)],
        grid=(count // tile,),
        in_specs=[
            WHOLE,
            pl.BlockSpec((width, tile), lambda j: (0, j)),
            pl.BlockSpec((1, tile), lambda j: (0, j)),
        ],
        out_specs=[
            pl.BlockSpec((tokens, tile), lambda j: (0, j)),
            pl.BlockSpec((tile, tokens), lambda j: (j, 0)),
        ],
        scratch_shapes=[pltpu.VMEM((tokens, width), bf16)],
    )


def decode_kernel(latents_ref, weight_ref, target_ref, out_ref):
    tile = weight_ref.shape[1]
    step = pl.program_id(0)
    at = pl.multiple_of(step * tile, tile)
    out_ref[:, pl.ds(at, tile)] = product(latents_ref[...], weight_ref[...]).astype(bf16)

    @pl.when(step == 0)
    def _():
        rows, tokens = target_ref.shape
        spare = -rows % 128
        padded = jnp.concatenate([target_ref[...], jnp.zeros((spare, tokens), bf16)], axis=0)
        out_ref[:, out_ref.shape[1] - rows - spare :] = padded.T


def decode(latents, weight, turned_target, room):
    tokens, count = latents.shape
    width = weight.shape[1]
    tile = width // 7
    return call(
        decode_kernel,
        array((tokens, width + room)),
        2 * tokens * width * count,
        [latents, weight, turned_target],
        grid=(7,),
        in_specs=[WHOLE, pl.BlockSpec((count, tile), lambda j: (0, j)), WHOLE],
        out_specs=WHOLE,
    )


def total_of(pieces_ref, width):
    total = pieces_ref[0, :, :width].astype(f32)
    for k in range(1, pieces_ref.shape[0]):
        total += pieces_ref[k, :, :width].astype(f32)
    return total


def send_to_all(out_ref, rows):
    for k in range(out_ref.shape[0]):
        out_ref[k] = rows


def mean_of(values):
    return jnp.sum(values, axis=1, keepdims=True) / values.shape[1]


def recon_kernel(pieces_ref, bias_ref, gain_ref, out_ref, recon_ref):
    recon = total_of(pieces_ref, recon_ref.shape[1]) + bias_ref[...].astype(f32)
    recon_ref[...] = recon
    scale_in = lax.rsqrt(mean_of(recon * recon) + epsilon)
    send_to_all(out_ref, (recon * scale_in * gain_ref[...].astype(f32)).astype(bf16))


def output_kernel(token_count, pieces_ref, recon_ref, target_ref, gain_ref, out_ref, grad_ref):
    gain = gain_ref[...].astype(f32)
    output = total_of(pieces_ref, recon_ref.shape[1])
    scale_out = lax.rsqrt(mean_of(output * output) + epsilon)
    normed_out = output * scale_out
    result = recon_ref[...] + normed_out * gain
    grad_result = 2.0 * (result - target_ref[...].astype(f32)) / token_count
    grad_ref[...] = grad_result
    grad_normed = grad_result * gain
    inner = mean_of(grad_normed * normed_out)
    send_to_all(out_ref, (scale_out * (grad_normed - normed_out * inner)).astype(bf16))


def input_kernel(pieces_ref, recon_ref, grad_ref, gain_ref, out_ref):
    recon = recon_ref[...]
    scale_in = lax.rsqrt(mean_of(recon * recon) + epsilon)
    unit = recon * scale_in
    grad_unit = total_of(pieces_ref, recon_ref.shape[1]) * gain_ref[...].astype(f32)
    inner = mean_of(grad_unit * unit)
    send_to_all(out_ref, (grad_ref[...] + scale_in * (grad_unit - unit * inner)).astype(bf16))


def local(body, outs, args):
    return call(body, outs, 0, args, in_specs=[WHOLE] * len(args), out_specs=[WHOLE] * len(outs))


def forward_kernel(rows_ref, gate_ref, up_ref, down_ref, out_ref, gelu_ref, slope_ref):
    gate_value = product_t(rows_ref[...], gate_ref[...])
    up_value = product_t(rows_ref[...], up_ref[...])
    root = 0.7978845608028654
    cube = 0.044715
    square = gate_value * gate_value
    curve = jnp.tanh(root * gate_value * (1.0 + cube * square))
    half = 0.5 * (1.0 + curve)
    gelu_value = gate_value * half
    rise = 0.5 * gate_value * (1.0 - curve * curve) * root * (1.0 + 3.0 * cube * square)
    gelu_ref[...] = gelu_value
    slope_ref[...] = up_value * (half + rise)
    hidden = (gelu_value * up_value).astype(bf16)
    for at in range(0, out_ref.shape[1], 512):
        out_ref[:, at : at + 512] = product(hidden, down_ref[:, at : at + 512]).astype(bf16)


def backward_kernel(
    rows_ref, gate_ref, up_ref, down_ref, gelu_ref, slope_ref, out_ref
):
    grad_hidden = product_t(rows_ref[...], down_ref[...])
    grad_gate = (grad_hidden * slope_ref[...]).astype(bf16)
    grad_up = (grad_hidden * gelu_ref[...]).astype(bf16)
    for at in range(0, out_ref.shape[1], 512):
        part = product(grad_gate, gate_ref[:, at : at + 512])
        part += product(grad_up, up_ref[:, at : at + 512])
        out_ref[:, at : at + 512] = part.astype(bf16)


def latent_kernel(rows_ref, weight_ref, latents_ref, out_ref):
    grad_latent = product_t(rows_ref[...], weight_ref[...])
    out_ref[...] = jnp.where(latents_ref[...].astype(f32) > 0, grad_latent, 0.0).astype(bf16)


def grad_of_preact(rows, weight, latents, tile):
    tokens, width = rows.shape
    count = weight.shape[0]
    return call(
        latent_kernel,
        array((tokens, count)),
        2 * tokens * width * count,
        [rows, weight, latents],
        grid=(count // tile,),
        in_specs=[
            WHOLE,
            pl.BlockSpec((tile, width), lambda j: (j, 0)),
            pl.BlockSpec((tokens, tile), lambda j: (0, j)),
        ],
        out_specs=pl.BlockSpec((tokens, tile), lambda j: (0, j)),
    )


def products_kernel(*refs):
    count = len(refs) // 2
    out_ref = refs[-1]
    total = product(refs[0][...], refs[count][...])
    for k in range(1, count):
        total += product(refs[k][...], refs[count + k][...])
    out_ref[...] = total.astype(bf16)


def sum_of_products(left, right, tile):
    rows, depth = left[0].shape
    columns = right[0].shape[1]
    return call(
        products_kernel,
        array((rows, columns)),
        2 * rows * depth * columns * len(left),
        [*left, *right],
        grid=(columns // tile,),
        in_specs=[pl.BlockSpec((rows, depth), lambda j: (0, 0))] * len(left)
        + [pl.BlockSpec((depth, tile), lambda j: (0, j))] * len(right),
        out_specs=pl.BlockSpec((rows, tile), lambda j: (0, j)),
    )


def per_device(
    residual,
    target,
    encoder_weight,
    encoder_bias,
    decoder_weight,
    decoder_bias,
    first_gain,
    second_gain,
    gate_weight,
    up_weight,
    down_weight,
):
    tokens, share_width = residual.shape
    shards = lax.axis_size(SHARDS)
    copies = lax.axis_size(BATCH)
    width = share_width * shards
    block = width // copies
    own_tokens = tokens // shards
    token_count = tokens * copies
    offset = lax.axis_index(SHARDS) * share_width
    bias, gain_in, gain_out = (a.reshape(1, width) for a in (decoder_bias, first_gain, second_gain))
    gate, up = gate_weight.T, up_weight.T
    everyone = array((shards, own_tokens, width))
    own_rows = array((own_tokens, width), f32)

    def to_owners(partial):
        return exchange(partial.reshape(shards, own_tokens, -1), SHARDS)

    def all_tokens(pieces):
        return exchange(pieces, SHARDS).reshape(tokens, width)

    bias_share = lax.dynamic_slice_in_dim(decoder_bias.astype(f32), offset, share_width)
    centered_share = (residual.astype(f32) - bias_share).astype(bf16).T
    pieces = jnp.broadcast_to(centered_share, (shards, share_width, tokens))
    centered = exchange(pieces, SHARDS).reshape(width, tokens)

    centered_blocks = blocks_of_all(
        lambda b: lax.dynamic_slice_in_dim(centered, b * block, block, axis=0)
    )
    latents, turned_latents = encode(centered, encoder_weight, encoder_bias, 256)
    partial_recon = decode(latents, decoder_weight, target.T, 128)
    partial_recon, *centered_blocks = lax.optimization_barrier((partial_recon, *centered_blocks))

    pieces = to_owners(partial_recon)
    own_target = pieces[:, :, width : width + share_width]
    own_target = jnp.moveaxis(own_target, 0, 1).reshape(own_tokens, width)
    pieces, recon = local(recon_kernel, [everyone, own_rows], [pieces, bias, gain_in])

    normed_input = all_tokens(pieces)
    latent_blocks = copies_of_all(turned_latents)
    hidden = array((tokens, gate.shape[0]), f32)
    partial_out, gelu_value, slope = local(
        forward_kernel,
        [array((tokens, width)), hidden, hidden],
        [normed_input, gate, up, down_weight],
    )
    partial_out, *latent_blocks = lax.optimization_barrier((partial_out, *latent_blocks))

    pieces, grad_result = local(
        functools.partial(output_kernel, token_count),
        [everyone, own_rows],
        [to_owners(partial_out), recon, own_target, gain_out],
    )
    grad_output = all_tokens(pieces)
    (partial_input,) = local(
        backward_kernel,
        [array((tokens, width))],
        [grad_output, gate, up, down_weight, gelu_value, slope],
    )
    (pieces,) = local(
        input_kernel, [everyone], [to_owners(partial_input), recon, grad_result, gain_in]
    )
    grad_recon = all_tokens(pieces)

    recon_blocks = blocks_of_all(
        lambda b: lax.dynamic_slice_in_dim(grad_recon, b * block, block, axis=1)
    )
    grad_preact = grad_of_preact(grad_recon, decoder_weight, latents, 256)
    decoder_grad = sum_of_products(latent_blocks, recon_blocks, 128)
    encoder_grad = sum_of_products(centered_blocks, copies_of_all(grad_preact), 256)
    return encoder_grad, decoder_grad


def solution(mesh):
    batch, latent = mesh.shape["batch"], mesh.shape["latent"]
    split = Mesh(
        mesh.devices.reshape(2, batch // 2, mesh.shape["tensor"] // 2, 2, latent),
        BATCH + SHARDS,
    )
    in_specs = (
        P(BATCH, SHARDS),
        P(BATCH, SHARDS),
        P(None, SHARDS),
        P(SHARDS),
        P(SHARDS, None),
        P(),
        P(),
        P(),
        P(None, SHARDS),
        P(None, SHARDS),
        P(SHARDS, None),
    )
    out_specs = (P(BATCH, SHARDS), P(SHARDS, BATCH))
    return jax.shard_map(
        per_device, mesh=split, in_specs=in_specs, out_specs=out_specs, check_vma=False
    )
```

```python
import functools

import jax
import jax.numpy as jnp
from jax import lax
from jax.experimental import pallas as pl
from jax.experimental.pallas import tpu as pltpu
from jax.sharding import Mesh
from jax.sharding import PartitionSpec as P

SHARDS = ("tensor_0", "tensor_1", "latent")
BATCH = ("batch_0", "batch_1")
HALF = ("tensor_0", "latent")
OTHER_HALF = ("batch_0", "tensor_1")

epsilon = 1e-06

f32 = jnp.float32
bf16 = jnp.bfloat16
LAST = (((1,), (1,)), ((), ()))
WHOLE = pl.BlockSpec(memory_space=pltpu.VMEM)
LIMIT = 40 * 1024 * 1024


def exchange(pieces, axes):
    return lax.all_to_all(pieces, axes, split_axis=0, concat_axis=0, tiled=True)


def swap(block, axes):
    for_all = lax.axis_size(axes)
    return lax.ppermute(block, axes, [(i, for_all - 1 - i) for i in range(for_all)])


def copies_of_all(block):
    near = swap(block, BATCH[1])
    far = swap(block, BATCH[0])
    return [block, near, far, swap(far, BATCH[1])]


def blocks_of_all(block_at):
    own = lax.axis_index(BATCH)
    steps = ((1, BATCH[1]), (2, BATCH[0]), (3, BATCH))
    return [block_at(own)] + [swap(block_at(own ^ step), axes) for step, axes in steps]


def call(body, outs, flops, args, **more):
    moved = sum(a.size * a.dtype.itemsize for a in [*args, *jax.tree.leaves(outs)])
    cost = pl.CostEstimate(flops=flops, bytes_accessed=moved, transcendentals=0)
    return pl.pallas_call(
        body,
        out_shape=outs,
        cost_estimate=cost,
        compiler_params=pltpu.CompilerParams(vmem_limit_bytes=LIMIT),
        **more,
    )(*args)


def array(shape, dtype=bf16):
    return jax.ShapeDtypeStruct(shape, dtype)


def product(left, right):
    return jnp.dot(left, right, preferred_element_type=f32)


def product_t(left, right):
    return lax.dot_general(left, right, LAST, preferred_element_type=f32)


def encode_kernel(centered_ref, weight_ref, bias_ref, latents_ref, turned_ref, rows_ref):
    width = centered_ref.shape[0]

    @pl.when(pl.program_id(0) == 0)
    def _():
        for at in range(0, width, 256):
            rows_ref[:, at : at + 256] = centered_ref[at : at + 256, :].T

    preact = product(rows_ref[...], weight_ref[...]) + bias_ref[...].astype(f32)
    latents = jnp.maximum(preact, 0.0).astype(bf16)
    latents_ref[...] = latents
    turned_ref[...] = latents.T


def encode(centered, weight, bias, tile):
    width, tokens = centered.shape
    count = weight.shape[1]
    return call(
        encode_kernel,
        [array((tokens, count)), array((count, tokens))],
        2 * tokens * width * count,
        [centered, weight, bias.reshape(1, count)],
        grid=(count // tile,),
        in_specs=[
            WHOLE,
            pl.BlockSpec((width, tile), lambda j: (0, j)),
            pl.BlockSpec((1, tile), lambda j: (0, j)),
        ],
        out_specs=[
            pl.BlockSpec((tokens, tile), lambda j: (0, j)),
            pl.BlockSpec((tile, tokens), lambda j: (j, 0)),
        ],
        scratch_shapes=[pltpu.VMEM((tokens, width), bf16)],
    )


def decode_kernel(latents_ref, weight_ref, target_ref, out_ref):
    tile = weight_ref.shape[1]
    step = pl.program_id(0)
    at = pl.multiple_of(step * tile, tile)
    out_ref[:, pl.ds(at, tile)] = product(latents_ref[...], weight_ref[...]).astype(bf16)

    @pl.when(step == 0)
    def _():
        rows, tokens = target_ref.shape
        spare = -rows % 128
        padded = jnp.concatenate([target_ref[...], jnp.zeros((spare, tokens), bf16)], axis=0)
        out_ref[:, out_ref.shape[1] - rows - spare :] = padded.T


def decode(latents, weight, turned_target, room):
    tokens, count = latents.shape
    width = weight.shape[1]
    tile = width // 7
    return call(
        decode_kernel,
        array((tokens, width + room)),
        2 * tokens * width * count,
        [latents, weight, turned_target],
        grid=(7,),
        in_specs=[WHOLE, pl.BlockSpec((count, tile), lambda j: (0, j)), WHOLE],
        out_specs=WHOLE,
    )


def total_of(pieces_ref, width):
    total = pieces_ref[0, :, :width].astype(f32)
    for k in range(1, pieces_ref.shape[0]):
        total += pieces_ref[k, :, :width].astype(f32)
    return total


def send_to_all(out_ref, rows):
    for k in range(out_ref.shape[0]):
        out_ref[k] = rows


def mean_of(values):
    return jnp.sum(values, axis=1, keepdims=True) / values.shape[1]


def recon_kernel(pieces_ref, bias_ref, gain_ref, out_ref, recon_ref):
    recon = total_of(pieces_ref, recon_ref.shape[1]) + bias_ref[...].astype(f32)
    recon_ref[...] = recon
    scale_in = lax.rsqrt(mean_of(recon * recon) + epsilon)
    send_to_all(out_ref, (recon * scale_in * gain_ref[...].astype(f32)).astype(bf16))


def output_kernel(token_count, pieces_ref, recon_ref, target_ref, gain_ref, out_ref, grad_ref):
    gain = gain_ref[...].astype(f32)
    output = total_of(pieces_ref, recon_ref.shape[1])
    scale_out = lax.rsqrt(mean_of(output * output) + epsilon)
    normed_out = output * scale_out
    result = recon_ref[...] + normed_out * gain
    grad_result = 2.0 * (result - target_ref[...].astype(f32)) / token_count
    grad_ref[...] = grad_result
    grad_normed = grad_result * gain
    inner = mean_of(grad_normed * normed_out)
    send_to_all(out_ref, (scale_out * (grad_normed - normed_out * inner)).astype(bf16))


def input_kernel(pieces_ref, recon_ref, grad_ref, gain_ref, out_ref):
    recon = recon_ref[...]
    scale_in = lax.rsqrt(mean_of(recon * recon) + epsilon)
    unit = recon * scale_in
    grad_unit = total_of(pieces_ref, recon_ref.shape[1]) * gain_ref[...].astype(f32)
    inner = mean_of(grad_unit * unit)
    send_to_all(out_ref, (grad_ref[...] + scale_in * (grad_unit - unit * inner)).astype(bf16))


def local(body, outs, args):
    return call(body, outs, 0, args, in_specs=[WHOLE] * len(args), out_specs=[WHOLE] * len(outs))


def parts_of(own, near, far):
    return [own, [near.at[k] for k in range(3)], [far.at[k] for k in range(3)]]


def forward_kernel(rows_ref, gate_ref, up_ref, down_ref, near_ref, far_ref, out_ref, *saved):
    root = 0.7978845608028654
    cube = 0.044715
    rows = rows_ref[...]
    parts = parts_of([gate_ref, up_ref, down_ref], near_ref, far_ref)
    hidden = []
    for (gate, up, _), gelu_ref, slope_ref in zip(parts, saved[0::2], saved[1::2]):
        gate_value = product_t(rows, gate[...])
        up_value = product_t(rows, up[...])
        square = gate_value * gate_value
        curve = jnp.tanh(root * gate_value * (1.0 + cube * square))
        half = 0.5 * (1.0 + curve)
        gelu_value = gate_value * half
        rise = 0.5 * gate_value * (1.0 - curve * curve) * root * (1.0 + 3.0 * cube * square)
        gelu_ref[...] = gelu_value
        slope_ref[...] = up_value * (half + rise)
        hidden.append((gelu_value * up_value).astype(bf16))
    for at in range(0, out_ref.shape[1], 512):
        span = slice(at, at + 512)
        terms = [product(h, down[:, span]) for h, (_, _, down) in zip(hidden, parts)]
        out_ref[:, span] = sum(terms[1:], terms[0]).astype(bf16)


def backward_kernel(rows_ref, gate_ref, up_ref, down_ref, near_ref, far_ref, *refs):
    saved, out_ref = refs[:-1], refs[-1]
    rows = rows_ref[...]
    parts = parts_of([gate_ref, up_ref, down_ref], near_ref, far_ref)
    grads = []
    for (_, _, down), gelu_ref, slope_ref in zip(parts, saved[0::2], saved[1::2]):
        grad_hidden = product_t(rows, down[...])
        grad_gate = (grad_hidden * slope_ref[...]).astype(bf16)
        grads.append((grad_gate, (grad_hidden * gelu_ref[...]).astype(bf16)))
    for at in range(0, out_ref.shape[1], 512):
        span = slice(at, at + 512)
        terms = []
        for (grad_gate, grad_up), (gate, up, _) in zip(grads, parts):
            terms += [product(grad_gate, gate[:, span]), product(grad_up, up[:, span])]
        out_ref[:, span] = sum(terms[1:], terms[0]).astype(bf16)


def latent_kernel(rows_ref, weight_ref, latents_ref, out_ref):
    grad_latent = product_t(rows_ref[...], weight_ref[...])
    out_ref[...] = jnp.where(latents_ref[...].astype(f32) > 0, grad_latent, 0.0).astype(bf16)


def grad_of_preact(rows, weight, latents, tile):
    tokens, width = rows.shape
    count = weight.shape[0]
    return call(
        latent_kernel,
        array((tokens, count)),
        2 * tokens * width * count,
        [rows, weight, latents],
        grid=(count // tile,),
        in_specs=[
            WHOLE,
            pl.BlockSpec((tile, width), lambda j: (j, 0)),
            pl.BlockSpec((tokens, tile), lambda j: (0, j)),
        ],
        out_specs=pl.BlockSpec((tokens, tile), lambda j: (0, j)),
    )


def products_kernel(*refs):
    count = len(refs) // 2
    out_ref = refs[-1]
    total = product(refs[0][...], refs[count][...])
    for k in range(1, count):
        total += product(refs[k][...], refs[count + k][...])
    out_ref[...] = total.astype(bf16)


def sum_of_products(left, right, tile):
    rows, depth = left[0].shape
    columns = right[0].shape[1]
    return call(
        products_kernel,
        array((rows, columns)),
        2 * rows * depth * columns * len(left),
        [*left, *right],
        grid=(columns // tile,),
        in_specs=[pl.BlockSpec((rows, depth), lambda j: (0, 0))] * len(left)
        + [pl.BlockSpec((depth, tile), lambda j: (0, j))] * len(right),
        out_specs=pl.BlockSpec((rows, tile), lambda j: (0, j)),
    )


def per_device(
    residual,
    target,
    encoder_weight,
    encoder_bias,
    decoder_weight,
    decoder_bias,
    first_gain,
    second_gain,
    gate_weight,
    up_weight,
    down_weight,
):
    tokens, share_width = residual.shape
    shards = lax.axis_size(SHARDS)
    copies = lax.axis_size(BATCH)
    width = share_width * shards
    block = width // copies
    own_tokens = tokens // shards
    token_count = tokens * copies
    offset = lax.axis_index(SHARDS) * share_width
    bias, gain_in, gain_out = (a.reshape(1, width) for a in (decoder_bias, first_gain, second_gain))
    gate, up = gate_weight.T, up_weight.T
    everyone = array((shards, own_tokens, width))
    half = lax.axis_size(HALF)
    half_of_them = array((half, own_tokens, width))
    own_rows = array((own_tokens, width), f32)

    def to_owners(partial, axes):
        return exchange(partial.reshape(lax.axis_size(axes), own_tokens, -1), axes)

    def all_tokens(pieces, axes):
        return exchange(pieces, axes).reshape(-1, width)

    units = gate.shape[0] // 2
    at = lax.axis_index(BATCH[1]) * units
    weights = [gate, up, down_weight]
    sent = jnp.stack([lax.dynamic_slice_in_dim(w, at, units, axis=0) for w in weights])
    near = swap(sent, OTHER_HALF)
    far = swap(near, BATCH[1])

    bias_share = lax.dynamic_slice_in_dim(decoder_bias.astype(f32), offset, share_width)
    centered_share = (residual.astype(f32) - bias_share).astype(bf16).T
    pieces = jnp.broadcast_to(centered_share, (shards, share_width, tokens))
    centered = exchange(pieces, SHARDS).reshape(width, tokens)

    centered_blocks = blocks_of_all(
        lambda b: lax.dynamic_slice_in_dim(centered, b * block, block, axis=0)
    )
    latents, turned_latents = encode(centered, encoder_weight, encoder_bias, 256)
    partial_recon = decode(latents, decoder_weight, target.T, 128)
    partial_recon, *centered_blocks = lax.optimization_barrier((partial_recon, *centered_blocks))

    pieces = to_owners(partial_recon, SHARDS)
    own_target = pieces[:, :, width : width + share_width]
    own_target = jnp.moveaxis(own_target, 0, 1).reshape(own_tokens, width)
    pieces, recon = local(recon_kernel, [half_of_them, own_rows], [pieces, bias, gain_in])

    normed_input = all_tokens(pieces, HALF)
    latent_blocks = copies_of_all(turned_latents)
    rows = half * own_tokens
    saved = [array((rows, n), f32) for n in (2 * units, 2 * units, units, units, units, units)]
    partial_out, *saved = local(
        forward_kernel,
        [array((rows, width)), *saved],
        [normed_input, *weights, near, far],
    )
    partial_out, *latent_blocks = lax.optimization_barrier((partial_out, *latent_blocks))

    pieces, grad_result = local(
        functools.partial(output_kernel, token_count),
        [half_of_them, own_rows],
        [to_owners(partial_out, HALF), recon, own_target, gain_out],
    )
    grad_output = all_tokens(pieces, HALF)
    (partial_input,) = local(
        backward_kernel,
        [array((rows, width))],
        [grad_output, *weights, near, far, *saved],
    )
    (pieces,) = local(
        input_kernel, [everyone], [to_owners(partial_input, HALF), recon, grad_result, gain_in]
    )
    grad_recon = all_tokens(pieces, SHARDS)

    recon_blocks = blocks_of_all(
        lambda b: lax.dynamic_slice_in_dim(grad_recon, b * block, block, axis=1)
    )
    grad_preact = grad_of_preact(grad_recon, decoder_weight, latents, 256)
    decoder_grad = sum_of_products(latent_blocks, recon_blocks, 128)
    encoder_grad = sum_of_products(centered_blocks, copies_of_all(grad_preact), 256)
    return encoder_grad, decoder_grad


def solution(mesh):
    batch, latent = mesh.shape["batch"], mesh.shape["latent"]
    split = Mesh(
        mesh.devices.reshape(2, batch // 2, mesh.shape["tensor"] // 2, 2, latent),
        BATCH + SHARDS,
    )
    in_specs = (
        P(BATCH, SHARDS),
        P(BATCH, SHARDS),
        P(None, SHARDS),
        P(SHARDS),
        P(SHARDS, None),
        P(),
        P(),
        P(),
        P(None, SHARDS),
        P(None, SHARDS),
        P(SHARDS, None),
    )
    out_specs = (P(BATCH, SHARDS), P(SHARDS, BATCH))
    return jax.shard_map(
        per_device, mesh=split, in_specs=in_specs, out_specs=out_specs, check_vma=False
    )
```

```python
import functools

import jax
import jax.numpy as jnp
from jax import lax
from jax.experimental import pallas as pl
from jax.experimental.pallas import tpu as pltpu
from jax.sharding import Mesh
from jax.sharding import PartitionSpec as P

SHARDS = ("tensor_0", "tensor_1", "latent")
BATCH = ("batch_0", "batch_1")
HALF = ("tensor_0", "latent")
OTHER_HALF = ("batch_0", "tensor_1")

epsilon = 1e-06

f32 = jnp.float32
bf16 = jnp.bfloat16
LAST = (((1,), (1,)), ((), ()))
WHOLE = pl.BlockSpec(memory_space=pltpu.VMEM)
LIMIT = 12 * 1024 * 1024


def exchange(pieces, axes):
    return lax.all_to_all(pieces, axes, split_axis=0, concat_axis=0, tiled=True)


def swap(block, axes):
    for_all = lax.axis_size(axes)
    return lax.ppermute(block, axes, [(i, for_all - 1 - i) for i in range(for_all)])


def copies_of_all(block):
    near = swap(block, BATCH[1])
    far = swap(block, BATCH[0])
    return [block, near, far, swap(far, BATCH[1])]


def blocks_of_all(block_at):
    own = lax.axis_index(BATCH)
    steps = ((1, BATCH[1]), (2, BATCH[0]), (3, BATCH))
    return [block_at(own)] + [swap(block_at(own ^ step), axes) for step, axes in steps]


def call(body, outs, flops, args, **more):
    moved = sum(a.size * a.dtype.itemsize for a in [*args, *jax.tree.leaves(outs)])
    cost = pl.CostEstimate(flops=flops, bytes_accessed=moved, transcendentals=0)
    return pl.pallas_call(
        body,
        out_shape=outs,
        cost_estimate=cost,
        compiler_params=pltpu.CompilerParams(vmem_limit_bytes=LIMIT),
        **more,
    )(*args)


def array(shape, dtype=bf16):
    return jax.ShapeDtypeStruct(shape, dtype)


def product(left, right):
    return jnp.dot(left, right, preferred_element_type=f32)


def product_t(left, right):
    return lax.dot_general(left, right, LAST, preferred_element_type=f32)


def encode_kernel(centered_ref, weight_ref, bias_ref, latents_ref, turned_ref, total_ref):
    step = pl.program_id(0)
    term = product(centered_ref[...].T, weight_ref[...])

    @pl.when(step == 0)
    def _():
        total_ref[...] = term + bias_ref[...].astype(f32)

    @pl.when(step > 0)
    def _():
        total_ref[...] += term

    @pl.when(step == pl.num_programs(0) - 1)
    def _():
        latents = jnp.maximum(total_ref[...], 0.0).astype(bf16)
        latents_ref[...] = latents
        turned_ref[...] = latents.T


def encode(centered, weight, bias, tile):
    width, tokens = centered.shape
    count = weight.shape[1]
    return call(
        encode_kernel,
        [array((tokens, count)), array((count, tokens))],
        2 * tokens * width * count,
        [centered, pltpu.with_memory_space_constraint(weight, pltpu.HBM), bias.reshape(1, count)],
        grid=(width // tile,),
        in_specs=[
            pl.BlockSpec((tile, tokens), lambda j: (j, 0)),
            pl.BlockSpec((tile, count), lambda j: (j, 0)),
            WHOLE,
        ],
        out_specs=[WHOLE, WHOLE],
        scratch_shapes=[pltpu.VMEM((tokens, count), f32)],
    )


def decode_kernel(latents_ref, weight_ref, target_ref, out_ref):
    tile = weight_ref.shape[1]
    step = pl.program_id(0)
    at = pl.multiple_of(step * tile, tile)
    out_ref[:, pl.ds(at, tile)] = product(latents_ref[...], weight_ref[...]).astype(bf16)

    @pl.when(step == 0)
    def _():
        rows, tokens = target_ref.shape
        spare = -rows % 128
        padded = jnp.concatenate([target_ref[...], jnp.zeros((spare, tokens), bf16)], axis=0)
        out_ref[:, out_ref.shape[1] - rows - spare :] = padded.T


def decode(latents, weight, turned_target, room):
    tokens, count = latents.shape
    width = weight.shape[1]
    tile = width // 7
    return call(
        decode_kernel,
        array((tokens, width + room)),
        2 * tokens * width * count,
        [latents, weight, turned_target],
        grid=(7,),
        in_specs=[WHOLE, pl.BlockSpec((count, tile), lambda j: (0, j)), WHOLE],
        out_specs=WHOLE,
    )


def total_of(pieces_ref, width):
    total = pieces_ref[0, :, :width].astype(f32)
    for k in range(1, pieces_ref.shape[0]):
        total += pieces_ref[k, :, :width].astype(f32)
    return total


def send_to_all(out_ref, rows):
    for k in range(out_ref.shape[0]):
        out_ref[k] = rows


def mean_of(values):
    return jnp.sum(values, axis=1, keepdims=True) / values.shape[1]


def recon_kernel(pieces_ref, bias_ref, gain_ref, out_ref, recon_ref):
    recon = total_of(pieces_ref, recon_ref.shape[1]) + bias_ref[...].astype(f32)
    recon_ref[...] = recon
    scale_in = lax.rsqrt(mean_of(recon * recon) + epsilon)
    send_to_all(out_ref, (recon * scale_in * gain_ref[...].astype(f32)).astype(bf16))


def output_kernel(token_count, pieces_ref, gain_ref, recon_ref, target_ref, out_ref, grad_ref):
    gain = gain_ref[...].astype(f32)
    output = total_of(pieces_ref, recon_ref.shape[1])
    scale_out = lax.rsqrt(mean_of(output * output) + epsilon)
    normed_out = output * scale_out
    result = recon_ref[...] + normed_out * gain
    grad_result = 2.0 * (result - target_ref[...].astype(f32)) / token_count
    grad_ref[...] = grad_result
    grad_normed = grad_result * gain
    inner = mean_of(grad_normed * normed_out)
    send_to_all(out_ref, (scale_out * (grad_normed - normed_out * inner)).astype(bf16))


def input_kernel(pieces_ref, gain_ref, recon_ref, grad_ref, out_ref):
    recon = recon_ref[...]
    scale_in = lax.rsqrt(mean_of(recon * recon) + epsilon)
    unit = recon * scale_in
    grad_unit = total_of(pieces_ref, recon_ref.shape[1]) * gain_ref[...].astype(f32)
    inner = mean_of(grad_unit * unit)
    send_to_all(out_ref, (grad_ref[...] + scale_in * (grad_unit - unit * inner)).astype(bf16))


def local(body, outs, args, kept=0):
    stay = len(args) - kept
    return call(body, outs, 0, args, in_specs=[WHOLE] * stay + [pl.BlockSpec()] * kept)


def parts_of(own, other):
    return [own, [other.at[k] for k in range(3)]]


def forward_kernel(rows_ref, gate_ref, up_ref, down_ref, other_ref, out_ref, *saved):
    root = 0.7978845608028654
    cube = 0.044715
    rows = rows_ref[...]
    parts = parts_of([gate_ref, up_ref, down_ref], other_ref)
    hidden = []
    for (gate, up, _), gelu_ref, slope_ref in zip(parts, saved[0::2], saved[1::2]):
        gate_value = product_t(rows, gate[...])
        up_value = product_t(rows, up[...])
        square = gate_value * gate_value
        curve = jnp.tanh(root * gate_value * (1.0 + cube * square))
        half = 0.5 * (1.0 + curve)
        gelu_value = gate_value * half
        rise = 0.5 * gate_value * (1.0 - curve * curve) * root * (1.0 + 3.0 * cube * square)
        gelu_ref[...] = gelu_value
        slope_ref[...] = up_value * (half + rise)
        hidden.append((gelu_value * up_value).astype(bf16))
    for at in range(0, out_ref.shape[1], 512):
        span = slice(at, at + 512)
        terms = [product(h, down[:, span]) for h, (_, _, down) in zip(hidden, parts)]
        out_ref[:, span] = sum(terms[1:], terms[0]).astype(bf16)


def backward_kernel(rows_ref, gate_ref, up_ref, down_ref, other_ref, *refs):
    saved, out_ref = refs[:-1], refs[-1]
    rows = rows_ref[...]
    parts = parts_of([gate_ref, up_ref, down_ref], other_ref)
    grads = []
    for (_, _, down), gelu_ref, slope_ref in zip(parts, saved[0::2], saved[1::2]):
        grad_hidden = product_t(rows, down[...])
        grad_gate = (grad_hidden * slope_ref[...]).astype(bf16)
        grads.append((grad_gate, (grad_hidden * gelu_ref[...]).astype(bf16)))
    for at in range(0, out_ref.shape[1], 512):
        span = slice(at, at + 512)
        terms = []
        for (grad_gate, grad_up), (gate, up, _) in zip(grads, parts):
            terms += [product(grad_gate, gate[:, span]), product(grad_up, up[:, span])]
        out_ref[:, span] = sum(terms[1:], terms[0]).astype(bf16)


def latent_kernel(rows_ref, weight_ref, latents_ref, out_ref):
    grad_latent = product_t(rows_ref[...], weight_ref[...])
    out_ref[...] = jnp.where(latents_ref[...].astype(f32) > 0, grad_latent, 0.0).astype(bf16)


def grad_of_preact(rows, weight, latents, tile):
    tokens, width = rows.shape
    count = weight.shape[0]
    return call(
        latent_kernel,
        array((tokens, count)),
        2 * tokens * width * count,
        [rows, weight, latents],
        grid=(count // tile,),
        in_specs=[
            WHOLE,
            pl.BlockSpec((tile, width), lambda j: (j, 0)),
            pl.BlockSpec((tokens, tile), lambda j: (0, j)),
        ],
        out_specs=pl.BlockSpec((tokens, tile), lambda j: (0, j)),
    )


def products_kernel(spans, *refs):
    count = len(refs) // 2
    out_ref = refs[-1]
    for span in spans:
        total = product(refs[0][...], refs[count][:, span])
        for k in range(1, count):
            total += product(refs[k][...], refs[count + k][:, span])
        out_ref[:, span] = total.astype(bf16)


def sum_of_products(left, right, tile):
    rows, depth = left[0].shape
    columns = right[0].shape[1]
    spans = [slice(at, min(at + 256, tile)) for at in range(0, tile, 256)]
    return call(
        functools.partial(products_kernel, spans),
        array((rows, columns)),
        2 * rows * depth * columns * len(left),
        [*left, *right],
        grid=(columns // tile,),
        in_specs=[WHOLE] * len(left)
        + [pl.BlockSpec((depth, tile), lambda j: (0, j))] * len(right),
        out_specs=pl.BlockSpec((rows, tile), lambda j: (0, j)),
    )


def per_device(
    residual,
    target,
    encoder_weight,
    encoder_bias,
    decoder_weight,
    decoder_bias,
    first_gain,
    second_gain,
    gate_weight,
    up_weight,
    down_weight,
):
    tokens, share_width = residual.shape
    shards = lax.axis_size(SHARDS)
    copies = lax.axis_size(BATCH)
    width = share_width * shards
    block = width // copies
    own_tokens = tokens // shards
    token_count = tokens * copies
    offset = lax.axis_index(SHARDS) * share_width
    bias, gain_in, gain_out = (a.reshape(1, width) for a in (decoder_bias, first_gain, second_gain))
    gate, up = gate_weight.T, up_weight.T
    everyone = array((shards, own_tokens, width))
    half = lax.axis_size(HALF)
    half_of_them = array((half, own_tokens, width))
    own_rows = array((own_tokens, width), f32)

    def to_owners(partial, axes):
        return exchange(partial.reshape(lax.axis_size(axes), own_tokens, -1), axes)

    def all_tokens(pieces, axes):
        return exchange(pieces, axes).reshape(-1, width)

    hidden = gate.shape[0]
    units = hidden // copies
    at = (lax.axis_index(BATCH) ^ (copies // 2)) * units
    weights = [gate, up, down_weight]
    sent = jnp.stack([lax.dynamic_slice_in_dim(w, at, units, axis=0) for w in weights])
    quarter = swap(sent, OTHER_HALF)
    bias_share = lax.dynamic_slice_in_dim(decoder_bias.astype(f32), offset, share_width)
    centered_share = (residual.astype(f32) - bias_share).astype(bf16).T
    pieces = jnp.broadcast_to(centered_share, (shards, share_width, tokens))
    centered = exchange(pieces, SHARDS).reshape(width, tokens)

    latents, turned_latents = encode(centered, encoder_weight, encoder_bias, 256)
    partial_recon = decode(latents, decoder_weight, target.T, 128)

    _, quarter = lax.optimization_barrier((partial_recon, quarter))
    other = jnp.concatenate(copies_of_all(quarter), axis=1)

    pieces = to_owners(partial_recon, SHARDS)
    own_target = pieces[:, :, width : width + share_width]
    own_target = jnp.moveaxis(own_target, 0, 1).reshape(own_tokens, width)
    pieces, recon = local(recon_kernel, [half_of_them, own_rows], [pieces, bias, gain_in])

    pieces, centered, turned_latents = lax.optimization_barrier((pieces, centered, turned_latents))
    normed_input = all_tokens(pieces, HALF)
    latent_blocks = copies_of_all(turned_latents)
    centered_blocks = blocks_of_all(
        lambda b: lax.dynamic_slice_in_dim(centered, b * block, block, axis=0)
    )
    rows = half * own_tokens
    partial_out, *saved = local(
        forward_kernel,
        [array((rows, width))] + [array((rows, hidden), f32)] * 4,
        [normed_input, *weights, other],
    )
    partial_out, latent_blocks = lax.optimization_barrier((partial_out, latent_blocks))

    pieces, grad_result = local(
        functools.partial(output_kernel, token_count),
        [half_of_them, own_rows],
        [to_owners(partial_out, HALF), gain_out, recon, own_target],
        kept=2,
    )
    grad_output = all_tokens(pieces, HALF)
    (partial_input,) = local(
        backward_kernel,
        [array((rows, width))],
        [grad_output, *weights, other, *saved],
        kept=4,
    )
    partial_input, centered_blocks = lax.optimization_barrier((partial_input, centered_blocks))
    (pieces,) = local(
        input_kernel,
        [everyone],
        [to_owners(partial_input, HALF), gain_in, recon, grad_result],
        kept=2,
    )
    grad_recon = all_tokens(pieces, SHARDS)

    recon_blocks = blocks_of_all(
        lambda b: lax.dynamic_slice_in_dim(grad_recon, b * block, block, axis=1)
    )
    grad_preact = grad_of_preact(grad_recon, decoder_weight, latents, 256)
    encoder_grad = sum_of_products(centered_blocks, copies_of_all(grad_preact), 256)
    encoder_grad, recon_blocks = lax.optimization_barrier((encoder_grad, recon_blocks))
    decoder_grad = sum_of_products(latent_blocks, recon_blocks, block)
    return encoder_grad, decoder_grad


def solution(mesh):
    batch, latent = mesh.shape["batch"], mesh.shape["latent"]
    split = Mesh(
        mesh.devices.reshape(2, batch // 2, mesh.shape["tensor"] // 2, 2, latent),
        BATCH + SHARDS,
    )
    in_specs = (
        P(BATCH, SHARDS),
        P(BATCH, SHARDS),
        P(None, SHARDS),
        P(SHARDS),
        P(SHARDS, None),
        P(),
        P(),
        P(),
        P(None, SHARDS),
        P(None, SHARDS),
        P(SHARDS, None),
    )
    out_specs = (P(BATCH, SHARDS), P(SHARDS, BATCH))
    return jax.shard_map(
        per_device, mesh=split, in_specs=in_specs, out_specs=out_specs, check_vma=False
    )
```

```python
import functools
import math

import jax
import jax.numpy as jnp
from jax import lax
from jax.experimental import pallas as pl
from jax.experimental.pallas import tpu as pltpu
from jax.sharding import Mesh
from jax.sharding import PartitionSpec as P

SHARDS = ("tensor_0", "tensor_1", "latent")
BATCH = ("batch_0", "batch_1")
HALF = ("tensor_0", "latent")
OTHER_HALF = ("batch_0", "tensor_1")

epsilon = 1e-06

f32 = jnp.float32
bf16 = jnp.bfloat16
LAST = (((1,), (1,)), ((), ()))
WHOLE = pl.BlockSpec(memory_space=pltpu.VMEM)
LIMIT = 24 * 1024 * 1024


def exchange(pieces, axes):
    return lax.all_to_all(pieces, axes, split_axis=0, concat_axis=0, tiled=True)


def swap(block, axes):
    for_all = lax.axis_size(axes)
    return lax.ppermute(block, axes, [(i, for_all - 1 - i) for i in range(for_all)])


def copies_of_all(block):
    near = swap(block, BATCH[1])
    far = swap(block, BATCH[0])
    return [block, near, far, swap(far, BATCH[1])]


def blocks_of_all(block_at):
    own = lax.axis_index(BATCH)
    steps = ((1, BATCH[1]), (2, BATCH[0]), (3, BATCH))
    return [block_at(own)] + [swap(block_at(own ^ step), axes) for step, axes in steps]


def call(body, outs, flops, args, **more):
    arrays = [*args, *jax.tree.leaves(outs)]
    moved = sum(math.prod(a.shape) * jnp.dtype(a.dtype).itemsize for a in arrays)
    cost = pl.CostEstimate(flops=flops, bytes_accessed=moved, transcendentals=0)
    return pl.pallas_call(
        body,
        out_shape=outs,
        cost_estimate=cost,
        compiler_params=pltpu.CompilerParams(vmem_limit_bytes=LIMIT),
        **more,
    )(*args)


def array(shape, dtype=bf16):
    return jax.ShapeDtypeStruct(shape, dtype)


def hbm_array(shape, dtype=bf16):
    return pltpu.HBM(shape, dtype)


def in_hbm(value):
    return pltpu.with_memory_space_constraint(value, pltpu.HBM)


def product(left, right):
    return jnp.dot(left, right, preferred_element_type=f32)


def product_t(left, right):
    return lax.dot_general(left, right, LAST, preferred_element_type=f32)


def encode_kernel(share, centered_ref, weight_ref, bias_ref, latents_ref, turned_ref, rows_ref):
    width = rows_ref.shape[1]

    @pl.when(pl.program_id(0) == 0)
    def _():
        for at in range(0, width, 256):
            runs, f = [], at
            while f < at + 256:
                shard, inside = divmod(f, share)
                far, half, near = shard // 8, shard // 4 % 2, shard % 4
                run = min(share - inside, at + 256 - f)
                start = (far * 8 + near * 2 + half) * share + inside
                runs.append(centered_ref[start : start + run, :])
                f += run
            rows_ref[:, at : at + 256] = jnp.concatenate(runs, axis=0).T

    preact = product(rows_ref[...], weight_ref[...]) + bias_ref[...].astype(f32)
    latents = jnp.maximum(preact, 0.0).astype(bf16)
    latents_ref[...] = latents
    turned_ref[...] = latents.T


def encode(centered, weight, bias, share, tile):
    width, tokens = centered.shape
    count = weight.shape[1]
    return call(
        functools.partial(encode_kernel, share),
        [array((tokens, count)), hbm_array((count, tokens))],
        2 * tokens * width * count,
        [centered, in_hbm(weight), bias.reshape(1, count)],
        grid=(count // tile,),
        in_specs=[
            pl.BlockSpec((width, tokens), lambda j: (0, 0)),
            pl.BlockSpec((width, tile), lambda j: (0, j)),
            pl.BlockSpec((1, tile), lambda j: (0, j)),
        ],
        out_specs=[
            pl.BlockSpec((tokens, tile), lambda j: (0, j)),
            pl.BlockSpec((tile, tokens), lambda j: (j, 0)),
        ],
        scratch_shapes=[pltpu.VMEM((tokens, width), bf16)],
    )


def gather_kernel(at_ref, *refs):
    *weights, out_ref, sems = refs
    count = out_ref.shape[1]
    at = pl.multiple_of(at_ref[0], count)
    copies = [
        pltpu.make_async_copy(w.at[pl.ds(at, count)], out_ref.at[k], sems.at[k])
        for k, w in enumerate(weights)
    ]
    for copy in copies:
        copy.start()
    for copy in copies:
        copy.wait()


def rows_of_each(weights, at, count):
    anywhere = pl.BlockSpec(memory_space=pl.ANY)
    return call(
        gather_kernel,
        hbm_array((len(weights), count, weights[0].shape[1])),
        0,
        [at.reshape(1), *(in_hbm(w) for w in weights)],
        in_specs=[pl.BlockSpec(memory_space=pltpu.SMEM)] + [anywhere] * len(weights),
        out_specs=anywhere,
        scratch_shapes=[pltpu.SemaphoreType.DMA((len(weights),))],
    )


def decode_kernel(latents_ref, weight_ref, target_ref, out_ref):
    tile = weight_ref.shape[1]
    step = pl.program_id(0)
    at = pl.multiple_of(step * tile, tile)
    out_ref[:, pl.ds(at, tile)] = product(latents_ref[...], weight_ref[...]).astype(bf16)

    @pl.when(step == 0)
    def _():
        rows, tokens = target_ref.shape
        spare = -rows % 128
        padded = jnp.concatenate([target_ref[...], jnp.zeros((spare, tokens), bf16)], axis=0)
        out_ref[:, out_ref.shape[1] - rows - spare :] = padded.T


def decode(latents, weight, turned_target, room):
    tokens, count = latents.shape
    width = weight.shape[1]
    tile = width // 7
    return call(
        decode_kernel,
        array((tokens, width + room)),
        2 * tokens * width * count,
        [latents, in_hbm(weight), turned_target],
        grid=(7,),
        in_specs=[WHOLE, pl.BlockSpec((count, tile), lambda j: (0, j)), WHOLE],
        out_specs=WHOLE,
    )


def total_of(pieces_ref, width):
    total = pieces_ref[0, :, :width].astype(f32)
    for k in range(1, pieces_ref.shape[0]):
        total += pieces_ref[k, :, :width].astype(f32)
    return total


def send_to_all(out_ref, rows):
    for k in range(out_ref.shape[0]):
        out_ref[k] = rows


def mean_of(values):
    return jnp.sum(values, axis=1, keepdims=True) / values.shape[1]


def recon_kernel(pieces_ref, bias_ref, gain_ref, out_ref, recon_ref):
    recon = total_of(pieces_ref, recon_ref.shape[1]) + bias_ref[...].astype(f32)
    recon_ref[...] = recon
    scale_in = lax.rsqrt(mean_of(recon * recon) + epsilon)
    send_to_all(out_ref, (recon * scale_in * gain_ref[...].astype(f32)).astype(bf16))


def output_kernel(token_count, pieces_ref, recon_ref, target_ref, gain_ref, out_ref, grad_ref):
    gain = gain_ref[...].astype(f32)
    output = total_of(pieces_ref, recon_ref.shape[1])
    scale_out = lax.rsqrt(mean_of(output * output) + epsilon)
    normed_out = output * scale_out
    result = recon_ref[...] + normed_out * gain
    grad_result = 2.0 * (result - target_ref[...].astype(f32)) / token_count
    grad_ref[...] = grad_result
    grad_normed = grad_result * gain
    inner = mean_of(grad_normed * normed_out)
    send_to_all(out_ref, (scale_out * (grad_normed - normed_out * inner)).astype(bf16))


def input_kernel(pieces_ref, recon_ref, grad_ref, gain_ref, out_ref):
    recon = recon_ref[...]
    scale_in = lax.rsqrt(mean_of(recon * recon) + epsilon)
    unit = recon * scale_in
    grad_unit = total_of(pieces_ref, recon_ref.shape[1]) * gain_ref[...].astype(f32)
    inner = mean_of(grad_unit * unit)
    send_to_all(out_ref, (grad_ref[...] + scale_in * (grad_unit - unit * inner)).astype(bf16))


def local(body, outs, args, kept=0):
    stay = len(args) - kept
    args = [*args[:stay], *(in_hbm(a) for a in args[stay:])]
    return call(body, outs, 0, args, in_specs=[WHOLE] * stay + [pl.BlockSpec()] * kept)


def parts_of(own, near, far):
    return [own, [near.at[k] for k in range(3)], [far.at[k] for k in range(3)]]


def forward_kernel(rows_ref, gate_ref, up_ref, down_ref, near_ref, far_ref, out_ref, *saved):
    root = 0.7978845608028654
    cube = 0.044715
    rows = rows_ref[...]
    parts = parts_of([gate_ref, up_ref, down_ref], near_ref, far_ref)
    hidden = []
    for (gate, up, _), gelu_ref, slope_ref in zip(parts, saved[0::2], saved[1::2]):
        gate_value = product_t(rows, gate[...])
        up_value = product_t(rows, up[...])
        square = gate_value * gate_value
        curve = jnp.tanh(root * gate_value * (1.0 + cube * square))
        half = 0.5 * (1.0 + curve)
        gelu_value = gate_value * half
        rise = 0.5 * gate_value * (1.0 - curve * curve) * root * (1.0 + 3.0 * cube * square)
        gelu_ref[...] = gelu_value
        slope_ref[...] = up_value * (half + rise)
        hidden.append((gelu_value * up_value).astype(bf16))
    for at in range(0, out_ref.shape[1], 512):
        span = slice(at, at + 512)
        terms = [product(h, down[:, span]) for h, (_, _, down) in zip(hidden, parts)]
        out_ref[:, span] = sum(terms[1:], terms[0]).astype(bf16)


def backward_kernel(rows_ref, gate_ref, up_ref, down_ref, near_ref, far_ref, *refs):
    saved, out_ref = refs[:-1], refs[-1]
    rows = rows_ref[...]
    parts = parts_of([gate_ref, up_ref, down_ref], near_ref, far_ref)
    grads = []
    for (_, _, down), gelu_ref, slope_ref in zip(parts, saved[0::2], saved[1::2]):
        grad_hidden = product_t(rows, down[...])
        grad_gate = (grad_hidden * slope_ref[...]).astype(bf16)
        grads.append((grad_gate, (grad_hidden * gelu_ref[...]).astype(bf16)))
    for at in range(0, out_ref.shape[1], 512):
        span = slice(at, at + 512)
        terms = []
        for (grad_gate, grad_up), (gate, up, _) in zip(grads, parts):
            terms += [product(grad_gate, gate[:, span]), product(grad_up, up[:, span])]
        out_ref[:, span] = sum(terms[1:], terms[0]).astype(bf16)


def latent_kernel(rows_ref, weight_ref, latents_ref, out_ref):
    grad_latent = product_t(rows_ref[...], weight_ref[...])
    out_ref[...] = jnp.where(latents_ref[...].astype(f32) > 0, grad_latent, 0.0).astype(bf16)


def grad_of_preact(rows, weight, latents, tile):
    tokens, width = rows.shape
    count = weight.shape[0]
    return call(
        latent_kernel,
        array((tokens, count)),
        2 * tokens * width * count,
        [rows, weight, latents],
        grid=(count // tile,),
        in_specs=[
            WHOLE,
            pl.BlockSpec((tile, width), lambda j: (j, 0)),
            pl.BlockSpec((tokens, tile), lambda j: (0, j)),
        ],
        out_specs=pl.BlockSpec((tokens, tile), lambda j: (0, j)),
    )


def products_kernel(spans, *refs):
    count = len(refs) // 2
    out_ref = refs[-1]
    for span in spans:
        total = product(refs[0][...], refs[count][:, span])
        for k in range(1, count):
            total += product(refs[k][...], refs[count + k][:, span])
        out_ref[:, span] = total.astype(bf16)


def sum_of_products(left, right, tile):
    rows, depth = left[0].shape
    columns = right[0].shape[1]
    spans = [slice(at, min(at + 256, tile)) for at in range(0, tile, 256)]
    return call(
        functools.partial(products_kernel, spans),
        array((rows, columns)),
        2 * rows * depth * columns * len(left),
        [*left, *right],
        grid=(columns // tile,),
        in_specs=[pl.BlockSpec((rows, depth), lambda j: (0, 0))] * len(left)
        + [pl.BlockSpec((depth, tile), lambda j: (0, j))] * len(right),
        out_specs=pl.BlockSpec((rows, tile), lambda j: (0, j)),
    )


def per_device(
    residual,
    target,
    encoder_weight,
    encoder_bias,
    decoder_weight,
    decoder_bias,
    first_gain,
    second_gain,
    gate_weight,
    up_weight,
    down_weight,
):
    tokens, share_width = residual.shape
    shards = lax.axis_size(SHARDS)
    copies = lax.axis_size(BATCH)
    width = share_width * shards
    block = width // copies
    own_tokens = tokens // shards
    token_count = tokens * copies
    offset = lax.axis_index(SHARDS) * share_width
    bias, gain_in, gain_out = (a.reshape(1, width) for a in (decoder_bias, first_gain, second_gain))
    gate, up = gate_weight.T, up_weight.T
    everyone = array((shards, own_tokens, width))
    half = lax.axis_size(HALF)
    half_of_them = hbm_array((half, own_tokens, width))
    own_rows = array((own_tokens, width), f32)

    def to_owners(partial, axes):
        return exchange(partial.reshape(lax.axis_size(axes), own_tokens, -1), axes)

    def all_tokens(pieces, axes):
        return exchange(pieces, axes).reshape(-1, width)

    units = gate.shape[0] // 2
    at = lax.axis_index(BATCH[1]) * units
    weights = [gate, up, down_weight]

    bias_share = lax.dynamic_slice_in_dim(decoder_bias.astype(f32), offset, share_width)
    centered_share = (residual.astype(f32) - bias_share).astype(bf16).T
    partner = swap(centered_share, SHARDS[1])
    first = lax.axis_index(SHARDS[1]) == 0
    pair = jnp.stack(
        [jnp.where(first, centered_share, partner), jnp.where(first, partner, centered_share)]
    )
    pieces = jnp.broadcast_to(pair, (lax.axis_size(HALF), *pair.shape))
    pieces, weights_then = lax.optimization_barrier((pieces, weights))
    sent = rows_of_each(weights_then, at, units)
    near = swap(sent, OTHER_HALF)
    far = swap(near, BATCH[1])
    centered = exchange(pieces, HALF).reshape(width, tokens)

    latents, turned_latents = encode(
        centered, encoder_weight, encoder_bias, share_width, 256
    )
    partial_recon = decode(latents, decoder_weight, target.T, 128)

    pieces = to_owners(partial_recon, SHARDS)
    own_target = pieces[:, :, width : width + share_width]
    own_target = jnp.moveaxis(own_target, 0, 1).reshape(own_tokens, width)
    pieces, recon = local(recon_kernel, [half_of_them, own_rows], [pieces, bias, gain_in])

    pieces, centered, turned_latents = lax.optimization_barrier((pieces, centered, turned_latents))
    normed_input = all_tokens(pieces, HALF)
    latent_blocks = copies_of_all(turned_latents)

    def feature_block(b):
        part = lax.dynamic_slice_in_dim(centered, b * block, block, axis=0)
        part = part.reshape(lax.axis_size(SHARDS[2]), lax.axis_size(SHARDS[1]), share_width, tokens)
        return jnp.swapaxes(part, 0, 1).reshape(block, tokens)

    centered_blocks = blocks_of_all(feature_block)
    rows = half * own_tokens
    saved = [hbm_array((rows, n), f32) for n in (2 * units, 2 * units, units, units, units, units)]
    partial_out, *saved = local(
        forward_kernel,
        [hbm_array((rows, width)), *saved],
        [normed_input, *weights, near, far],
    )

    pieces, grad_result = local(
        functools.partial(output_kernel, token_count),
        [half_of_them, own_rows],
        [to_owners(partial_out, HALF), recon, own_target, gain_out],
    )
    pieces, latent_blocks, centered_blocks = lax.optimization_barrier(
        (pieces, latent_blocks, centered_blocks)
    )
    grad_output = all_tokens(pieces, HALF)
    (partial_input,) = local(
        backward_kernel,
        [array((rows, width))],
        [grad_output, *weights, near, far, *saved],
        kept=6,
    )
    (pieces,) = local(
        input_kernel, [everyone], [to_owners(partial_input, HALF), recon, grad_result, gain_in]
    )
    grad_recon = all_tokens(pieces, SHARDS)

    recon_blocks = blocks_of_all(
        lambda b: lax.dynamic_slice_in_dim(grad_recon, b * block, block, axis=1)
    )
    grad_preact = grad_of_preact(grad_recon, decoder_weight, latents, 256)
    encoder_grad = sum_of_products(centered_blocks, copies_of_all(grad_preact), 256)
    decoder_grad = sum_of_products(latent_blocks, recon_blocks, block)
    return encoder_grad, decoder_grad


def solution(mesh):
    batch, latent = mesh.shape["batch"], mesh.shape["latent"]
    split = Mesh(
        mesh.devices.reshape(2, batch // 2, mesh.shape["tensor"] // 2, 2, latent),
        BATCH + SHARDS,
    )
    in_specs = (
        P(BATCH, SHARDS),
        P(BATCH, SHARDS),
        P(None, SHARDS),
        P(SHARDS),
        P(SHARDS, None),
        P(),
        P(),
        P(),
        P(None, SHARDS),
        P(None, SHARDS),
        P(SHARDS, None),
    )
    out_specs = (P(BATCH, SHARDS), P(SHARDS, BATCH))
    return jax.shard_map(
        per_device, mesh=split, in_specs=in_specs, out_specs=out_specs, check_vma=False
    )
```

```python
import functools
import math

import jax
import jax.numpy as jnp
from jax import lax
from jax.experimental import pallas as pl
from jax.experimental.pallas import tpu as pltpu
from jax.sharding import Mesh
from jax.sharding import PartitionSpec as P

SHARDS = ("tensor_0", "tensor_1", "latent")
BATCH = ("batch_0", "batch_1")
HALF = ("tensor_0", "latent")
OTHER_HALF = ("batch_0", "tensor_1")

epsilon = 1e-06

f32 = jnp.float32
bf16 = jnp.bfloat16
LAST = (((1,), (1,)), ((), ()))
WHOLE = pl.BlockSpec(memory_space=pltpu.VMEM)
EFFORT = 8
LIMIT = 24 * 1024 * 1024


def exchange(pieces, axes):
    return lax.all_to_all(pieces, axes, split_axis=0, concat_axis=0, tiled=True)


def swap(block, axes):
    for_all = lax.axis_size(axes)
    return lax.ppermute(block, axes, [(i, for_all - 1 - i) for i in range(for_all)])


def copies_of_all(block):
    near = swap(block, BATCH[1])
    far = swap(block, BATCH[0])
    return [block, near, far, swap(far, BATCH[1])]


def blocks_of_all(block_at):
    own = lax.axis_index(BATCH)
    steps = ((1, BATCH[1]), (2, BATCH[0]), (3, BATCH))
    return [block_at(own)] + [swap(block_at(own ^ step), axes) for step, axes in steps]


def call(body, outs, flops, args, **more):
    arrays = [*args, *jax.tree.leaves(outs)]
    moved = sum(math.prod(a.shape) * jnp.dtype(a.dtype).itemsize for a in arrays)
    cost = pl.CostEstimate(flops=flops, bytes_accessed=moved, transcendentals=0)
    return pl.pallas_call(
        body,
        out_shape=outs,
        cost_estimate=cost,
        compiler_params=pltpu.CompilerParams(vmem_limit_bytes=LIMIT),
        **more,
    )(*args)


def array(shape, dtype=bf16):
    return jax.ShapeDtypeStruct(shape, dtype)


def hbm_array(shape, dtype=bf16):
    return pltpu.HBM(shape, dtype)


def in_hbm(value):
    return pltpu.with_memory_space_constraint(value, pltpu.HBM)


def product(left, right):
    return jnp.dot(left, right, preferred_element_type=f32)


def product_t(left, right):
    return lax.dot_general(left, right, LAST, preferred_element_type=f32)


def encode_kernel(share, centered_ref, weight_ref, bias_ref, latents_ref, turned_ref, rows_ref):
    width = rows_ref.shape[1]

    @pl.when(pl.program_id(0) == 0)
    def _():
        for at in range(0, width, 256):
            runs, f = [], at
            while f < at + 256:
                shard, inside = divmod(f, share)
                far, half, near = shard // 8, shard // 4 % 2, shard % 4
                run = min(share - inside, at + 256 - f)
                start = (far * 8 + near * 2 + half) * share + inside
                runs.append(centered_ref[start : start + run, :])
                f += run
            rows_ref[:, at : at + 256] = jnp.concatenate(runs, axis=0).T

    preact = product(rows_ref[...], weight_ref[...]) + bias_ref[...].astype(f32)
    latents = jnp.maximum(preact, 0.0).astype(bf16)
    latents_ref[...] = latents
    turned_ref[...] = latents.T


def encode(centered, weight, bias, share, tile):
    width, tokens = centered.shape
    count = weight.shape[1]
    return call(
        functools.partial(encode_kernel, share),
        [array((tokens, count)), hbm_array((count, tokens))],
        EFFORT * 2 * tokens * width * count,
        [centered, in_hbm(weight), bias.reshape(1, count)],
        grid=(count // tile,),
        in_specs=[
            pl.BlockSpec((width, tokens), lambda j: (0, 0)),
            pl.BlockSpec((width, tile), lambda j: (0, j)),
            pl.BlockSpec((1, tile), lambda j: (0, j)),
        ],
        out_specs=[
            pl.BlockSpec((tokens, tile), lambda j: (0, j)),
            pl.BlockSpec((tile, tokens), lambda j: (j, 0)),
        ],
        scratch_shapes=[pltpu.VMEM((tokens, width), bf16)],
    )


def decode_kernel(latents_ref, weight_ref, target_ref, out_ref):
    tile = weight_ref.shape[1]
    step = pl.program_id(0)
    at = pl.multiple_of(step * tile, tile)
    out_ref[:, pl.ds(at, tile)] = product(latents_ref[...], weight_ref[...]).astype(bf16)

    @pl.when(step == 0)
    def _():
        rows, tokens = target_ref.shape
        spare = -rows % 128
        padded = jnp.concatenate([target_ref[...], jnp.zeros((spare, tokens), bf16)], axis=0)
        out_ref[:, out_ref.shape[1] - rows - spare :] = padded.T


def decode(latents, weight, turned_target, room):
    tokens, count = latents.shape
    width = weight.shape[1]
    tile = width // 7
    return call(
        decode_kernel,
        array((tokens, width + room)),
        2 * tokens * width * count,
        [latents, weight, turned_target],
        grid=(7,),
        in_specs=[WHOLE, pl.BlockSpec((count, tile), lambda j: (0, j)), WHOLE],
        out_specs=WHOLE,
    )


def total_of(pieces_ref, width):
    total = pieces_ref[0, :, :width].astype(f32)
    for k in range(1, pieces_ref.shape[0]):
        total += pieces_ref[k, :, :width].astype(f32)
    return total


def send_to_all(out_ref, rows):
    for k in range(out_ref.shape[0]):
        out_ref[k] = rows


def mean_of(values):
    return jnp.sum(values, axis=1, keepdims=True) / values.shape[1]


def recon_kernel(pieces_ref, bias_ref, gain_ref, out_ref, recon_ref):
    recon = total_of(pieces_ref, recon_ref.shape[1]) + bias_ref[...].astype(f32)
    recon_ref[...] = recon
    scale_in = lax.rsqrt(mean_of(recon * recon) + epsilon)
    send_to_all(out_ref, (recon * scale_in * gain_ref[...].astype(f32)).astype(bf16))


def output_kernel(token_count, pieces_ref, recon_ref, target_ref, gain_ref, out_ref, grad_ref):
    gain = gain_ref[...].astype(f32)
    output = total_of(pieces_ref, recon_ref.shape[1])
    scale_out = lax.rsqrt(mean_of(output * output) + epsilon)
    normed_out = output * scale_out
    result = recon_ref[...] + normed_out * gain
    grad_result = 2.0 * (result - target_ref[...].astype(f32)) / token_count
    grad_ref[...] = grad_result
    grad_normed = grad_result * gain
    inner = mean_of(grad_normed * normed_out)
    send_to_all(out_ref, (scale_out * (grad_normed - normed_out * inner)).astype(bf16))


def input_kernel(pieces_ref, recon_ref, grad_ref, gain_ref, out_ref):
    recon = recon_ref[...]
    scale_in = lax.rsqrt(mean_of(recon * recon) + epsilon)
    unit = recon * scale_in
    grad_unit = total_of(pieces_ref, recon_ref.shape[1]) * gain_ref[...].astype(f32)
    inner = mean_of(grad_unit * unit)
    send_to_all(out_ref, (grad_ref[...] + scale_in * (grad_unit - unit * inner)).astype(bf16))


def local(body, outs, args, kept=0):
    stay = len(args) - kept
    args = [*args[:stay], *(in_hbm(a) for a in args[stay:])]
    return call(body, outs, 0, args, in_specs=[WHOLE] * stay + [pl.BlockSpec()] * kept)


def parts_of(own, near, far):
    return [own, [near.at[k] for k in range(3)], [far.at[k] for k in range(3)]]


def forward_kernel(rows_ref, gate_ref, up_ref, down_ref, near_ref, far_ref, out_ref, *saved):
    root = 0.7978845608028654
    cube = 0.044715
    rows = rows_ref[...]
    parts = parts_of([gate_ref, up_ref, down_ref], near_ref, far_ref)
    hidden = []
    for (gate, up, _), gelu_ref, slope_ref in zip(parts, saved[0::2], saved[1::2]):
        gate_value = product_t(rows, gate[...])
        up_value = product_t(rows, up[...])
        square = gate_value * gate_value
        curve = jnp.tanh(root * gate_value * (1.0 + cube * square))
        half = 0.5 * (1.0 + curve)
        gelu_value = gate_value * half
        rise = 0.5 * gate_value * (1.0 - curve * curve) * root * (1.0 + 3.0 * cube * square)
        gelu_ref[...] = gelu_value
        slope_ref[...] = up_value * (half + rise)
        hidden.append((gelu_value * up_value).astype(bf16))
    for at in range(0, out_ref.shape[1], 512):
        span = slice(at, at + 512)
        terms = [product(h, down[:, span]) for h, (_, _, down) in zip(hidden, parts)]
        out_ref[:, span] = sum(terms[1:], terms[0]).astype(bf16)


def backward_kernel(rows_ref, gate_ref, up_ref, down_ref, near_ref, far_ref, *refs):
    saved, out_ref = refs[:-1], refs[-1]
    rows = rows_ref[...]
    parts = parts_of([gate_ref, up_ref, down_ref], near_ref, far_ref)
    grads = []
    for (_, _, down), gelu_ref, slope_ref in zip(parts, saved[0::2], saved[1::2]):
        grad_hidden = product_t(rows, down[...])
        grad_gate = (grad_hidden * slope_ref[...]).astype(bf16)
        grads.append((grad_gate, (grad_hidden * gelu_ref[...]).astype(bf16)))
    for at in range(0, out_ref.shape[1], 512):
        span = slice(at, at + 512)
        terms = []
        for (grad_gate, grad_up), (gate, up, _) in zip(grads, parts):
            terms += [product(grad_gate, gate[:, span]), product(grad_up, up[:, span])]
        out_ref[:, span] = sum(terms[1:], terms[0]).astype(bf16)


def latent_kernel(rows_ref, weight_ref, latents_ref, out_ref):
    grad_latent = product_t(rows_ref[...], weight_ref[...])
    out_ref[...] = jnp.where(latents_ref[...].astype(f32) > 0, grad_latent, 0.0).astype(bf16)


def grad_of_preact(rows, weight, latents, tile):
    tokens, width = rows.shape
    count = weight.shape[0]
    return call(
        latent_kernel,
        array((tokens, count)),
        2 * tokens * width * count,
        [rows, in_hbm(weight), latents],
        grid=(count // tile,),
        in_specs=[
            WHOLE,
            pl.BlockSpec((tile, width), lambda j: (j, 0)),
            pl.BlockSpec((tokens, tile), lambda j: (0, j)),
        ],
        out_specs=pl.BlockSpec((tokens, tile), lambda j: (0, j)),
    )


def products_kernel(spans, *refs):
    count = len(refs) // 2
    out_ref = refs[-1]
    for span in spans:
        total = product(refs[0][...], refs[count][:, span])
        for k in range(1, count):
            total += product(refs[k][...], refs[count + k][:, span])
        out_ref[:, span] = total.astype(bf16)


def sum_of_products(left, right, tile):
    rows, depth = left[0].shape
    columns = right[0].shape[1]
    spans = [slice(at, min(at + 256, tile)) for at in range(0, tile, 256)]
    return call(
        functools.partial(products_kernel, spans),
        array((rows, columns)),
        2 * rows * depth * columns * len(left),
        [*left, *right],
        grid=(columns // tile,),
        in_specs=[pl.BlockSpec((rows, depth), lambda j: (0, 0))] * len(left)
        + [pl.BlockSpec((depth, tile), lambda j: (0, j))] * len(right),
        out_specs=pl.BlockSpec((rows, tile), lambda j: (0, j)),
    )


def per_device(
    residual,
    target,
    encoder_weight,
    encoder_bias,
    decoder_weight,
    decoder_bias,
    first_gain,
    second_gain,
    gate_weight,
    up_weight,
    down_weight,
):
    tokens, share_width = residual.shape
    shards = lax.axis_size(SHARDS)
    copies = lax.axis_size(BATCH)
    width = share_width * shards
    block = width // copies
    own_tokens = tokens // shards
    token_count = tokens * copies
    offset = lax.axis_index(SHARDS) * share_width
    bias, gain_in, gain_out = (a.reshape(1, width) for a in (decoder_bias, first_gain, second_gain))
    gate, up = gate_weight.T, up_weight.T
    everyone = array((shards, own_tokens, width))
    half = lax.axis_size(HALF)
    half_of_them = hbm_array((half, own_tokens, width))
    own_rows = array((own_tokens, width), f32)

    def to_owners(partial, axes):
        return exchange(partial.reshape(lax.axis_size(axes), own_tokens, -1), axes)

    def all_tokens(pieces, axes):
        return exchange(pieces, axes).reshape(-1, width)

    units = gate.shape[0] // 2
    at = lax.axis_index(BATCH[1]) * units
    weights = [gate, up, down_weight]

    bias_share = lax.dynamic_slice_in_dim(decoder_bias.astype(f32), offset, share_width)
    centered_share = (residual.astype(f32) - bias_share).astype(bf16).T
    partner = swap(centered_share, SHARDS[1])
    first = lax.axis_index(SHARDS[1]) == 0
    pair = jnp.stack(
        [jnp.where(first, centered_share, partner), jnp.where(first, partner, centered_share)]
    )
    pieces = jnp.broadcast_to(pair, (lax.axis_size(HALF), *pair.shape))
    pieces, weights_then = lax.optimization_barrier((pieces, weights))
    sent = jnp.stack([lax.dynamic_slice_in_dim(w, at, units, axis=0) for w in weights_then])
    near = swap(sent, OTHER_HALF)
    far = swap(near, BATCH[1])
    centered = exchange(pieces, HALF).reshape(width, tokens)

    latents, turned_latents = encode(
        centered, encoder_weight, encoder_bias, share_width, 256
    )
    partial_recon = decode(latents, decoder_weight, target.T, 128)

    pieces = to_owners(partial_recon, SHARDS)
    own_target = pieces[:, :, width : width + share_width]
    own_target = jnp.moveaxis(own_target, 0, 1).reshape(own_tokens, width)
    pieces, recon = local(recon_kernel, [half_of_them, own_rows], [pieces, bias, gain_in])

    pieces, centered, turned_latents = lax.optimization_barrier((pieces, centered, turned_latents))
    normed_input = all_tokens(pieces, HALF)
    latent_blocks = copies_of_all(turned_latents)

    def feature_block(b):
        part = lax.dynamic_slice_in_dim(centered, b * block, block, axis=0)
        part = part.reshape(lax.axis_size(SHARDS[2]), lax.axis_size(SHARDS[1]), share_width, tokens)
        return jnp.swapaxes(part, 0, 1).reshape(block, tokens)

    centered_blocks = blocks_of_all(feature_block)
    rows = half * own_tokens
    saved = [hbm_array((rows, n), f32) for n in (2 * units, 2 * units, units, units, units, units)]
    partial_out, *saved = local(
        forward_kernel,
        [hbm_array((rows, width)), *saved],
        [normed_input, *weights, near, far],
    )

    pieces, grad_result = local(
        functools.partial(output_kernel, token_count),
        [half_of_them, own_rows],
        [to_owners(partial_out, HALF), recon, own_target, gain_out],
    )
    pieces, latent_blocks = lax.optimization_barrier((pieces, latent_blocks))
    grad_output = all_tokens(pieces, HALF)
    (partial_input,) = local(
        backward_kernel,
        [array((rows, width))],
        [grad_output, *weights, near, far, *saved],
        kept=6,
    )
    partial_input, centered_blocks = lax.optimization_barrier((partial_input, centered_blocks))
    (pieces,) = local(
        input_kernel, [everyone], [to_owners(partial_input, HALF), recon, grad_result, gain_in]
    )
    grad_recon = all_tokens(pieces, SHARDS)

    recon_blocks = blocks_of_all(
        lambda b: lax.dynamic_slice_in_dim(grad_recon, b * block, block, axis=1)
    )
    grad_preact = grad_of_preact(grad_recon, decoder_weight, latents, 256)
    encoder_grad = sum_of_products(centered_blocks, copies_of_all(grad_preact), 256)
    decoder_grad = sum_of_products(latent_blocks, recon_blocks, block)
    return encoder_grad, decoder_grad


def solution(mesh):
    batch, latent = mesh.shape["batch"], mesh.shape["latent"]
    split = Mesh(
        mesh.devices.reshape(2, batch // 2, mesh.shape["tensor"] // 2, 2, latent),
        BATCH + SHARDS,
    )
    in_specs = (
        P(BATCH, SHARDS),
        P(BATCH, SHARDS),
        P(None, SHARDS),
        P(SHARDS),
        P(SHARDS, None),
        P(),
        P(),
        P(),
        P(None, SHARDS),
        P(None, SHARDS),
        P(SHARDS, None),
    )
    out_specs = (P(BATCH, SHARDS), P(SHARDS, BATCH))
    return jax.shard_map(
        per_device, mesh=split, in_specs=in_specs, out_specs=out_specs, check_vma=False
    )
```

```python
import functools
import math

import jax
import jax.numpy as jnp
from jax import lax
from jax.experimental import pallas as pl
from jax.experimental.pallas import tpu as pltpu
from jax.sharding import Mesh
from jax.sharding import PartitionSpec as P

SHARDS = ("tensor_0", "tensor_1", "latent")
BATCH = ("batch_0", "batch_1")
HALF = ("tensor_0", "latent")
OWNERS = ("tensor_0", "latent", "tensor_1")
OTHER_HALF = ("batch_0", "tensor_1")

epsilon = 1e-06

f32 = jnp.float32
bf16 = jnp.bfloat16
LAST = (((1,), (1,)), ((), ()))
WHOLE = pl.BlockSpec(memory_space=pltpu.VMEM)
EFFORT = 8
LIMIT = 24 * 1024 * 1024


def exchange(pieces, axes):
    return lax.all_to_all(pieces, axes, split_axis=0, concat_axis=0, tiled=True)


def swap(block, axes):
    for_all = lax.axis_size(axes)
    return lax.ppermute(block, axes, [(i, for_all - 1 - i) for i in range(for_all)])


def copies_of_all(block):
    near = swap(block, BATCH[1])
    far = swap(block, BATCH[0])
    return [block, near, far, swap(far, BATCH[1])]


def blocks_of_all(block_at):
    own = lax.axis_index(BATCH)
    steps = ((1, BATCH[1]), (2, BATCH[0]), (3, BATCH))
    return [block_at(own)] + [swap(block_at(own ^ step), axes) for step, axes in steps]


def call(body, outs, flops, args, **more):
    arrays = [*args, *jax.tree.leaves(outs)]
    moved = sum(math.prod(a.shape) * jnp.dtype(a.dtype).itemsize for a in arrays)
    cost = pl.CostEstimate(flops=flops, bytes_accessed=moved, transcendentals=0)
    return pl.pallas_call(
        body,
        out_shape=outs,
        cost_estimate=cost,
        compiler_params=pltpu.CompilerParams(vmem_limit_bytes=LIMIT),
        **more,
    )(*args)


def array(shape, dtype=bf16):
    return jax.ShapeDtypeStruct(shape, dtype)


def hbm_array(shape, dtype=bf16):
    return pltpu.HBM(shape, dtype)


def in_hbm(value):
    return pltpu.with_memory_space_constraint(value, pltpu.HBM)


def product(left, right):
    return jnp.dot(left, right, preferred_element_type=f32)


def product_t(left, right):
    return lax.dot_general(left, right, LAST, preferred_element_type=f32)


def encode_kernel(centered_ref, weight_ref, bias_ref, latents_ref, turned_ref, rows_ref):
    width = centered_ref.shape[0]

    @pl.when(pl.program_id(0) == 0)
    def _():
        for at in range(0, width, 256):
            rows_ref[:, at : at + 256] = centered_ref[at : at + 256, :].T

    preact = product(rows_ref[...], weight_ref[...]) + bias_ref[...].astype(f32)
    latents = jnp.maximum(preact, 0.0).astype(bf16)
    latents_ref[...] = latents
    turned_ref[...] = latents.T


def encode(centered, weight, bias, tile):
    width, tokens = centered.shape
    count = weight.shape[1]
    return call(
        encode_kernel,
        [array((tokens, count)), hbm_array((count, tokens))],
        EFFORT * 2 * tokens * width * count,
        [centered, in_hbm(weight), bias.reshape(1, count)],
        grid=(count // tile,),
        in_specs=[
            pl.BlockSpec((width, tokens), lambda j: (0, 0)),
            pl.BlockSpec((width, tile), lambda j: (0, j)),
            pl.BlockSpec((1, tile), lambda j: (0, j)),
        ],
        out_specs=[
            pl.BlockSpec((tokens, tile), lambda j: (0, j)),
            pl.BlockSpec((tile, tokens), lambda j: (j, 0)),
        ],
        scratch_shapes=[pltpu.VMEM((tokens, width), bf16)],
    )


def decode_kernel(latents_ref, weight_ref, target_ref, out_ref):
    tile = weight_ref.shape[1]
    step = pl.program_id(0)
    at = pl.multiple_of(step * tile, tile)
    out_ref[:, pl.ds(at, tile)] = product(latents_ref[...], weight_ref[...]).astype(bf16)

    @pl.when(step == 0)
    def _():
        rows, tokens = target_ref.shape
        spare = -rows % 128
        padded = jnp.concatenate([target_ref[...], jnp.zeros((spare, tokens), bf16)], axis=0)
        out_ref[:, out_ref.shape[1] - rows - spare :] = padded.T


def decode(latents, weight, turned_target, room):
    tokens, count = latents.shape
    width = weight.shape[1]
    tile = width // 7
    return call(
        decode_kernel,
        array((tokens, width + room)),
        2 * tokens * width * count,
        [latents, weight, turned_target],
        grid=(7,),
        in_specs=[WHOLE, pl.BlockSpec((count, tile), lambda j: (0, j)), WHOLE],
        out_specs=WHOLE,
    )


def total_of(pieces_ref, width):
    total = pieces_ref[0, :, :width].astype(f32)
    for k in range(1, pieces_ref.shape[0]):
        total += pieces_ref[k, :, :width].astype(f32)
    return total


def send_to_all(out_ref, rows):
    for k in range(out_ref.shape[0]):
        out_ref[k] = rows


def mean_of(values):
    return jnp.sum(values, axis=1, keepdims=True) / values.shape[1]


def halves_kernel(side_ref, pieces_ref, sum_ref, target_ref, sent_ref):
    rows, width = sum_ref.shape
    count = pieces_ref.shape[0]
    first = side_ref[0] == 0
    total = total_of(pieces_ref, width)
    sum_ref[...] = jnp.where(first, total[:rows], total[rows:])
    sent_ref[:, :width] = jnp.where(first, total[rows:], total[:rows]).astype(bf16)
    for k in range(count):
        piece = pieces_ref[k, :, width:].astype(f32)
        target_ref[k] = jnp.where(first, piece[:rows], piece[rows:]).astype(bf16)
        other = jnp.where(first, piece[rows:], piece[:rows]).astype(bf16)
        sent_ref[:, width + 128 * k : width + 128 * (k + 1)] = other


def recon_kernel(sum_ref, partner_ref, bias_ref, gain_ref, out_ref, recon_ref):
    partner = partner_ref[:, : recon_ref.shape[1]].astype(f32)
    recon = sum_ref[...] + partner + bias_ref[...].astype(f32)
    recon_ref[...] = recon
    scale_in = lax.rsqrt(mean_of(recon * recon) + epsilon)
    send_to_all(out_ref, (recon * scale_in * gain_ref[...].astype(f32)).astype(bf16))


def output_kernel(token_count, pieces_ref, recon_ref, target_ref, gain_ref, out_ref, grad_ref):
    gain = gain_ref[...].astype(f32)
    output = total_of(pieces_ref, recon_ref.shape[1])
    scale_out = lax.rsqrt(mean_of(output * output) + epsilon)
    normed_out = output * scale_out
    result = recon_ref[...] + normed_out * gain
    grad_result = 2.0 * (result - target_ref[...].astype(f32)) / token_count
    grad_ref[...] = grad_result
    grad_normed = grad_result * gain
    inner = mean_of(grad_normed * normed_out)
    send_to_all(out_ref, (scale_out * (grad_normed - normed_out * inner)).astype(bf16))


def input_kernel(pieces_ref, recon_ref, grad_ref, gain_ref, out_ref):
    recon = recon_ref[...]
    scale_in = lax.rsqrt(mean_of(recon * recon) + epsilon)
    unit = recon * scale_in
    grad_unit = total_of(pieces_ref, recon_ref.shape[1]) * gain_ref[...].astype(f32)
    inner = mean_of(grad_unit * unit)
    send_to_all(out_ref, (grad_ref[...] + scale_in * (grad_unit - unit * inner)).astype(bf16))


def local(body, outs, args, kept=0):
    stay = len(args) - kept
    args = [*args[:stay], *(in_hbm(a) for a in args[stay:])]
    return call(body, outs, 0, args, in_specs=[WHOLE] * stay + [pl.BlockSpec()] * kept)


def parts_of(own, near, far):
    return [own, [near.at[k] for k in range(3)], [far.at[k] for k in range(3)]]


def forward_kernel(rows_ref, gate_ref, up_ref, down_ref, near_ref, far_ref, out_ref, *saved):
    root = 0.7978845608028654
    cube = 0.044715
    rows = rows_ref[...]
    parts = parts_of([gate_ref, up_ref, down_ref], near_ref, far_ref)
    hidden = []
    for (gate, up, _), gelu_ref, slope_ref in zip(parts, saved[0::2], saved[1::2]):
        gate_value = product_t(rows, gate[...])
        up_value = product_t(rows, up[...])
        square = gate_value * gate_value
        curve = jnp.tanh(root * gate_value * (1.0 + cube * square))
        half = 0.5 * (1.0 + curve)
        gelu_value = gate_value * half
        rise = 0.5 * gate_value * (1.0 - curve * curve) * root * (1.0 + 3.0 * cube * square)
        gelu_ref[...] = gelu_value
        slope_ref[...] = up_value * (half + rise)
        hidden.append((gelu_value * up_value).astype(bf16))
    for at in range(0, out_ref.shape[1], 512):
        span = slice(at, at + 512)
        terms = [product(h, down[:, span]) for h, (_, _, down) in zip(hidden, parts)]
        out_ref[:, span] = sum(terms[1:], terms[0]).astype(bf16)


def backward_kernel(rows_ref, gate_ref, up_ref, down_ref, near_ref, far_ref, *refs):
    saved, out_ref = refs[:-1], refs[-1]
    rows = rows_ref[...]
    parts = parts_of([gate_ref, up_ref, down_ref], near_ref, far_ref)
    grads = []
    for (_, _, down), gelu_ref, slope_ref in zip(parts, saved[0::2], saved[1::2]):
        grad_hidden = product_t(rows, down[...])
        grad_gate = (grad_hidden * slope_ref[...]).astype(bf16)
        grads.append((grad_gate, (grad_hidden * gelu_ref[...]).astype(bf16)))
    for at in range(0, out_ref.shape[1], 512):
        span = slice(at, at + 512)
        terms = []
        for (grad_gate, grad_up), (gate, up, _) in zip(grads, parts):
            terms += [product(grad_gate, gate[:, span]), product(grad_up, up[:, span])]
        out_ref[:, span] = sum(terms[1:], terms[0]).astype(bf16)


def latent_kernel(rows_ref, weight_ref, latents_ref, out_ref):
    grad_latent = product_t(rows_ref[...], weight_ref[...])
    out_ref[...] = jnp.where(latents_ref[...].astype(f32) > 0, grad_latent, 0.0).astype(bf16)


def grad_of_preact(rows, weight, latents, tile):
    tokens, width = rows.shape
    count = weight.shape[0]
    return call(
        latent_kernel,
        array((tokens, count)),
        2 * tokens * width * count,
        [rows, weight, latents],
        grid=(count // tile,),
        in_specs=[
            WHOLE,
            pl.BlockSpec((tile, width), lambda j: (j, 0)),
            pl.BlockSpec((tokens, tile), lambda j: (0, j)),
        ],
        out_specs=pl.BlockSpec((tokens, tile), lambda j: (0, j)),
    )


def products_kernel(spans, count, *refs):
    out_ref = refs[-1]
    for span in spans:
        total = refs[2 * count][:, span] if len(refs) > 2 * count + 1 else None
        for k in range(count):
            term = product(refs[k][...], refs[count + k][:, span])
            total = term if total is None else total + term
        out_ref[:, span] = total.astype(out_ref.dtype)


def sum_of_products(left, right, tile, rows_tile=None, start=None, kind=bf16):
    rows, depth = left[0].shape
    columns = right[0].shape[1]
    rows_tile = rows_tile or rows
    spans = [slice(at, min(at + 256, tile)) for at in range(0, tile, 256)]
    count = len(left)
    out_spec = pl.BlockSpec((rows_tile, tile), lambda i, j: (i, j))
    return call(
        functools.partial(products_kernel, spans, count),
        array((rows, columns), kind),
        2 * rows * depth * columns * count,
        [*map(in_hbm, left), *right, *([] if start is None else [start])],
        grid=(rows // rows_tile, columns // tile),
        in_specs=[pl.BlockSpec((rows_tile, depth), lambda i, j: (i, 0))] * count
        + [pl.BlockSpec((depth, tile), lambda i, j: (0, j))] * count
        + ([] if start is None else [out_spec]),
        out_specs=out_spec,
    )


def per_device(
    residual,
    target,
    encoder_weight,
    encoder_bias,
    decoder_weight,
    decoder_bias,
    first_gain,
    second_gain,
    gate_weight,
    up_weight,
    down_weight,
):
    tokens, share_width = residual.shape
    shards = lax.axis_size(SHARDS)
    copies = lax.axis_size(BATCH)
    width = share_width * shards
    block = width // copies
    own_tokens = tokens // shards
    token_count = tokens * copies
    offset = lax.axis_index(SHARDS) * share_width
    bias, gain_in, gain_out = (a.reshape(1, width) for a in (decoder_bias, first_gain, second_gain))
    gate, up = gate_weight.T, up_weight.T
    everyone = array((shards, own_tokens, width))
    half = lax.axis_size(HALF)
    half_of_them = hbm_array((half, own_tokens, width))
    own_rows = array((own_tokens, width), f32)

    def to_owners(partial, axes):
        return exchange(partial.reshape(lax.axis_size(axes), own_tokens, -1), axes)

    def all_tokens(pieces, axes):
        return exchange(pieces, axes).reshape(-1, width)

    units = gate.shape[0] // 2
    at = lax.axis_index(BATCH[1]) * units
    weights = [gate, up, down_weight]

    bias_share = lax.dynamic_slice_in_dim(decoder_bias.astype(f32), offset, share_width)
    centered_share = (residual.astype(f32) - bias_share).astype(bf16).T
    pieces = jnp.broadcast_to(centered_share, (shards, share_width, tokens))
    pieces, weights_then = lax.optimization_barrier((pieces, weights))
    sent = jnp.stack([lax.dynamic_slice_in_dim(w, at, units, axis=0) for w in weights_then])
    near = swap(sent, OTHER_HALF)
    far = swap(near, BATCH[1])
    centered = exchange(pieces, SHARDS).reshape(width, tokens)

    latents, turned_latents = encode(centered, encoder_weight, encoder_bias, 256)
    partial_recon = decode(latents, decoder_weight, target.T, 128)

    pieces = exchange(partial_recon.reshape(half, 2 * own_tokens, -1), HALF)
    side = lax.axis_index(SHARDS[1]).reshape(1)
    own_sum, own_targets, sent = call(
        halves_kernel,
        [
            array((own_tokens, width), f32),
            hbm_array((half, own_tokens, 128)),
            array((own_tokens, width + half * 128)),
        ],
        0,
        [side, pieces],
        in_specs=[pl.BlockSpec(memory_space=pltpu.SMEM), WHOLE],
    )
    partner = swap(sent, SHARDS[1])
    pieces, recon = local(
        recon_kernel, [half_of_them, own_rows], [own_sum, partner, bias, gain_in]
    )
    partner_targets = partner[:, width:].reshape(own_tokens, half, 128)
    targets = jnp.stack([jnp.moveaxis(own_targets, 0, 1), partner_targets], axis=2)
    targets = jnp.where(side[0] == 0, targets, jnp.flip(targets, 2))[..., :share_width]
    targets = targets.reshape(own_tokens, *(lax.axis_size(a) for a in OWNERS), share_width)
    own_target = jnp.swapaxes(targets, 2, 3).reshape(own_tokens, width)

    pieces, centered, turned_latents = lax.optimization_barrier((pieces, centered, turned_latents))
    normed_input = all_tokens(pieces, HALF)
    latent_blocks = copies_of_all(turned_latents)

    centered_blocks = blocks_of_all(
        lambda b: lax.dynamic_slice_in_dim(centered, b * block, block, axis=0)
    )
    rows = half * own_tokens
    saved = [hbm_array((rows, n), f32) for n in (2 * units, 2 * units, units, units, units, units)]
    partial_out, *saved = local(
        forward_kernel,
        [hbm_array((rows, width)), *saved],
        [normed_input, *weights, near, far],
    )

    pieces, grad_result = local(
        functools.partial(output_kernel, token_count),
        [half_of_them, own_rows],
        [to_owners(partial_out, HALF), recon, own_target, gain_out],
    )
    pieces, latent_blocks, centered_blocks[:3] = lax.optimization_barrier(
        (pieces, latent_blocks, centered_blocks[:3])
    )
    grad_output = all_tokens(pieces, HALF)
    (partial_input,) = local(
        backward_kernel,
        [array((rows, width))],
        [grad_output, *weights, near, far, *saved],
        kept=11,
    )
    partial_input, centered_blocks[3] = lax.optimization_barrier(
        (partial_input, centered_blocks[3])
    )
    (pieces,) = local(
        input_kernel, [everyone], [to_owners(partial_input, HALF), recon, grad_result, gain_in]
    )
    grad_recon = all_tokens(pieces, OWNERS)

    recon_blocks = blocks_of_all(
        lambda b: lax.dynamic_slice_in_dim(grad_recon, b * block, block, axis=1)
    )
    grad_preact = grad_of_preact(grad_recon, decoder_weight, latents, 256)
    part = sum_of_products(latent_blocks[:3], recon_blocks[:3], block, kind=f32)
    encoder_grad = sum_of_products(centered_blocks, copies_of_all(grad_preact), 256)
    part, encoder_grad = lax.optimization_barrier((part, encoder_grad))
    decoder_grad = sum_of_products(latent_blocks[3:], recon_blocks[3:], block, 256, part)
    return encoder_grad, decoder_grad


def solution(mesh):
    batch, latent = mesh.shape["batch"], mesh.shape["latent"]
    split = Mesh(
        mesh.devices.reshape(2, batch // 2, mesh.shape["tensor"] // 2, 2, latent),
        BATCH + SHARDS,
    )
    in_specs = (
        P(BATCH, SHARDS),
        P(BATCH, SHARDS),
        P(None, SHARDS),
        P(SHARDS),
        P(SHARDS, None),
        P(),
        P(),
        P(),
        P(None, SHARDS),
        P(None, SHARDS),
        P(SHARDS, None),
    )
    out_specs = (P(BATCH, SHARDS), P(SHARDS, BATCH))
    return jax.shard_map(
        per_device, mesh=split, in_specs=in_specs, out_specs=out_specs, check_vma=False
    )
```

```python
import functools
import math

import jax
import jax.numpy as jnp
from jax import lax
from jax.experimental import pallas as pl
from jax.experimental.pallas import tpu as pltpu
from jax.sharding import Mesh
from jax.sharding import PartitionSpec as P

SHARDS = ("tensor_0", "tensor_1", "latent")
BATCH = ("batch_0", "batch_1")
HALF = ("tensor_0", "latent")
OWNERS = ("tensor_0", "latent", "tensor_1")
OTHER_HALF = ("batch_0", "tensor_1")

epsilon = 1e-06

f32 = jnp.float32
bf16 = jnp.bfloat16
LAST = (((1,), (1,)), ((), ()))
WHOLE = pl.BlockSpec(memory_space=pltpu.VMEM)
EFFORT = 8
LIGHT = 1.0
LIMIT = 24 * 1024 * 1024


def exchange(pieces, axes):
    return lax.all_to_all(pieces, axes, split_axis=0, concat_axis=0, tiled=True)


def swap(block, axes):
    for_all = lax.axis_size(axes)
    return lax.ppermute(block, axes, [(i, for_all - 1 - i) for i in range(for_all)])


def copies_of_all(block):
    near = swap(block, BATCH[1])
    far = swap(block, BATCH[0])
    return [block, near, far, swap(far, BATCH[1])]


def blocks_of_all(block_at):
    own = lax.axis_index(BATCH)
    steps = ((1, BATCH[1]), (2, BATCH[0]), (3, BATCH))
    return [block_at(own)] + [swap(block_at(own ^ step), axes) for step, axes in steps]


def call(body, outs, flops, args, effort=1.0, **more):
    arrays = [*args, *jax.tree.leaves(outs)]
    moved = sum(math.prod(a.shape) * jnp.dtype(a.dtype).itemsize for a in arrays)
    cost = pl.CostEstimate(
        flops=int(effort * flops), bytes_accessed=int(effort * moved), transcendentals=0
    )
    return pl.pallas_call(
        body,
        out_shape=outs,
        cost_estimate=cost,
        compiler_params=pltpu.CompilerParams(vmem_limit_bytes=LIMIT),
        **more,
    )(*args)


def array(shape, dtype=bf16):
    return jax.ShapeDtypeStruct(shape, dtype)


def hbm_array(shape, dtype=bf16):
    return pltpu.HBM(shape, dtype)


def in_hbm(value):
    return pltpu.with_memory_space_constraint(value, pltpu.HBM)


def product(left, right):
    return jnp.dot(left, right, preferred_element_type=f32)


def product_t(left, right):
    return lax.dot_general(left, right, LAST, preferred_element_type=f32)


def encode_kernel(centered_ref, weight_ref, bias_ref, latents_ref, turned_ref, rows_ref):
    width = centered_ref.shape[0]

    @pl.when(pl.program_id(0) == 0)
    def _():
        for at in range(0, width, 256):
            rows_ref[:, at : at + 256] = centered_ref[at : at + 256, :].T

    preact = product(rows_ref[...], weight_ref[...]) + bias_ref[...].astype(f32)
    latents = jnp.maximum(preact, 0.0).astype(bf16)
    latents_ref[...] = latents
    turned_ref[...] = latents.T


def encode(centered, weight, bias, tile):
    width, tokens = centered.shape
    count = weight.shape[1]
    return call(
        encode_kernel,
        [array((tokens, count)), hbm_array((count, tokens))],
        2 * tokens * width * count,
        [centered, in_hbm(weight), bias.reshape(1, count)],
        EFFORT,
        grid=(count // tile,),
        in_specs=[
            pl.BlockSpec((width, tokens), lambda j: (0, 0)),
            pl.BlockSpec((width, tile), lambda j: (0, j)),
            pl.BlockSpec((1, tile), lambda j: (0, j)),
        ],
        out_specs=[
            pl.BlockSpec((tokens, tile), lambda j: (0, j)),
            pl.BlockSpec((tile, tokens), lambda j: (j, 0)),
        ],
        scratch_shapes=[pltpu.VMEM((tokens, width), bf16)],
    )


def decode_kernel(latents_ref, weight_ref, target_ref, out_ref):
    tile = weight_ref.shape[1]
    step = pl.program_id(0)
    at = pl.multiple_of(step * tile, tile)
    out_ref[:, pl.ds(at, tile)] = product(latents_ref[...], weight_ref[...]).astype(bf16)

    @pl.when(step == 0)
    def _():
        rows, tokens = target_ref.shape
        spare = -rows % 128
        padded = jnp.concatenate([target_ref[...], jnp.zeros((spare, tokens), bf16)], axis=0)
        out_ref[:, out_ref.shape[1] - rows - spare :] = padded.T


def decode(latents, weight, turned_target, room):
    tokens, count = latents.shape
    width = weight.shape[1]
    tile = width // 7
    return call(
        decode_kernel,
        array((tokens, width + room)),
        2 * tokens * width * count,
        [latents, weight, turned_target],
        grid=(7,),
        in_specs=[WHOLE, pl.BlockSpec((count, tile), lambda j: (0, j)), WHOLE],
        out_specs=WHOLE,
    )


def total_of(pieces_ref, width):
    total = pieces_ref[0, :, :width].astype(f32)
    for k in range(1, pieces_ref.shape[0]):
        total += pieces_ref[k, :, :width].astype(f32)
    return total


def send_to_all(out_ref, rows):
    for k in range(out_ref.shape[0]):
        out_ref[k] = rows


def mean_of(values):
    return jnp.sum(values, axis=1, keepdims=True) / values.shape[1]


def halves_kernel(side_ref, pieces_ref, sum_ref, target_ref, sent_ref):
    rows, width = sum_ref.shape
    count = pieces_ref.shape[0]
    first = side_ref[0] == 0
    total = total_of(pieces_ref, width)
    sum_ref[...] = jnp.where(first, total[:rows], total[rows:])
    sent_ref[:, :width] = jnp.where(first, total[rows:], total[:rows]).astype(bf16)
    for k in range(count):
        piece = pieces_ref[k, :, width:].astype(f32)
        target_ref[k] = jnp.where(first, piece[:rows], piece[rows:]).astype(bf16)
        other = jnp.where(first, piece[rows:], piece[:rows]).astype(bf16)
        sent_ref[:, width + 128 * k : width + 128 * (k + 1)] = other


def recon_kernel(sum_ref, partner_ref, bias_ref, gain_ref, out_ref, recon_ref):
    partner = partner_ref[:, : recon_ref.shape[1]].astype(f32)
    recon = sum_ref[...] + partner + bias_ref[...].astype(f32)
    recon_ref[...] = recon
    scale_in = lax.rsqrt(mean_of(recon * recon) + epsilon)
    send_to_all(out_ref, (recon * scale_in * gain_ref[...].astype(f32)).astype(bf16))


def output_kernel(token_count, pieces_ref, recon_ref, target_ref, gain_ref, out_ref, grad_ref):
    gain = gain_ref[...].astype(f32)
    output = total_of(pieces_ref, recon_ref.shape[1])
    scale_out = lax.rsqrt(mean_of(output * output) + epsilon)
    normed_out = output * scale_out
    result = recon_ref[...] + normed_out * gain
    grad_result = 2.0 * (result - target_ref[...].astype(f32)) / token_count
    grad_ref[...] = grad_result
    grad_normed = grad_result * gain
    inner = mean_of(grad_normed * normed_out)
    send_to_all(out_ref, (scale_out * (grad_normed - normed_out * inner)).astype(bf16))


def input_kernel(pieces_ref, recon_ref, grad_ref, gain_ref, out_ref):
    recon = recon_ref[...]
    scale_in = lax.rsqrt(mean_of(recon * recon) + epsilon)
    unit = recon * scale_in
    grad_unit = total_of(pieces_ref, recon_ref.shape[1]) * gain_ref[...].astype(f32)
    inner = mean_of(grad_unit * unit)
    send_to_all(out_ref, (grad_ref[...] + scale_in * (grad_unit - unit * inner)).astype(bf16))


def local(body, outs, args, kept=0):
    stay = len(args) - kept
    args = [*args[:stay], *(in_hbm(a) for a in args[stay:])]
    return call(body, outs, 0, args, in_specs=[WHOLE] * stay + [pl.BlockSpec()] * kept)


def parts_of(own, near, far):
    return [own, [near.at[k] for k in range(3)], [far.at[k] for k in range(3)]]


def forward_kernel(rows_ref, gate_ref, up_ref, down_ref, near_ref, far_ref, out_ref, *saved):
    root = 0.7978845608028654
    cube = 0.044715
    rows = rows_ref[...]
    parts = parts_of([gate_ref, up_ref, down_ref], near_ref, far_ref)
    hidden = []
    for (gate, up, _), gelu_ref, slope_ref in zip(parts, saved[0::2], saved[1::2]):
        gate_value = product_t(rows, gate[...])
        up_value = product_t(rows, up[...])
        square = gate_value * gate_value
        curve = jnp.tanh(root * gate_value * (1.0 + cube * square))
        half = 0.5 * (1.0 + curve)
        gelu_value = gate_value * half
        rise = 0.5 * gate_value * (1.0 - curve * curve) * root * (1.0 + 3.0 * cube * square)
        gelu_ref[...] = gelu_value
        slope_ref[...] = up_value * (half + rise)
        hidden.append((gelu_value * up_value).astype(bf16))
    for at in range(0, out_ref.shape[1], 512):
        span = slice(at, at + 512)
        terms = [product(h, down[:, span]) for h, (_, _, down) in zip(hidden, parts)]
        out_ref[:, span] = sum(terms[1:], terms[0]).astype(bf16)


def backward_kernel(rows_ref, gate_ref, up_ref, down_ref, near_ref, far_ref, *refs):
    saved, out_ref, (own, near, far, sems) = refs[:6], refs[6], refs[7:]
    pairs = [(down_ref, own.at[2]), (near_ref.at[2], near.at[2]), (far_ref.at[2], far.at[2])]
    pairs += [(gate_ref, own.at[0]), (near_ref.at[0], near.at[0]), (far_ref.at[0], far.at[0])]
    pairs += [(up_ref, own.at[1]), (near_ref.at[1], near.at[1]), (far_ref.at[1], far.at[1])]
    copies = [pltpu.make_async_copy(*pair, sems.at[k]) for k, pair in enumerate(pairs)]
    for copy in copies:
        copy.start()
    rows = rows_ref[...]
    grads = []
    for k, (part, gelu_ref, slope_ref) in enumerate(
        zip((own, near, far), saved[0::2], saved[1::2])
    ):
        copies[k].wait()
        grad_hidden = product_t(rows, part[2])
        grad_gate = (grad_hidden * slope_ref[...]).astype(bf16)
        grads.append((grad_gate, (grad_hidden * gelu_ref[...]).astype(bf16)))
    for copy in copies[3:]:
        copy.wait()
    for at in range(0, out_ref.shape[1], 512):
        span = slice(at, at + 512)
        terms = []
        for (grad_gate, grad_up), part in zip(grads, (own, near, far)):
            terms += [product(grad_gate, part[0, :, span]), product(grad_up, part[1, :, span])]
        out_ref[:, span] = sum(terms[1:], terms[0]).astype(bf16)


def backward(rows, weights, near, far, saved):
    anywhere = pl.BlockSpec(memory_space=pl.ANY)
    units, width = weights[0].shape
    tokens = rows.shape[0]
    return call(
        backward_kernel,
        array((tokens, width)),
        12 * tokens * width * units,
        [rows, *(in_hbm(a) for a in (*weights, near, far, *saved))],
        in_specs=[WHOLE] + [anywhere] * 5 + [pl.BlockSpec()] * len(saved),
        scratch_shapes=[pltpu.VMEM((3, units, width), bf16)]
        + [pltpu.VMEM(near.shape, bf16)] * 2
        + [pltpu.SemaphoreType.DMA((9,))],
    )


def latent_kernel(rows_ref, weight_ref, latents_ref, out_ref):
    grad_latent = product_t(rows_ref[...], weight_ref[...])
    out_ref[...] = jnp.where(latents_ref[...].astype(f32) > 0, grad_latent, 0.0).astype(bf16)


def grad_of_preact(rows, weight, latents, tile):
    tokens, width = rows.shape
    count = weight.shape[0]
    return call(
        latent_kernel,
        array((tokens, count)),
        2 * tokens * width * count,
        [rows, weight, latents],
        grid=(count // tile,),
        in_specs=[
            WHOLE,
            pl.BlockSpec((tile, width), lambda j: (j, 0)),
            pl.BlockSpec((tokens, tile), lambda j: (0, j)),
        ],
        out_specs=pl.BlockSpec((tokens, tile), lambda j: (0, j)),
    )


def products_kernel(spans, count, *refs):
    out_ref = refs[-1]
    for span in spans:
        total = None
        if len(refs) > 2 * count + 1:
            rows = out_ref.shape[0]
            at = pl.multiple_of(pl.program_id(0) * rows, rows)
            total = refs[2 * count][pl.ds(at, rows), span]
        for k in range(count):
            term = product(refs[k][...], refs[count + k][:, span])
            total = term if total is None else total + term
        out_ref[:, span] = total.astype(out_ref.dtype)


def sum_of_products(left, right, tile, rows_tile=None, start=None, kind=bf16, effort=LIGHT):
    rows, depth = left[0].shape
    columns = right[0].shape[1]
    rows_tile = rows_tile or rows
    spans = [slice(at, min(at + 256, tile)) for at in range(0, tile, 256)]
    count = len(left)
    out_spec = pl.BlockSpec((rows_tile, tile), lambda i, j: (i, j))
    return call(
        functools.partial(products_kernel, spans, count),
        array((rows, columns), kind),
        2 * rows * depth * columns * count,
        [*map(in_hbm, left), *right, *([] if start is None else [start])],
        effort,
        grid=(rows // rows_tile, columns // tile),
        in_specs=[pl.BlockSpec((rows_tile, depth), lambda i, j: (i, 0))] * count
        + [pl.BlockSpec((depth, tile), lambda i, j: (0, j))] * count
        + ([] if start is None else [WHOLE]),
        out_specs=out_spec,
    )


def per_device(
    residual,
    target,
    encoder_weight,
    encoder_bias,
    decoder_weight,
    decoder_bias,
    first_gain,
    second_gain,
    gate_weight,
    up_weight,
    down_weight,
):
    tokens, share_width = residual.shape
    shards = lax.axis_size(SHARDS)
    copies = lax.axis_size(BATCH)
    width = share_width * shards
    block = width // copies
    own_tokens = tokens // shards
    token_count = tokens * copies
    offset = lax.axis_index(SHARDS) * share_width
    bias, gain_in, gain_out = (a.reshape(1, width) for a in (decoder_bias, first_gain, second_gain))
    gate, up = gate_weight.T, up_weight.T
    everyone = array((shards, own_tokens, width))
    half = lax.axis_size(HALF)
    half_of_them = hbm_array((half, own_tokens, width))
    own_rows = array((own_tokens, width), f32)

    def to_owners(partial, axes):
        return exchange(partial.reshape(lax.axis_size(axes), own_tokens, -1), axes)

    def all_tokens(pieces, axes):
        return exchange(pieces, axes).reshape(-1, width)

    units = gate.shape[0] // 2
    at = lax.axis_index(BATCH[1]) * units
    weights = [gate, up, down_weight]

    bias_share = lax.dynamic_slice_in_dim(decoder_bias.astype(f32), offset, share_width)
    centered_share = (residual.astype(f32) - bias_share).astype(bf16).T
    pieces = jnp.broadcast_to(centered_share, (shards, share_width, tokens))
    pieces, weights_then = lax.optimization_barrier((pieces, weights))
    sent = jnp.stack([lax.dynamic_slice_in_dim(w, at, units, axis=0) for w in weights_then])
    near = swap(sent, OTHER_HALF)
    centered = exchange(pieces, SHARDS).reshape(width, tokens)

    latents, turned_latents = encode(centered, encoder_weight, encoder_bias, 256)
    partial_recon = decode(latents, decoder_weight, target.T, 128)

    partial_recon, centered, turned_latents = lax.optimization_barrier(
        (partial_recon, centered, turned_latents)
    )
    far_latents = swap(turned_latents, BATCH[0])
    centered_blocks = blocks_of_all(
        lambda b: lax.dynamic_slice_in_dim(centered, b * block, block, axis=0)
    )
    pieces = exchange(partial_recon.reshape(half, 2 * own_tokens, -1), HALF)
    side = lax.axis_index(SHARDS[1]).reshape(1)
    own_sum, own_targets, sent = call(
        halves_kernel,
        [
            array((own_tokens, width), f32),
            hbm_array((half, own_tokens, 128)),
            array((own_tokens, width + half * 128)),
        ],
        0,
        [side, pieces],
        in_specs=[pl.BlockSpec(memory_space=pltpu.SMEM), WHOLE],
    )
    sent, far_latents, centered_blocks[3] = lax.optimization_barrier(
        (sent, far_latents, centered_blocks[3])
    )
    partner = swap(sent, SHARDS[1])
    pieces, recon = local(
        recon_kernel, [half_of_them, own_rows], [own_sum, partner, bias, gain_in]
    )
    partner_targets = partner[:, width:].reshape(own_tokens, half, 128)
    targets = jnp.stack([jnp.moveaxis(own_targets, 0, 1), partner_targets], axis=2)
    targets = jnp.where(side[0] == 0, targets, jnp.flip(targets, 2))[..., :share_width]
    targets = targets.reshape(own_tokens, *(lax.axis_size(a) for a in OWNERS), share_width)
    own_target = jnp.swapaxes(targets, 2, 3).reshape(own_tokens, width)

    pieces, near = lax.optimization_barrier((pieces, near))
    far = swap(near, BATCH[1])
    normed_input = all_tokens(pieces, HALF)
    rows = half * own_tokens
    saved = [hbm_array((rows, n), f32) for n in (2 * units, 2 * units, units, units, units, units)]
    partial_out, *saved = local(
        forward_kernel,
        [hbm_array((rows, width)), *saved],
        [normed_input, *weights, near, far],
    )

    partial_out, centered_blocks[2] = lax.optimization_barrier((partial_out, centered_blocks[2]))

    pieces, grad_result = local(
        functools.partial(output_kernel, token_count),
        [half_of_them, own_rows],
        [to_owners(partial_out, HALF), recon, own_target, gain_out],
    )
    latent_blocks = [turned_latents, swap(turned_latents, BATCH[1])]
    latent_blocks += [far_latents, swap(far_latents, BATCH[1])]
    pieces, latent_blocks, centered_blocks[1] = lax.optimization_barrier(
        (pieces, latent_blocks, centered_blocks[1])
    )
    grad_output = all_tokens(pieces, HALF)
    partial_input = backward(grad_output, weights, near, far, saved)
    (pieces,) = local(
        input_kernel, [everyone], [to_owners(partial_input, HALF), recon, grad_result, gain_in]
    )
    grad_recon = all_tokens(pieces, OWNERS)

    own = lax.axis_index(BATCH)
    recon_blocks = [
        lax.dynamic_slice_in_dim(grad_recon, (own ^ step) * block, block, axis=1)
        for step in range(copies)
    ]
    recon_blocks[2] = swap(recon_blocks[2], BATCH[0])
    recon_blocks[3] = swap(recon_blocks[3], BATCH)
    grad_preact = grad_of_preact(grad_recon, decoder_weight, latents, 256)
    far = swap(grad_preact, BATCH[0])
    far, near, recon_blocks[1] = lax.optimization_barrier((far, grad_preact, recon_blocks[1]))
    recon_blocks[1] = swap(recon_blocks[1], BATCH[1])
    preact_blocks = [grad_preact, swap(near, BATCH[1]), far, swap(far, BATCH[1])]
    part = sum_of_products(latent_blocks[:3], recon_blocks[:3], block, kind=f32)
    encoder_grad = sum_of_products(centered_blocks, preact_blocks, 256)
    part, encoder_grad = lax.optimization_barrier((part, encoder_grad))
    decoder_grad = sum_of_products(latent_blocks[3:], recon_blocks[3:], block, 256, part)
    return encoder_grad, decoder_grad


def solution(mesh):
    batch, latent = mesh.shape["batch"], mesh.shape["latent"]
    split = Mesh(
        mesh.devices.reshape(2, batch // 2, mesh.shape["tensor"] // 2, 2, latent),
        BATCH + SHARDS,
    )
    in_specs = (
        P(BATCH, SHARDS),
        P(BATCH, SHARDS),
        P(None, SHARDS),
        P(SHARDS),
        P(SHARDS, None),
        P(),
        P(),
        P(),
        P(None, SHARDS),
        P(None, SHARDS),
        P(SHARDS, None),
    )
    out_specs = (P(BATCH, SHARDS), P(SHARDS, BATCH))
    return jax.shard_map(
        per_device, mesh=split, in_specs=in_specs, out_specs=out_specs, check_vma=False
    )
```

```python
import functools
import math

import jax
import jax.numpy as jnp
from jax import lax
from jax.experimental import pallas as pl
from jax.experimental.pallas import tpu as pltpu
from jax.sharding import Mesh
from jax.sharding import PartitionSpec as P

SHARDS = ("tensor_0", "tensor_1", "latent")
BATCH = ("batch_0", "batch_1")
HALF = ("tensor_0", "latent")
OWNERS = ("tensor_0", "latent", "tensor_1")
OTHER_HALF = ("batch_0", "tensor_1")

epsilon = 1e-06

f32 = jnp.float32
bf16 = jnp.bfloat16
LAST = (((1,), (1,)), ((), ()))
WHOLE = pl.BlockSpec(memory_space=pltpu.VMEM)
EFFORT = 8
LIGHT = 1.0
LIMIT = 24 * 1024 * 1024


def exchange(pieces, axes):
    return lax.all_to_all(pieces, axes, split_axis=0, concat_axis=0, tiled=True)


def swap(block, axes):
    for_all = lax.axis_size(axes)
    return lax.ppermute(block, axes, [(i, for_all - 1 - i) for i in range(for_all)])


def copies_of_all(block):
    near = swap(block, BATCH[1])
    far = swap(block, BATCH[0])
    return [block, near, far, swap(far, BATCH[1])]


def blocks_of_all(block_at):
    own = lax.axis_index(BATCH)
    steps = ((1, BATCH[1]), (2, BATCH[0]), (3, BATCH))
    return [block_at(own)] + [swap(block_at(own ^ step), axes) for step, axes in steps]


def call(body, outs, flops, args, effort=1.0, **more):
    arrays = [*args, *jax.tree.leaves(outs)]
    moved = sum(math.prod(a.shape) * jnp.dtype(a.dtype).itemsize for a in arrays)
    cost = pl.CostEstimate(
        flops=int(effort * flops), bytes_accessed=int(effort * moved), transcendentals=0
    )
    return pl.pallas_call(
        body,
        out_shape=outs,
        cost_estimate=cost,
        compiler_params=pltpu.CompilerParams(vmem_limit_bytes=LIMIT),
        **more,
    )(*args)


def array(shape, dtype=bf16):
    return jax.ShapeDtypeStruct(shape, dtype)


def hbm_array(shape, dtype=bf16):
    return pltpu.HBM(shape, dtype)


def in_hbm(value):
    return pltpu.with_memory_space_constraint(value, pltpu.HBM)


def product(left, right):
    return jnp.dot(left, right, preferred_element_type=f32)


def product_t(left, right):
    return lax.dot_general(left, right, LAST, preferred_element_type=f32)


def encode_kernel(centered_ref, weight_ref, bias_ref, latents_ref, turned_ref, rows_ref):
    width = centered_ref.shape[0]

    def finish(total):
        latents = jnp.maximum(total + bias_ref[...].astype(f32), 0.0).astype(bf16)
        latents_ref[...] = latents
        turned_ref[...] = latents.T

    @pl.when(pl.program_id(0) == 0)
    def _():
        total = None
        for at in range(0, width, 256):
            chunk = centered_ref[at : at + 256, :].T
            rows_ref[:, at : at + 256] = chunk
            term = product(chunk, weight_ref[at : at + 256, :])
            total = term if total is None else total + term
        finish(total)

    @pl.when(pl.program_id(0) > 0)
    def _():
        finish(product(rows_ref[...], weight_ref[...]))


def encode(centered, weight, bias, tile):
    width, tokens = centered.shape
    count = weight.shape[1]
    return call(
        encode_kernel,
        [array((tokens, count)), hbm_array((count, tokens))],
        2 * tokens * width * count,
        [centered, in_hbm(weight), bias.reshape(1, count)],
        EFFORT,
        grid=(count // tile,),
        in_specs=[
            pl.BlockSpec((width, tokens), lambda j: (0, 0)),
            pl.BlockSpec((width, tile), lambda j: (0, j)),
            pl.BlockSpec((1, tile), lambda j: (0, j)),
        ],
        out_specs=[
            pl.BlockSpec((tokens, tile), lambda j: (0, j)),
            pl.BlockSpec((tile, tokens), lambda j: (j, 0)),
        ],
        scratch_shapes=[pltpu.VMEM((tokens, width), bf16)],
    )


def decode_kernel(latents_ref, weight_ref, target_ref, out_ref, held_ref, sems):
    tile = weight_ref.shape[1]
    step = pl.program_id(0)
    last = pl.num_programs(0) - 1
    rows, tokens = target_ref.shape
    spare = -rows % 128
    width = out_ref.shape[1] - rows - spare

    def to_out(at, size, k):
        span = pl.ds(at, size)
        return pltpu.make_async_copy(held_ref.at[:, span], out_ref.at[:, span], sems.at[k])

    @pl.when(step == 0)
    def _():
        padded = jnp.concatenate([target_ref[...], jnp.zeros((spare, tokens), bf16)], axis=0)
        held_ref[:, width:] = padded.T
        to_out(width, rows + spare, width // tile).start()

    at = pl.multiple_of(step * tile, tile)
    held_ref[:, pl.ds(at, tile)] = product(latents_ref[...], weight_ref[...]).astype(bf16)
    to_out(at, tile, step).start()

    @pl.when(step == last)
    def _():
        for k in range(width // tile):
            to_out(k * tile, tile, k).wait()
        to_out(width, rows + spare, width // tile).wait()


def decode(latents, weight, turned_target, room):
    tokens, count = latents.shape
    width = weight.shape[1]
    tile = width // 7
    return call(
        decode_kernel,
        hbm_array((tokens, width + room)),
        2 * tokens * width * count,
        [latents, weight, turned_target],
        grid=(7,),
        in_specs=[WHOLE, pl.BlockSpec((count, tile), lambda j: (0, j)), WHOLE],
        out_specs=pl.BlockSpec(memory_space=pl.ANY),
        scratch_shapes=[
            pltpu.VMEM((tokens, width + room), bf16),
            pltpu.SemaphoreType.DMA((8,)),
        ],
    )


def total_of(pieces_ref, width):
    total = pieces_ref[0, :, :width].astype(f32)
    for k in range(1, pieces_ref.shape[0]):
        total += pieces_ref[k, :, :width].astype(f32)
    return total


def send_to_all(out_ref, rows):
    for k in range(out_ref.shape[0]):
        out_ref[k] = rows


def mean_of(values):
    return jnp.sum(values, axis=1, keepdims=True) / values.shape[1]


def halves_kernel(side_ref, pieces_ref, sum_ref, target_ref, sent_ref):
    rows, width = sum_ref.shape
    count = pieces_ref.shape[0]
    first = side_ref[0] == 0
    total = total_of(pieces_ref, width)
    sum_ref[...] = jnp.where(first, total[:rows], total[rows:])
    sent_ref[:, :width] = jnp.where(first, total[rows:], total[:rows]).astype(bf16)
    for k in range(count):
        piece = pieces_ref[k, :, width:].astype(f32)
        target_ref[k] = jnp.where(first, piece[:rows], piece[rows:]).astype(bf16)
        other = jnp.where(first, piece[rows:], piece[:rows]).astype(bf16)
        sent_ref[:, width + 128 * k : width + 128 * (k + 1)] = other


def recon_kernel(sum_ref, partner_ref, bias_ref, gain_ref, out_ref, recon_ref):
    partner = partner_ref[:, : recon_ref.shape[1]].astype(f32)
    recon = sum_ref[...] + partner + bias_ref[...].astype(f32)
    recon_ref[...] = recon
    scale_in = lax.rsqrt(mean_of(recon * recon) + epsilon)
    send_to_all(out_ref, (recon * scale_in * gain_ref[...].astype(f32)).astype(bf16))


def output_kernel(token_count, pieces_ref, recon_ref, target_ref, gain_ref, out_ref, grad_ref):
    gain = gain_ref[...].astype(f32)
    output = total_of(pieces_ref, recon_ref.shape[1])
    scale_out = lax.rsqrt(mean_of(output * output) + epsilon)
    normed_out = output * scale_out
    result = recon_ref[...] + normed_out * gain
    grad_result = 2.0 * (result - target_ref[...].astype(f32)) / token_count
    grad_ref[...] = grad_result
    grad_normed = grad_result * gain
    inner = mean_of(grad_normed * normed_out)
    send_to_all(out_ref, (scale_out * (grad_normed - normed_out * inner)).astype(bf16))


def input_kernel(pieces_ref, recon_ref, grad_ref, gain_ref, out_ref):
    recon = recon_ref[...]
    scale_in = lax.rsqrt(mean_of(recon * recon) + epsilon)
    unit = recon * scale_in
    grad_unit = total_of(pieces_ref, recon_ref.shape[1]) * gain_ref[...].astype(f32)
    inner = mean_of(grad_unit * unit)
    send_to_all(out_ref, (grad_ref[...] + scale_in * (grad_unit - unit * inner)).astype(bf16))


def local(body, outs, args, kept=0):
    stay = len(args) - kept
    args = [*args[:stay], *(in_hbm(a) for a in args[stay:])]
    return call(body, outs, 0, args, in_specs=[WHOLE] * stay + [pl.BlockSpec()] * kept)


def fetches(refs, weights_ref, sems, order):
    *own, near, far = refs
    units, more = own[0].shape[0], near.shape[1]
    copies = []
    for k in order:
        rows = weights_ref.at[k]
        pairs = [(own[k], rows.at[pl.ds(0, units)])]
        pairs += [(near.at[k], rows.at[pl.ds(units, more)])]
        pairs += [(far.at[k], rows.at[pl.ds(units + more, more)])]
        copies.append([pltpu.make_async_copy(*p, sems.at[k, i]) for i, p in enumerate(pairs)])
    for copy in sum(copies, []):
        copy.start()
    return copies


def arrive(copies):
    for copy in copies:
        copy.wait()


def forward_kernel(rows_ref, *refs):
    out_ref, gelu_ref, slope_ref, weights_ref, sems = refs[5:]
    root = 0.7978845608028654
    cube = 0.044715
    gate, up, down = fetches(refs[:5], weights_ref, sems, (0, 1, 2))
    rows = rows_ref[...]
    arrive(gate)
    gate_value = product_t(rows, weights_ref[0])
    arrive(up)
    up_value = product_t(rows, weights_ref[1])
    square = gate_value * gate_value
    curve = jnp.tanh(root * gate_value * (1.0 + cube * square))
    half = 0.5 * (1.0 + curve)
    gelu_value = gate_value * half
    rise = 0.5 * gate_value * (1.0 - curve * curve) * root * (1.0 + 3.0 * cube * square)
    gelu_ref[...] = gelu_value
    slope_ref[...] = up_value * (half + rise)
    hidden = (gelu_value * up_value).astype(bf16)
    arrive(down)
    for at in range(0, out_ref.shape[1], 512):
        span = slice(at, at + 512)
        out_ref[:, span] = product(hidden, weights_ref[2, :, span]).astype(bf16)


def backward_kernel(rows_ref, *refs):
    gelu_ref, slope_ref, out_ref, weights_ref, sems = refs[5:]
    down, gate, up = fetches(refs[:5], weights_ref, sems, (2, 0, 1))
    arrive(down)
    grad_hidden = product_t(rows_ref[...], weights_ref[2])
    grad_gate = (grad_hidden * slope_ref[...]).astype(bf16)
    grad_up = (grad_hidden * gelu_ref[...]).astype(bf16)
    arrive(gate)
    arrive(up)
    for at in range(0, out_ref.shape[1], 512):
        span = slice(at, at + 512)
        part = product(grad_gate, weights_ref[0, :, span])
        part += product(grad_up, weights_ref[1, :, span])
        out_ref[:, span] = part.astype(bf16)


def with_weights(body, outs, rows, weights, near, far, saved=()):
    anywhere = pl.BlockSpec(memory_space=pl.ANY)
    units, width = weights[0].shape
    units += 2 * near.shape[1]
    return call(
        body,
        outs,
        6 * rows.shape[0] * width * units,
        [rows, *(in_hbm(a) for a in (*weights, near, far, *saved))],
        in_specs=[WHOLE] + [anywhere] * 5 + [pl.BlockSpec()] * len(saved),
        scratch_shapes=[pltpu.VMEM((3, units, width), bf16), pltpu.SemaphoreType.DMA((3, 3))],
    )


def latent_kernel(rows_ref, weight_ref, latents_ref, out_ref):
    grad_latent = product_t(rows_ref[...], weight_ref[...])
    out_ref[...] = jnp.where(latents_ref[...].astype(f32) > 0, grad_latent, 0.0).astype(bf16)


def grad_of_preact(rows, weight, latents, tile):
    tokens, width = rows.shape
    count = weight.shape[0]
    return call(
        latent_kernel,
        array((tokens, count)),
        2 * tokens * width * count,
        [rows, weight, latents],
        grid=(count // tile,),
        in_specs=[
            WHOLE,
            pl.BlockSpec((tile, width), lambda j: (j, 0)),
            pl.BlockSpec((tokens, tile), lambda j: (0, j)),
        ],
        out_specs=pl.BlockSpec((tokens, tile), lambda j: (0, j)),
    )


def products_kernel(spans, count, *refs):
    out_ref = refs[-1]
    for span in spans:
        total = None
        if len(refs) > 2 * count + 1:
            rows = out_ref.shape[0]
            at = pl.multiple_of(pl.program_id(0) * rows, rows)
            total = refs[2 * count][pl.ds(at, rows), span]
        for k in range(count):
            term = product(refs[k][...], refs[count + k][:, span])
            total = term if total is None else total + term
        out_ref[:, span] = total.astype(out_ref.dtype)


def sum_of_products(left, right, tile, rows_tile=None, start=None, kind=bf16, effort=LIGHT):
    rows, depth = left[0].shape
    columns = right[0].shape[1]
    rows_tile = rows_tile or rows
    spans = [slice(at, min(at + 256, tile)) for at in range(0, tile, 256)]
    count = len(left)
    out_spec = pl.BlockSpec((rows_tile, tile), lambda i, j: (i, j))
    return call(
        functools.partial(products_kernel, spans, count),
        array((rows, columns), kind),
        2 * rows * depth * columns * count,
        [*map(in_hbm, left), *right, *([] if start is None else [start])],
        effort,
        grid=(rows // rows_tile, columns // tile),
        in_specs=[pl.BlockSpec((rows_tile, depth), lambda i, j: (i, 0))] * count
        + [pl.BlockSpec((depth, tile), lambda i, j: (0, j))] * count
        + ([] if start is None else [WHOLE]),
        out_specs=out_spec,
    )


def per_device(
    residual,
    target,
    encoder_weight,
    encoder_bias,
    decoder_weight,
    decoder_bias,
    first_gain,
    second_gain,
    gate_weight,
    up_weight,
    down_weight,
):
    tokens, share_width = residual.shape
    shards = lax.axis_size(SHARDS)
    copies = lax.axis_size(BATCH)
    width = share_width * shards
    block = width // copies
    own_tokens = tokens // shards
    token_count = tokens * copies
    offset = lax.axis_index(SHARDS) * share_width
    bias, gain_in, gain_out = (a.reshape(1, width) for a in (decoder_bias, first_gain, second_gain))
    gate, up = gate_weight.T, up_weight.T
    everyone = array((shards, own_tokens, width))
    half = lax.axis_size(HALF)
    half_of_them = hbm_array((half, own_tokens, width))
    own_rows = array((own_tokens, width), f32)

    def to_owners(partial, axes):
        return exchange(partial.reshape(lax.axis_size(axes), own_tokens, -1), axes)

    def all_tokens(pieces, axes):
        return exchange(pieces, axes).reshape(-1, width)

    units = gate.shape[0] // 2
    at = lax.axis_index(BATCH[1]) * units
    weights = [gate, up, down_weight]

    bias_share = lax.dynamic_slice_in_dim(decoder_bias.astype(f32), offset, share_width)
    centered_share = (residual.astype(f32) - bias_share).astype(bf16).T
    pieces = jnp.broadcast_to(centered_share, (shards, share_width, tokens))
    pieces, weights_then = lax.optimization_barrier((pieces, weights))
    sent = jnp.stack([lax.dynamic_slice_in_dim(w, at, units, axis=0) for w in weights_then])
    near = swap(sent, OTHER_HALF)
    centered = exchange(pieces, SHARDS).reshape(width, tokens)

    latents, turned_latents = encode(centered, encoder_weight, encoder_bias, 256)
    partial_recon = decode(latents, decoder_weight, target.T, 128)

    partial_recon, centered, turned_latents = lax.optimization_barrier(
        (partial_recon, centered, turned_latents)
    )
    far_latents = swap(turned_latents, BATCH[0])
    centered_blocks = blocks_of_all(
        lambda b: lax.dynamic_slice_in_dim(centered, b * block, block, axis=0)
    )
    pieces = exchange(partial_recon.reshape(half, 2 * own_tokens, -1), HALF)
    side = lax.axis_index(SHARDS[1]).reshape(1)
    own_sum, own_targets, sent = call(
        halves_kernel,
        [
            array((own_tokens, width), f32),
            hbm_array((half, own_tokens, 128)),
            array((own_tokens, width + half * 128)),
        ],
        0,
        [side, pieces],
        in_specs=[pl.BlockSpec(memory_space=pltpu.SMEM), WHOLE],
    )
    sent, far_latents, centered_blocks[3] = lax.optimization_barrier(
        (sent, far_latents, centered_blocks[3])
    )
    partner = swap(sent, SHARDS[1])
    pieces, recon = local(
        recon_kernel, [half_of_them, own_rows], [own_sum, partner, bias, gain_in]
    )
    partner_targets = partner[:, width:].reshape(own_tokens, half, 128)
    targets = jnp.stack([jnp.moveaxis(own_targets, 0, 1), partner_targets], axis=2)
    targets = jnp.where(side[0] == 0, targets, jnp.flip(targets, 2))[..., :share_width]
    targets = targets.reshape(own_tokens, *(lax.axis_size(a) for a in OWNERS), share_width)
    own_target = jnp.swapaxes(targets, 2, 3).reshape(own_tokens, width)

    pieces, near = lax.optimization_barrier((pieces, near))
    far = swap(near, BATCH[1])
    normed_input = all_tokens(pieces, HALF)
    rows = half * own_tokens
    hidden = gate.shape[0] + 2 * units
    partial_out, *saved = with_weights(
        forward_kernel,
        [hbm_array((rows, width))] + [hbm_array((rows, hidden), f32)] * 2,
        normed_input,
        weights,
        near,
        far,
    )
    partial_out, centered_blocks[2] = lax.optimization_barrier((partial_out, centered_blocks[2]))

    pieces, grad_result = local(
        functools.partial(output_kernel, token_count),
        [half_of_them, own_rows],
        [to_owners(partial_out, HALF), recon, own_target, gain_out],
    )
    latent_blocks = [turned_latents, swap(turned_latents, BATCH[1])]
    latent_blocks += [far_latents, swap(far_latents, BATCH[1])]
    pieces, latent_blocks, centered_blocks[1] = lax.optimization_barrier(
        (pieces, latent_blocks, centered_blocks[1])
    )
    grad_output = all_tokens(pieces, HALF)
    partial_input = with_weights(
        backward_kernel, array((rows, width)), grad_output, weights, near, far, saved
    )
    (pieces,) = local(
        input_kernel, [everyone], [to_owners(partial_input, HALF), recon, grad_result, gain_in]
    )
    grad_recon = all_tokens(pieces, OWNERS)

    own = lax.axis_index(BATCH)
    recon_blocks = [
        lax.dynamic_slice_in_dim(grad_recon, (own ^ step) * block, block, axis=1)
        for step in range(copies)
    ]
    recon_blocks[2] = swap(recon_blocks[2], BATCH[0])
    recon_blocks[3] = swap(recon_blocks[3], BATCH)
    grad_preact = grad_of_preact(grad_recon, decoder_weight, latents, 256)
    far = swap(grad_preact, BATCH[0])
    far, near, recon_blocks[1] = lax.optimization_barrier((far, grad_preact, recon_blocks[1]))
    recon_blocks[1] = swap(recon_blocks[1], BATCH[1])
    preact_blocks = [grad_preact, swap(near, BATCH[1]), far, swap(far, BATCH[1])]
    part = sum_of_products(latent_blocks[:3], recon_blocks[:3], block, kind=f32)
    encoder_grad = sum_of_products(centered_blocks, preact_blocks, 256)
    part, encoder_grad = lax.optimization_barrier((part, encoder_grad))
    decoder_grad = sum_of_products(latent_blocks[3:], recon_blocks[3:], block, 256, part)
    return encoder_grad, decoder_grad


def solution(mesh):
    batch, latent = mesh.shape["batch"], mesh.shape["latent"]
    split = Mesh(
        mesh.devices.reshape(2, batch // 2, mesh.shape["tensor"] // 2, 2, latent),
        BATCH + SHARDS,
    )
    in_specs = (
        P(BATCH, SHARDS),
        P(BATCH, SHARDS),
        P(None, SHARDS),
        P(SHARDS),
        P(SHARDS, None),
        P(),
        P(),
        P(),
        P(None, SHARDS),
        P(None, SHARDS),
        P(SHARDS, None),
    )
    out_specs = (P(BATCH, SHARDS), P(SHARDS, BATCH))
    return jax.shard_map(
        per_device, mesh=split, in_specs=in_specs, out_specs=out_specs, check_vma=False
    )
```

```python
import functools
import math

import jax
import jax.numpy as jnp
from jax import lax
from jax.experimental import pallas as pl
from jax.experimental.pallas import tpu as pltpu
from jax.sharding import Mesh
from jax.sharding import PartitionSpec as P

SHARDS = ("tensor_0", "tensor_1", "latent")
BATCH = ("batch_0", "batch_1")
HALF = ("tensor_0", "latent")
OWNERS = ("tensor_0", "latent", "tensor_1")
OTHER_HALF = ("batch_0", "tensor_1")

epsilon = 1e-06

f32 = jnp.float32
bf16 = jnp.bfloat16
LAST = (((1,), (1,)), ((), ()))
WHOLE = pl.BlockSpec(memory_space=pltpu.VMEM)
LIMIT = 24 * 1024 * 1024


def exchange(pieces, axes):
    return lax.all_to_all(pieces, axes, split_axis=0, concat_axis=0, tiled=True)


def swap(block, axes):
    for_all = lax.axis_size(axes)
    return lax.ppermute(block, axes, [(i, for_all - 1 - i) for i in range(for_all)])


def copies_of_all(block):
    near = swap(block, BATCH[1])
    far = swap(block, BATCH[0])
    return [block, near, far, swap(far, BATCH[1])]


def blocks_of_all(block_at):
    own = lax.axis_index(BATCH)
    steps = ((1, BATCH[1]), (2, BATCH[0]), (3, BATCH))
    return [block_at(own)] + [swap(block_at(own ^ step), axes) for step, axes in steps]


def call(body, outs, flops, args, **more):
    arrays = [*args, *jax.tree.leaves(outs)]
    moved = sum(math.prod(a.shape) * jnp.dtype(a.dtype).itemsize for a in arrays)
    cost = pl.CostEstimate(flops=flops, bytes_accessed=moved, transcendentals=0)
    return pl.pallas_call(
        body,
        out_shape=outs,
        cost_estimate=cost,
        compiler_params=pltpu.CompilerParams(vmem_limit_bytes=LIMIT),
        **more,
    )(*args)


def array(shape, dtype=bf16):
    return jax.ShapeDtypeStruct(shape, dtype)


def hbm_array(shape, dtype=bf16):
    return pltpu.HBM(shape, dtype)


def in_hbm(value):
    return pltpu.with_memory_space_constraint(value, pltpu.HBM)


def product(left, right):
    return jnp.dot(left, right, preferred_element_type=f32)


def product_t(left, right):
    return lax.dot_general(left, right, LAST, preferred_element_type=f32)


def encode_kernel(centered_ref, weight_ref, bias_ref, latents_ref, turned_ref, rows_ref):
    width = centered_ref.shape[0]

    def finish(total):
        latents = jnp.maximum(total + bias_ref[...].astype(f32), 0.0).astype(bf16)
        latents_ref[...] = latents
        turned_ref[...] = latents.T

    @pl.when(pl.program_id(0) == 0)
    def _():
        total = None
        for at in range(0, width, 256):
            chunk = centered_ref[at : at + 256, :].T
            rows_ref[:, at : at + 256] = chunk
            term = product(chunk, weight_ref[at : at + 256, :])
            total = term if total is None else total + term
        finish(total)

    @pl.when(pl.program_id(0) > 0)
    def _():
        finish(product(rows_ref[...], weight_ref[...]))


def encode(centered, weight, bias, tile):
    width, tokens = centered.shape
    count = weight.shape[1]
    return call(
        encode_kernel,
        [array((tokens, count)), hbm_array((count, tokens))],
        2 * tokens * width * count,
        [centered, in_hbm(weight), bias.reshape(1, count)],
        grid=(count // tile,),
        in_specs=[
            pl.BlockSpec((width, tokens), lambda j: (0, 0)),
            pl.BlockSpec((width, tile), lambda j: (0, j)),
            pl.BlockSpec((1, tile), lambda j: (0, j)),
        ],
        out_specs=[
            pl.BlockSpec((tokens, tile), lambda j: (0, j)),
            pl.BlockSpec((tile, tokens), lambda j: (j, 0)),
        ],
        scratch_shapes=[pltpu.VMEM((tokens, width), bf16)],
    )


def decode_kernel(latents_ref, weight_ref, target_ref, out_ref, held_ref, sems):
    tile = weight_ref.shape[1]
    step = pl.program_id(0)
    last = pl.num_programs(0) - 1
    rows, tokens = target_ref.shape
    spare = -rows % 128
    width = out_ref.shape[1] - rows - spare

    def to_out(at, size, k):
        span = pl.ds(at, size)
        return pltpu.make_async_copy(held_ref.at[:, span], out_ref.at[:, span], sems.at[k])

    @pl.when(step == 0)
    def _():
        padded = jnp.concatenate([target_ref[...], jnp.zeros((spare, tokens), bf16)], axis=0)
        held_ref[:, width:] = padded.T
        to_out(width, rows + spare, width // tile).start()

    at = pl.multiple_of(step * tile, tile)
    held_ref[:, pl.ds(at, tile)] = product(latents_ref[...], weight_ref[...]).astype(bf16)
    to_out(at, tile, step).start()

    @pl.when(step == last)
    def _():
        for k in range(width // tile):
            to_out(k * tile, tile, k).wait()
        to_out(width, rows + spare, width // tile).wait()


def decode(latents, weight, turned_target, room):
    tokens, count = latents.shape
    width = weight.shape[1]
    tile = width // 7
    return call(
        decode_kernel,
        hbm_array((tokens, width + room)),
        2 * tokens * width * count,
        [latents, weight, turned_target],
        grid=(7,),
        in_specs=[WHOLE, pl.BlockSpec((count, tile), lambda j: (0, j)), WHOLE],
        out_specs=pl.BlockSpec(memory_space=pl.ANY),
        scratch_shapes=[
            pltpu.VMEM((tokens, width + room), bf16),
            pltpu.SemaphoreType.DMA((8,)),
        ],
    )


def total_of(pieces_ref, width):
    total = pieces_ref[0, :, :width].astype(f32)
    for k in range(1, pieces_ref.shape[0]):
        total += pieces_ref[k, :, :width].astype(f32)
    return total


def send_to_all(out_ref, rows):
    for k in range(out_ref.shape[0]):
        out_ref[k] = rows


def mean_of(values):
    return jnp.sum(values, axis=1, keepdims=True) / values.shape[1]


def halves_kernel(side_ref, pieces_ref, sum_ref, target_ref, sent_ref):
    rows, width = sum_ref.shape
    count = pieces_ref.shape[0]
    first = side_ref[0] == 0
    total = total_of(pieces_ref, width)
    sum_ref[...] = jnp.where(first, total[:rows], total[rows:])
    sent_ref[:, :width] = jnp.where(first, total[rows:], total[:rows]).astype(bf16)
    for k in range(count):
        piece = pieces_ref[k, :, width:].astype(f32)
        target_ref[k] = jnp.where(first, piece[:rows], piece[rows:]).astype(bf16)
        other = jnp.where(first, piece[rows:], piece[:rows]).astype(bf16)
        sent_ref[:, width + 128 * k : width + 128 * (k + 1)] = other


def recon_kernel(sum_ref, partner_ref, bias_ref, gain_ref, out_ref, recon_ref):
    partner = partner_ref[:, : recon_ref.shape[1]].astype(f32)
    recon = sum_ref[...] + partner + bias_ref[...].astype(f32)
    recon_ref[...] = recon
    scale_in = lax.rsqrt(mean_of(recon * recon) + epsilon)
    send_to_all(out_ref, (recon * scale_in * gain_ref[...].astype(f32)).astype(bf16))


def output_kernel(token_count, pieces_ref, recon_ref, target_ref, gain_ref, out_ref, grad_ref):
    gain = gain_ref[...].astype(f32)
    output = total_of(pieces_ref, recon_ref.shape[1])
    scale_out = lax.rsqrt(mean_of(output * output) + epsilon)
    normed_out = output * scale_out
    result = recon_ref[...] + normed_out * gain
    grad_result = 2.0 * (result - target_ref[...].astype(f32)) / token_count
    grad_ref[...] = grad_result
    grad_normed = grad_result * gain
    inner = mean_of(grad_normed * normed_out)
    send_to_all(out_ref, (scale_out * (grad_normed - normed_out * inner)).astype(bf16))


def input_kernel(pieces_ref, recon_ref, grad_ref, gain_ref, out_ref):
    recon = recon_ref[...]
    scale_in = lax.rsqrt(mean_of(recon * recon) + epsilon)
    unit = recon * scale_in
    grad_unit = total_of(pieces_ref, recon_ref.shape[1]) * gain_ref[...].astype(f32)
    inner = mean_of(grad_unit * unit)
    send_to_all(out_ref, (grad_ref[...] + scale_in * (grad_unit - unit * inner)).astype(bf16))


def local(body, outs, args, kept=0):
    stay = len(args) - kept
    args = [*args[:stay], *(in_hbm(a) for a in args[stay:])]
    return call(body, outs, 0, args, in_specs=[WHOLE] * stay + [pl.BlockSpec()] * kept)


def fetches(refs, weights_ref, sems, order):
    *own, near, far = refs
    units, more = own[0].shape[0], near.shape[1]
    copies = []
    for k in order:
        rows = weights_ref.at[k]
        pairs = [(own[k], rows.at[pl.ds(0, units)])]
        pairs += [(near.at[k], rows.at[pl.ds(units, more)])]
        pairs += [(far.at[k], rows.at[pl.ds(units + more, more)])]
        copies.append([pltpu.make_async_copy(*p, sems.at[k, i]) for i, p in enumerate(pairs)])
    for copy in sum(copies, []):
        copy.start()
    return copies


def arrive(copies):
    for copy in copies:
        copy.wait()


def forward_kernel(rows_ref, *refs):
    out_ref, gelu_ref, slope_ref, weights_ref, sems = refs[5:]
    root = 0.7978845608028654
    cube = 0.044715
    gate, up, down = fetches(refs[:5], weights_ref, sems, (0, 1, 2))
    rows = rows_ref[...]
    arrive(gate)
    gate_value = product_t(rows, weights_ref[0])
    arrive(up)
    up_value = product_t(rows, weights_ref[1])
    square = gate_value * gate_value
    curve = jnp.tanh(root * gate_value * (1.0 + cube * square))
    half = 0.5 * (1.0 + curve)
    gelu_value = gate_value * half
    rise = 0.5 * gate_value * (1.0 - curve * curve) * root * (1.0 + 3.0 * cube * square)
    gelu_ref[...] = gelu_value
    slope_ref[...] = up_value * (half + rise)
    hidden = (gelu_value * up_value).astype(bf16)
    arrive(down)
    for at in range(0, out_ref.shape[1], 512):
        span = slice(at, at + 512)
        out_ref[:, span] = product(hidden, weights_ref[2, :, span]).astype(bf16)


def backward_kernel(rows_ref, *refs):
    gelu_ref, slope_ref, out_ref, weights_ref, sems = refs[5:]
    down, gate, up = fetches(refs[:5], weights_ref, sems, (2, 0, 1))
    arrive(down)
    grad_hidden = product_t(rows_ref[...], weights_ref[2])
    grad_gate = (grad_hidden * slope_ref[...]).astype(bf16)
    grad_up = (grad_hidden * gelu_ref[...]).astype(bf16)
    grads = jnp.concatenate([grad_gate, grad_up], axis=1)
    arrive(gate)
    arrive(up)
    for at in range(0, out_ref.shape[1], 512):
        span = slice(at, at + 512)
        part = jnp.concatenate([weights_ref[0, :, span], weights_ref[1, :, span]], axis=0)
        out_ref[:, span] = product(grads, part).astype(bf16)


def with_weights(body, outs, rows, weights, near, far, saved=()):
    anywhere = pl.BlockSpec(memory_space=pl.ANY)
    units, width = weights[0].shape
    units += 2 * near.shape[1]
    return call(
        body,
        outs,
        6 * rows.shape[0] * width * units,
        [rows, *(in_hbm(a) for a in (*weights, near, far, *saved))],
        in_specs=[WHOLE] + [anywhere] * 5 + [pl.BlockSpec()] * len(saved),
        scratch_shapes=[pltpu.VMEM((3, units, width), bf16), pltpu.SemaphoreType.DMA((3, 3))],
    )


def latent_kernel(rows_ref, weight_ref, latents_ref, out_ref):
    grad_latent = product_t(rows_ref[...], weight_ref[...])
    out_ref[...] = jnp.where(latents_ref[...].astype(f32) > 0, grad_latent, 0.0).astype(bf16)


def grad_of_preact(rows, weight, latents, tile):
    tokens, width = rows.shape
    count = weight.shape[0]
    return call(
        latent_kernel,
        array((tokens, count)),
        2 * tokens * width * count,
        [rows, weight, latents],
        grid=(count // tile,),
        in_specs=[
            WHOLE,
            pl.BlockSpec((tile, width), lambda j: (j, 0)),
            pl.BlockSpec((tokens, tile), lambda j: (0, j)),
        ],
        out_specs=pl.BlockSpec((tokens, tile), lambda j: (0, j)),
    )


def products_kernel(spans, count, *refs):
    out_ref = refs[-1]
    left = jnp.concatenate([ref[...] for ref in refs[:count]], axis=1)
    for span in spans:
        right = jnp.concatenate([ref[:, span] for ref in refs[count : 2 * count]], axis=0)
        total = product(left, right)
        if len(refs) > 2 * count + 1:
            rows = out_ref.shape[0]
            at = pl.multiple_of(pl.program_id(0) * rows, rows)
            total += refs[2 * count][pl.ds(at, rows), span]
        out_ref[:, span] = total.astype(out_ref.dtype)


def sum_of_products(left, right, tile, rows_tile=None, start=None, kind=bf16):
    rows, depth = left[0].shape
    columns = right[0].shape[1]
    rows_tile = rows_tile or rows
    spans = [slice(at, min(at + 256, tile)) for at in range(0, tile, 256)]
    count = len(left)
    out_spec = pl.BlockSpec((rows_tile, tile), lambda i, j: (i, j))
    return call(
        functools.partial(products_kernel, spans, count),
        array((rows, columns), kind),
        2 * rows * depth * columns * count,
        [*map(in_hbm, left), *right, *([] if start is None else [start])],
        grid=(rows // rows_tile, columns // tile),
        in_specs=[pl.BlockSpec((rows_tile, depth), lambda i, j: (i, 0))] * count
        + [pl.BlockSpec((depth, tile), lambda i, j: (0, j))] * count
        + ([] if start is None else [WHOLE]),
        out_specs=out_spec,
    )


def per_device(
    residual,
    target,
    encoder_weight,
    encoder_bias,
    decoder_weight,
    decoder_bias,
    first_gain,
    second_gain,
    gate_weight,
    up_weight,
    down_weight,
):
    tokens, share_width = residual.shape
    shards = lax.axis_size(SHARDS)
    copies = lax.axis_size(BATCH)
    width = share_width * shards
    block = width // copies
    own_tokens = tokens // shards
    token_count = tokens * copies
    offset = lax.axis_index(SHARDS) * share_width
    bias, gain_in, gain_out = (a.reshape(1, width) for a in (decoder_bias, first_gain, second_gain))
    gate, up = gate_weight.T, up_weight.T
    everyone = array((shards, own_tokens, width))
    half = lax.axis_size(HALF)
    half_of_them = hbm_array((half, own_tokens, width))
    own_rows = array((own_tokens, width), f32)

    def to_owners(partial, axes):
        return exchange(partial.reshape(lax.axis_size(axes), own_tokens, -1), axes)

    def all_tokens(pieces, axes):
        return exchange(pieces, axes).reshape(-1, width)

    units = gate.shape[0] // 2
    at = lax.axis_index(BATCH[1]) * units
    weights = [gate, up, down_weight]

    bias_share = lax.dynamic_slice_in_dim(decoder_bias.astype(f32), offset, share_width)
    centered_share = (residual.astype(f32) - bias_share).astype(bf16).T
    pieces = jnp.broadcast_to(centered_share, (shards, share_width, tokens))
    pieces, weights_then = lax.optimization_barrier((pieces, weights))
    sent = jnp.stack([lax.dynamic_slice_in_dim(w, at, units, axis=0) for w in weights_then])
    near = swap(sent, OTHER_HALF)
    centered = exchange(pieces, SHARDS).reshape(width, tokens)

    latents, turned_latents = encode(centered, encoder_weight, encoder_bias, 256)
    partial_recon = decode(latents, decoder_weight, target.T, 128)

    partial_recon, centered, turned_latents = lax.optimization_barrier(
        (partial_recon, centered, turned_latents)
    )
    far_latents = swap(turned_latents, BATCH[0])
    centered_blocks = blocks_of_all(
        lambda b: lax.dynamic_slice_in_dim(centered, b * block, block, axis=0)
    )
    pieces = exchange(partial_recon.reshape(half, 2 * own_tokens, -1), HALF)
    side = lax.axis_index(SHARDS[1]).reshape(1)
    own_sum, own_targets, sent = call(
        halves_kernel,
        [
            array((own_tokens, width), f32),
            hbm_array((half, own_tokens, 128)),
            array((own_tokens, width + half * 128)),
        ],
        0,
        [side, pieces],
        in_specs=[pl.BlockSpec(memory_space=pltpu.SMEM), WHOLE],
    )
    sent, far_latents, centered_blocks[3] = lax.optimization_barrier(
        (sent, far_latents, centered_blocks[3])
    )
    partner = swap(sent, SHARDS[1])
    pieces, recon = local(
        recon_kernel, [half_of_them, own_rows], [own_sum, partner, bias, gain_in]
    )
    partner_targets = partner[:, width:].reshape(own_tokens, half, 128)
    targets = jnp.stack([jnp.moveaxis(own_targets, 0, 1), partner_targets], axis=2)
    targets = jnp.where(side[0] == 0, targets, jnp.flip(targets, 2))[..., :share_width]
    targets = targets.reshape(own_tokens, *(lax.axis_size(a) for a in OWNERS), share_width)
    own_target = jnp.swapaxes(targets, 2, 3).reshape(own_tokens, width)

    pieces, near = lax.optimization_barrier((pieces, near))
    far = swap(near, BATCH[1])
    normed_input = all_tokens(pieces, HALF)
    rows = half * own_tokens
    hidden = gate.shape[0] + 2 * units
    partial_out, *saved = with_weights(
        forward_kernel,
        [hbm_array((rows, width))] + [hbm_array((rows, hidden), f32)] * 2,
        normed_input,
        weights,
        near,
        far,
    )
    partial_out, centered_blocks[2] = lax.optimization_barrier((partial_out, centered_blocks[2]))

    pieces, grad_result = local(
        functools.partial(output_kernel, token_count),
        [half_of_them, own_rows],
        [to_owners(partial_out, HALF), recon, own_target, gain_out],
    )
    latent_blocks = [turned_latents, swap(turned_latents, BATCH[1])]
    latent_blocks += [far_latents, swap(far_latents, BATCH[1])]
    pieces, latent_blocks, centered_blocks[1] = lax.optimization_barrier(
        (pieces, latent_blocks, centered_blocks[1])
    )
    grad_output = all_tokens(pieces, HALF)
    partial_input = with_weights(
        backward_kernel, array((rows, width)), grad_output, weights, near, far, saved
    )
    (pieces,) = local(
        input_kernel, [everyone], [to_owners(partial_input, HALF), recon, grad_result, gain_in]
    )
    grad_recon = all_tokens(pieces, OWNERS)

    own = lax.axis_index(BATCH)
    recon_blocks = [
        lax.dynamic_slice_in_dim(grad_recon, (own ^ step) * block, block, axis=1)
        for step in range(copies)
    ]
    recon_blocks[2] = swap(recon_blocks[2], BATCH[0])
    recon_blocks[3] = swap(recon_blocks[3], BATCH)
    grad_preact = grad_of_preact(grad_recon, decoder_weight, latents, 256)
    far = swap(grad_preact, BATCH[0])
    far, near, recon_blocks[1] = lax.optimization_barrier((far, grad_preact, recon_blocks[1]))
    recon_blocks[1] = swap(recon_blocks[1], BATCH[1])
    preact_blocks = [grad_preact, swap(near, BATCH[1]), far, swap(far, BATCH[1])]
    part = sum_of_products(latent_blocks[:3], recon_blocks[:3], block, kind=f32)
    encoder_grad = sum_of_products(centered_blocks, preact_blocks, 256)
    part, encoder_grad = lax.optimization_barrier((part, encoder_grad))
    decoder_grad = sum_of_products(latent_blocks[3:], recon_blocks[3:], block, 256, part)
    return encoder_grad, decoder_grad


def solution(mesh):
    batch, latent = mesh.shape["batch"], mesh.shape["latent"]
    split = Mesh(
        mesh.devices.reshape(2, batch // 2, mesh.shape["tensor"] // 2, 2, latent),
        BATCH + SHARDS,
    )
    in_specs = (
        P(BATCH, SHARDS),
        P(BATCH, SHARDS),
        P(None, SHARDS),
        P(SHARDS),
        P(SHARDS, None),
        P(),
        P(),
        P(),
        P(None, SHARDS),
        P(None, SHARDS),
        P(SHARDS, None),
    )
    out_specs = (P(BATCH, SHARDS), P(SHARDS, BATCH))
    return jax.shard_map(
        per_device, mesh=split, in_specs=in_specs, out_specs=out_specs, check_vma=False
    )
```

```python
import functools
import math

import jax
import jax.numpy as jnp
from jax import lax
from jax.experimental import pallas as pl
from jax.experimental.pallas import tpu as pltpu
from jax.sharding import Mesh
from jax.sharding import PartitionSpec as P

SHARDS = ("tensor_0", "tensor_1", "latent")
BATCH = ("batch_0", "batch_1")
HALF = ("tensor_0", "latent")
OWNERS = ("tensor_0", "latent", "tensor_1")
OTHER_HALF = ("batch_0", "tensor_1")

epsilon = 1e-06

f32 = jnp.float32
bf16 = jnp.bfloat16
LAST = (((1,), (1,)), ((), ()))
WHOLE = pl.BlockSpec(memory_space=pltpu.VMEM)
LIMIT = 24 * 1024 * 1024


def exchange(pieces, axes):
    return lax.all_to_all(pieces, axes, split_axis=0, concat_axis=0, tiled=True)


def swap(block, axes):
    for_all = lax.axis_size(axes)
    return lax.ppermute(block, axes, [(i, for_all - 1 - i) for i in range(for_all)])


def copies_of_all(block):
    near = swap(block, BATCH[1])
    far = swap(block, BATCH[0])
    return [block, near, far, swap(far, BATCH[1])]


def blocks_of_all(block_at):
    own = lax.axis_index(BATCH)
    steps = ((1, BATCH[1]), (2, BATCH[0]), (3, BATCH))
    return [block_at(own)] + [swap(block_at(own ^ step), axes) for step, axes in steps]


def call(body, outs, flops, args, **more):
    arrays = [*args, *jax.tree.leaves(outs)]
    moved = sum(math.prod(a.shape) * jnp.dtype(a.dtype).itemsize for a in arrays)
    cost = pl.CostEstimate(flops=flops, bytes_accessed=moved, transcendentals=0)
    return pl.pallas_call(
        body,
        out_shape=outs,
        cost_estimate=cost,
        compiler_params=pltpu.CompilerParams(vmem_limit_bytes=LIMIT),
        **more,
    )(*args)


def array(shape, dtype=bf16):
    return jax.ShapeDtypeStruct(shape, dtype)


def hbm_array(shape, dtype=bf16):
    return pltpu.HBM(shape, dtype)


def in_hbm(value):
    return pltpu.with_memory_space_constraint(value, pltpu.HBM)


def product(left, right):
    return jnp.dot(left, right, preferred_element_type=f32)


def product_t(left, right):
    return lax.dot_general(left, right, LAST, preferred_element_type=f32)


def encode_kernel(centered_ref, weight_ref, bias_ref, latents_ref, turned_ref, rows_ref):
    width = centered_ref.shape[0]

    def finish(total):
        latents = jnp.maximum(total + bias_ref[...].astype(f32), 0.0).astype(bf16)
        latents_ref[...] = latents
        turned_ref[...] = latents.T

    @pl.when(pl.program_id(0) == 0)
    def _():
        total = None
        for at in range(0, width, 256):
            chunk = centered_ref[at : at + 256, :].T
            rows_ref[:, at : at + 256] = chunk
            term = product(chunk, weight_ref[at : at + 256, :])
            total = term if total is None else total + term
        finish(total)

    @pl.when(pl.program_id(0) > 0)
    def _():
        finish(product(rows_ref[...], weight_ref[...]))


def encode(centered, weight, bias, tile):
    width, tokens = centered.shape
    count = weight.shape[1]
    return call(
        encode_kernel,
        [array((tokens, count)), hbm_array((count, tokens))],
        2 * tokens * width * count,
        [centered, in_hbm(weight), bias.reshape(1, count)],
        grid=(count // tile,),
        in_specs=[
            pl.BlockSpec((width, tokens), lambda j: (0, 0)),
            pl.BlockSpec((width, tile), lambda j: (0, j)),
            pl.BlockSpec((1, tile), lambda j: (0, j)),
        ],
        out_specs=[
            pl.BlockSpec((tokens, tile), lambda j: (0, j)),
            pl.BlockSpec((tile, tokens), lambda j: (j, 0)),
        ],
        scratch_shapes=[pltpu.VMEM((tokens, width), bf16)],
    )


def decode_kernel(latents_ref, weight_ref, target_ref, out_ref, held_ref, sems):
    tile = weight_ref.shape[1]
    step = pl.program_id(0)
    last = pl.num_programs(0) - 1
    rows, tokens = target_ref.shape
    spare = -rows % 128
    width = out_ref.shape[1] - rows - spare

    def to_out(at, size, k):
        span = pl.ds(at, size)
        return pltpu.make_async_copy(held_ref.at[:, span], out_ref.at[:, span], sems.at[k])

    @pl.when(step == 0)
    def _():
        padded = jnp.concatenate([target_ref[...], jnp.zeros((spare, tokens), bf16)], axis=0)
        held_ref[:, width:] = padded.T
        to_out(width, rows + spare, width // tile).start()

    at = pl.multiple_of(step * tile, tile)
    held_ref[:, pl.ds(at, tile)] = product(latents_ref[...], weight_ref[...]).astype(bf16)
    to_out(at, tile, step).start()

    @pl.when(step == last)
    def _():
        for k in range(width // tile):
            to_out(k * tile, tile, k).wait()
        to_out(width, rows + spare, width // tile).wait()


def decode(latents, weight, turned_target, room):
    tokens, count = latents.shape
    width = weight.shape[1]
    tile = width // 4
    return call(
        decode_kernel,
        hbm_array((tokens, width + room)),
        2 * tokens * width * count,
        [latents, weight, turned_target],
        grid=(width // tile,),
        in_specs=[WHOLE, pl.BlockSpec((count, tile), lambda j: (0, j)), WHOLE],
        out_specs=pl.BlockSpec(memory_space=pl.ANY),
        scratch_shapes=[
            pltpu.VMEM((tokens, width + room), bf16),
            pltpu.SemaphoreType.DMA((width // tile + 1,)),
        ],
    )


def total_of(pieces_ref, width):
    total = pieces_ref[0, :, :width].astype(f32)
    for k in range(1, pieces_ref.shape[0]):
        total += pieces_ref[k, :, :width].astype(f32)
    return total


def send_to_all(out_ref, rows):
    for k in range(out_ref.shape[0]):
        out_ref[k] = rows


def mean_of(values):
    return jnp.sum(values, axis=1, keepdims=True) / values.shape[1]


def halves_kernel(side_ref, pieces_ref, sum_ref, target_ref, sent_ref):
    rows, width = sum_ref.shape
    count = pieces_ref.shape[0]
    first = side_ref[0] == 0
    total = total_of(pieces_ref, width)
    sum_ref[...] = jnp.where(first, total[:rows], total[rows:])
    sent_ref[:, :width] = jnp.where(first, total[rows:], total[:rows]).astype(bf16)
    for k in range(count):
        piece = pieces_ref[k, :, width:].astype(f32)
        target_ref[k] = jnp.where(first, piece[:rows], piece[rows:]).astype(bf16)
        other = jnp.where(first, piece[rows:], piece[:rows]).astype(bf16)
        sent_ref[:, width + 128 * k : width + 128 * (k + 1)] = other


def recon_kernel(sum_ref, partner_ref, bias_ref, gain_ref, out_ref, recon_ref):
    partner = partner_ref[:, : recon_ref.shape[1]].astype(f32)
    recon = sum_ref[...] + partner + bias_ref[...].astype(f32)
    recon_ref[...] = recon
    scale_in = lax.rsqrt(mean_of(recon * recon) + epsilon)
    send_to_all(out_ref, (recon * scale_in * gain_ref[...].astype(f32)).astype(bf16))


def output_kernel(token_count, pieces_ref, recon_ref, target_ref, gain_ref, out_ref, grad_ref):
    gain = gain_ref[...].astype(f32)
    output = total_of(pieces_ref, recon_ref.shape[1])
    scale_out = lax.rsqrt(mean_of(output * output) + epsilon)
    normed_out = output * scale_out
    result = recon_ref[...] + normed_out * gain
    grad_result = 2.0 * (result - target_ref[...].astype(f32)) / token_count
    grad_ref[...] = grad_result
    grad_normed = grad_result * gain
    inner = mean_of(grad_normed * normed_out)
    send_to_all(out_ref, (scale_out * (grad_normed - normed_out * inner)).astype(bf16))


def input_kernel(pieces_ref, recon_ref, grad_ref, gain_ref, out_ref):
    recon = recon_ref[...]
    scale_in = lax.rsqrt(mean_of(recon * recon) + epsilon)
    unit = recon * scale_in
    grad_unit = total_of(pieces_ref, recon_ref.shape[1]) * gain_ref[...].astype(f32)
    inner = mean_of(grad_unit * unit)
    send_to_all(out_ref, (grad_ref[...] + scale_in * (grad_unit - unit * inner)).astype(bf16))


def local(body, outs, args, kept=0):
    stay = len(args) - kept
    args = [*args[:stay], *(in_hbm(a) for a in args[stay:])]
    return call(body, outs, 0, args, in_specs=[WHOLE] * stay + [pl.BlockSpec()] * kept)


def fetches(refs, weights_ref, sems, order):
    *own, near, far = refs
    units, more = own[0].shape[0], near.shape[1]
    copies = []
    for k in order:
        rows = weights_ref.at[k]
        pairs = [(own[k], rows.at[pl.ds(0, units)])]
        pairs += [(near.at[k], rows.at[pl.ds(units, more)])]
        pairs += [(far.at[k], rows.at[pl.ds(units + more, more)])]
        copies.append([pltpu.make_async_copy(*p, sems.at[k, i]) for i, p in enumerate(pairs)])
    for copy in sum(copies, []):
        copy.start()
    return copies


def arrive(copies):
    for copy in copies:
        copy.wait()


def forward_kernel(rows_ref, *refs):
    out_ref, gelu_ref, slope_ref, weights_ref, sems = refs[5:]
    root = 0.7978845608028654
    cube = 0.044715
    gate, up, down = fetches(refs[:5], weights_ref, sems, (0, 1, 2))
    rows = rows_ref[...]
    arrive(gate)
    gate_value = product_t(rows, weights_ref[0])
    arrive(up)
    up_value = product_t(rows, weights_ref[1])
    square = gate_value * gate_value
    curve = jnp.tanh(root * gate_value * (1.0 + cube * square))
    half = 0.5 * (1.0 + curve)
    gelu_value = gate_value * half
    rise = 0.5 * gate_value * (1.0 - curve * curve) * root * (1.0 + 3.0 * cube * square)
    gelu_ref[...] = gelu_value
    slope_ref[...] = up_value * (half + rise)
    hidden = (gelu_value * up_value).astype(bf16)
    arrive(down)
    for at in range(0, out_ref.shape[1], 512):
        span = slice(at, at + 512)
        out_ref[:, span] = product(hidden, weights_ref[2, :, span]).astype(bf16)


def backward_kernel(rows_ref, *refs):
    gelu_ref, slope_ref, out_ref, weights_ref, sems = refs[5:]
    down, gate, up = fetches(refs[:5], weights_ref, sems, (2, 0, 1))
    arrive(down)
    grad_hidden = product_t(rows_ref[...], weights_ref[2])
    grad_gate = (grad_hidden * slope_ref[...]).astype(bf16)
    grad_up = (grad_hidden * gelu_ref[...]).astype(bf16)
    grads = jnp.concatenate([grad_gate, grad_up], axis=1)
    arrive(gate)
    arrive(up)
    for at in range(0, out_ref.shape[1], 512):
        span = slice(at, at + 512)
        part = jnp.concatenate([weights_ref[0, :, span], weights_ref[1, :, span]], axis=0)
        out_ref[:, span] = product(grads, part).astype(bf16)


def with_weights(body, outs, rows, weights, near, far, saved=()):
    anywhere = pl.BlockSpec(memory_space=pl.ANY)
    units, width = weights[0].shape
    units += 2 * near.shape[1]
    return call(
        body,
        outs,
        6 * rows.shape[0] * width * units,
        [rows, *map(in_hbm, weights), in_hbm(near), far, *map(in_hbm, saved)],
        in_specs=[WHOLE] + [anywhere] * 5 + [pl.BlockSpec()] * len(saved),
        scratch_shapes=[pltpu.VMEM((3, units, width), bf16), pltpu.SemaphoreType.DMA((3, 3))],
    )


def latent_kernel(rows_ref, weight_ref, latents_ref, out_ref):
    grad_latent = product_t(rows_ref[...], weight_ref[...])
    out_ref[...] = jnp.where(latents_ref[...].astype(f32) > 0, grad_latent, 0.0).astype(bf16)


def grad_of_preact(rows, weight, latents, tile):
    tokens, width = rows.shape
    count = weight.shape[0]
    return call(
        latent_kernel,
        array((tokens, count)),
        2 * tokens * width * count,
        [rows, weight, latents],
        grid=(count // tile,),
        in_specs=[
            WHOLE,
            pl.BlockSpec((tile, width), lambda j: (j, 0)),
            pl.BlockSpec((tokens, tile), lambda j: (0, j)),
        ],
        out_specs=pl.BlockSpec((tokens, tile), lambda j: (0, j)),
    )


def products_kernel(tile, count, *refs):
    out_ref = refs[-1]
    left = jnp.concatenate([ref[...] for ref in refs[:count]], axis=1)
    first = pl.program_id(1) * tile
    for at in range(0, tile, 256):
        size = min(256, tile - at)
        columns = pl.ds(pl.multiple_of(first + at, 128), size)
        span = slice(at, at + size)
        right = jnp.concatenate([ref[:, columns] for ref in refs[count : 2 * count]], axis=0)
        total = product(left, right)
        if len(refs) > 2 * count + 1:
            rows = out_ref.shape[0]
            start = pl.multiple_of(pl.program_id(0) * rows, rows)
            total += refs[2 * count][pl.ds(start, rows), span]
        out_ref[:, span] = total.astype(out_ref.dtype)


def sum_of_products(left, right, tile, rows_tile=None, start=None, kind=bf16):
    rows, depth = left[0].shape
    columns = right[0].shape[1]
    rows_tile = rows_tile or rows
    count = len(left)
    out_spec = pl.BlockSpec((rows_tile, tile), lambda i, j: (i, j))
    return call(
        functools.partial(products_kernel, tile, count),
        array((rows, columns), kind),
        2 * rows * depth * columns * count,
        [*map(in_hbm, left), *right, *([] if start is None else [start])],
        grid=(rows // rows_tile, columns // tile),
        in_specs=[pl.BlockSpec((rows_tile, depth), lambda i, j: (i, 0))] * count
        + [WHOLE] * count
        + ([] if start is None else [WHOLE]),
        out_specs=out_spec,
    )


def per_device(
    residual,
    target,
    encoder_weight,
    encoder_bias,
    decoder_weight,
    decoder_bias,
    first_gain,
    second_gain,
    gate_weight,
    up_weight,
    down_weight,
):
    tokens, share_width = residual.shape
    shards = lax.axis_size(SHARDS)
    copies = lax.axis_size(BATCH)
    width = share_width * shards
    block = width // copies
    own_tokens = tokens // shards
    token_count = tokens * copies
    offset = lax.axis_index(SHARDS) * share_width
    bias, gain_in, gain_out = (a.reshape(1, width) for a in (decoder_bias, first_gain, second_gain))
    gate, up = gate_weight.T, up_weight.T
    everyone = array((shards, own_tokens, width))
    half = lax.axis_size(HALF)
    half_of_them = hbm_array((half, own_tokens, width))
    own_rows = array((own_tokens, width), f32)

    def to_owners(partial, axes):
        return exchange(partial.reshape(lax.axis_size(axes), own_tokens, -1), axes)

    def all_tokens(pieces, axes):
        return exchange(pieces, axes).reshape(-1, width)

    units = gate.shape[0] // 2
    at = lax.axis_index(BATCH[1]) * units
    weights = [gate, up, down_weight]

    bias_share = lax.dynamic_slice_in_dim(decoder_bias.astype(f32), offset, share_width)
    centered_share = (residual.astype(f32) - bias_share).astype(bf16).T
    pieces = jnp.broadcast_to(centered_share, (shards, share_width, tokens))
    pieces, weights_then = lax.optimization_barrier((pieces, weights))
    sent = jnp.stack([lax.dynamic_slice_in_dim(w, at, units, axis=0) for w in weights_then])
    near = swap(sent, OTHER_HALF)
    centered = exchange(pieces, SHARDS).reshape(width, tokens)

    latents, turned_latents = encode(centered, encoder_weight, encoder_bias, 512)
    partial_recon = decode(latents, decoder_weight, target.T, 128)

    partial_recon, centered, turned_latents = lax.optimization_barrier(
        (partial_recon, centered, turned_latents)
    )
    far_latents = swap(turned_latents, BATCH[0])
    centered_blocks = blocks_of_all(
        lambda b: lax.dynamic_slice_in_dim(centered, b * block, block, axis=0)
    )
    pieces = exchange(partial_recon.reshape(half, 2 * own_tokens, -1), HALF)
    side = lax.axis_index(SHARDS[1]).reshape(1)
    own_sum, own_targets, sent = call(
        halves_kernel,
        [
            array((own_tokens, width), f32),
            hbm_array((half, own_tokens, 128)),
            array((own_tokens, width + half * 128)),
        ],
        0,
        [side, pieces],
        in_specs=[pl.BlockSpec(memory_space=pltpu.SMEM), WHOLE],
    )
    sent, far_latents, centered_blocks[3] = lax.optimization_barrier(
        (sent, far_latents, centered_blocks[3])
    )
    partner = swap(sent, SHARDS[1])
    pieces, recon = local(
        recon_kernel, [half_of_them, own_rows], [own_sum, partner, bias, gain_in]
    )
    partner_targets = partner[:, width:].reshape(own_tokens, half, 128)
    targets = jnp.stack([jnp.moveaxis(own_targets, 0, 1), partner_targets], axis=2)
    targets = jnp.where(side[0] == 0, targets, jnp.flip(targets, 2))[..., :share_width]
    targets = targets.reshape(own_tokens, *(lax.axis_size(a) for a in OWNERS), share_width)
    own_target = jnp.swapaxes(targets, 2, 3).reshape(own_tokens, width)

    pieces, near = lax.optimization_barrier((pieces, near))
    far = swap(near, BATCH[1])
    normed_input = all_tokens(pieces, HALF)
    rows = half * own_tokens
    hidden = gate.shape[0] + 2 * units
    partial_out, *saved = with_weights(
        forward_kernel,
        [hbm_array((rows, width))] + [hbm_array((rows, hidden), f32)] * 2,
        normed_input,
        weights,
        near,
        far,
    )
    partial_out, centered_blocks[2] = lax.optimization_barrier((partial_out, centered_blocks[2]))

    pieces, grad_result = local(
        functools.partial(output_kernel, token_count),
        [half_of_them, own_rows],
        [to_owners(partial_out, HALF), recon, own_target, gain_out],
    )
    latent_blocks = [turned_latents, swap(turned_latents, BATCH[1])]
    latent_blocks += [far_latents, swap(far_latents, BATCH[1])]
    pieces, latent_blocks, centered_blocks[1] = lax.optimization_barrier(
        (pieces, latent_blocks, centered_blocks[1])
    )
    grad_output = all_tokens(pieces, HALF)
    partial_input = with_weights(
        backward_kernel, array((rows, width)), grad_output, weights, near, in_hbm(far), saved
    )
    (pieces,) = local(
        input_kernel, [everyone], [to_owners(partial_input, HALF), recon, grad_result, gain_in]
    )
    grad_recon = all_tokens(pieces, OWNERS)

    own = lax.axis_index(BATCH)
    recon_blocks = [
        lax.dynamic_slice_in_dim(grad_recon, (own ^ step) * block, block, axis=1)
        for step in range(copies)
    ]
    recon_blocks[2] = swap(recon_blocks[2], BATCH[0])
    recon_blocks[3] = swap(recon_blocks[3], BATCH)
    grad_preact = grad_of_preact(grad_recon, decoder_weight, latents, 512)
    far = swap(grad_preact, BATCH[0])
    far, near, recon_blocks[1] = lax.optimization_barrier((far, grad_preact, recon_blocks[1]))
    recon_blocks[1] = swap(recon_blocks[1], BATCH[1])
    preact_blocks = [grad_preact, swap(near, BATCH[1]), far, swap(far, BATCH[1])]
    part = sum_of_products(latent_blocks[:3], recon_blocks[:3], block, kind=f32)
    encoder_grad = sum_of_products(centered_blocks, preact_blocks, 512)
    part, encoder_grad = lax.optimization_barrier((part, encoder_grad))
    decoder_grad = sum_of_products(latent_blocks[3:], recon_blocks[3:], block, 512, part)
    return encoder_grad, decoder_grad


def solution(mesh):
    batch, latent = mesh.shape["batch"], mesh.shape["latent"]
    split = Mesh(
        mesh.devices.reshape(2, batch // 2, mesh.shape["tensor"] // 2, 2, latent),
        BATCH + SHARDS,
    )
    in_specs = (
        P(BATCH, SHARDS),
        P(BATCH, SHARDS),
        P(None, SHARDS),
        P(SHARDS),
        P(SHARDS, None),
        P(),
        P(),
        P(),
        P(None, SHARDS),
        P(None, SHARDS),
        P(SHARDS, None),
    )
    out_specs = (P(BATCH, SHARDS), P(SHARDS, BATCH))
    return jax.shard_map(
        per_device, mesh=split, in_specs=in_specs, out_specs=out_specs, check_vma=False
    )
```

```python
import functools
import math

import jax
import jax.numpy as jnp
from jax import lax
from jax.experimental import pallas as pl
from jax.experimental.pallas import tpu as pltpu
from jax.sharding import Mesh
from jax.sharding import PartitionSpec as P

SHARDS = ("tensor_0", "tensor_1", "latent")
BATCH = ("batch_0", "batch_1")
HALF = ("tensor_0", "latent")
OWNERS = ("tensor_0", "latent", "tensor_1")
OTHER_HALF = ("batch_0", "tensor_1")

epsilon = 1e-06

f32 = jnp.float32
bf16 = jnp.bfloat16
LAST = (((1,), (1,)), ((), ()))
WHOLE = pl.BlockSpec(memory_space=pltpu.VMEM)
LIMIT = 24 * 1024 * 1024


def exchange(pieces, axes):
    return lax.all_to_all(pieces, axes, split_axis=0, concat_axis=0, tiled=True)


def swap(block, axes):
    for_all = lax.axis_size(axes)
    return lax.ppermute(block, axes, [(i, for_all - 1 - i) for i in range(for_all)])


def copies_of_all(block):
    near = swap(block, BATCH[1])
    far = swap(block, BATCH[0])
    return [block, near, far, swap(far, BATCH[1])]


def blocks_of_all(block_at):
    own = lax.axis_index(BATCH)
    steps = ((1, BATCH[1]), (2, BATCH[0]), (3, BATCH))
    return [block_at(own)] + [swap(block_at(own ^ step), axes) for step, axes in steps]


def call(body, outs, flops, args, **more):
    arrays = [*args, *jax.tree.leaves(outs)]
    moved = sum(math.prod(a.shape) * jnp.dtype(a.dtype).itemsize for a in arrays)
    cost = pl.CostEstimate(flops=flops, bytes_accessed=moved, transcendentals=0)
    return pl.pallas_call(
        body,
        out_shape=outs,
        cost_estimate=cost,
        compiler_params=pltpu.CompilerParams(vmem_limit_bytes=LIMIT),
        **more,
    )(*args)


def array(shape, dtype=bf16):
    return jax.ShapeDtypeStruct(shape, dtype)


def hbm_array(shape, dtype=bf16):
    return pltpu.HBM(shape, dtype)


def in_hbm(value):
    return pltpu.with_memory_space_constraint(value, pltpu.HBM)


def product(left, right):
    return jnp.dot(left, right, preferred_element_type=f32)


def product_t(left, right):
    return lax.dot_general(left, right, LAST, preferred_element_type=f32)


def encode_kernel(centered_ref, weight_ref, bias_ref, latents_ref, turned_ref, rows_ref):
    width = centered_ref.shape[0]

    def finish(total):
        latents = jnp.maximum(total + bias_ref[...].astype(f32), 0.0).astype(bf16)
        latents_ref[...] = latents
        turned_ref[...] = latents.T

    @pl.when(pl.program_id(0) == 0)
    def _():
        total = None
        for at in range(0, width, 256):
            chunk = centered_ref[at : at + 256, :].T
            rows_ref[:, at : at + 256] = chunk
            term = product(chunk, weight_ref[at : at + 256, :])
            total = term if total is None else total + term
        finish(total)

    @pl.when(pl.program_id(0) > 0)
    def _():
        finish(product(rows_ref[...], weight_ref[...]))


def encode(centered, weight, bias, tile):
    width, tokens = centered.shape
    count = weight.shape[1]
    return call(
        encode_kernel,
        [array((tokens, count)), hbm_array((count, tokens))],
        2 * tokens * width * count,
        [centered, in_hbm(weight), bias.reshape(1, count)],
        grid=(count // tile,),
        in_specs=[
            pl.BlockSpec((width, tokens), lambda j: (0, 0)),
            pl.BlockSpec((width, tile), lambda j: (0, j)),
            pl.BlockSpec((1, tile), lambda j: (0, j)),
        ],
        out_specs=[
            pl.BlockSpec((tokens, tile), lambda j: (0, j)),
            pl.BlockSpec((tile, tokens), lambda j: (j, 0)),
        ],
        scratch_shapes=[pltpu.VMEM((tokens, width), bf16)],
    )


def gather_kernel(at_ref, *refs):
    *weights, out_ref, sems = refs
    count = out_ref.shape[1]
    at = pl.multiple_of(at_ref[0], count)
    copies = [
        pltpu.make_async_copy(w.at[pl.ds(at, count)], out_ref.at[k], sems.at[k])
        for k, w in enumerate(weights)
    ]
    for copy in copies:
        copy.start()
    arrive(copies)


def rows_of_each(weights, at, count):
    anywhere = pl.BlockSpec(memory_space=pl.ANY)
    return call(
        gather_kernel,
        hbm_array((len(weights), count, weights[0].shape[1])),
        0,
        [at.reshape(1), *map(in_hbm, weights)],
        in_specs=[pl.BlockSpec(memory_space=pltpu.SMEM)] + [anywhere] * len(weights),
        scratch_shapes=[pltpu.SemaphoreType.DMA((len(weights),))],
    )


def decode_kernel(latents_ref, weight_ref, target_ref, out_ref, held_ref, sems):
    tile = weight_ref.shape[1]
    step = pl.program_id(0)
    last = pl.num_programs(0) - 1
    rows, tokens = target_ref.shape
    spare = -rows % 128
    width = out_ref.shape[1] - rows - spare

    def to_out(at, size, k):
        span = pl.ds(at, size)
        return pltpu.make_async_copy(held_ref.at[:, span], out_ref.at[:, span], sems.at[k])

    @pl.when(step == 0)
    def _():
        padded = jnp.concatenate([target_ref[...], jnp.zeros((spare, tokens), bf16)], axis=0)
        held_ref[:, width:] = padded.T
        to_out(width, rows + spare, width // tile).start()

    at = pl.multiple_of(step * tile, tile)
    held_ref[:, pl.ds(at, tile)] = product(latents_ref[...], weight_ref[...]).astype(bf16)
    to_out(at, tile, step).start()

    @pl.when(step == last)
    def _():
        for k in range(width // tile):
            to_out(k * tile, tile, k).wait()
        to_out(width, rows + spare, width // tile).wait()


def decode(latents, weight, turned_target, room):
    tokens, count = latents.shape
    width = weight.shape[1]
    tile = width // 4
    return call(
        decode_kernel,
        hbm_array((tokens, width + room)),
        2 * tokens * width * count,
        [latents, weight, turned_target],
        grid=(width // tile,),
        in_specs=[WHOLE, pl.BlockSpec((count, tile), lambda j: (0, j)), WHOLE],
        out_specs=pl.BlockSpec(memory_space=pl.ANY),
        scratch_shapes=[
            pltpu.VMEM((tokens, width + room), bf16),
            pltpu.SemaphoreType.DMA((width // tile + 1,)),
        ],
    )


def total_of(pieces_ref, width):
    total = pieces_ref[0, :, :width].astype(f32)
    for k in range(1, pieces_ref.shape[0]):
        total += pieces_ref[k, :, :width].astype(f32)
    return total


def send_to_all(out_ref, rows):
    for k in range(out_ref.shape[0]):
        out_ref[k] = rows


def mean_of(values):
    return jnp.sum(values, axis=1, keepdims=True) / values.shape[1]


def halves_kernel(side_ref, pieces_ref, sum_ref, target_ref, sent_ref):
    rows, width = sum_ref.shape
    count = pieces_ref.shape[0]
    first = side_ref[0] == 0
    total = total_of(pieces_ref, width)
    sum_ref[...] = jnp.where(first, total[:rows], total[rows:])
    sent_ref[:, :width] = jnp.where(first, total[rows:], total[:rows]).astype(bf16)
    for k in range(count):
        piece = pieces_ref[k, :, width:].astype(f32)
        target_ref[k] = jnp.where(first, piece[:rows], piece[rows:]).astype(bf16)
        other = jnp.where(first, piece[rows:], piece[:rows]).astype(bf16)
        sent_ref[:, width + 128 * k : width + 128 * (k + 1)] = other


def recon_kernel(sum_ref, partner_ref, bias_ref, gain_ref, out_ref, recon_ref):
    partner = partner_ref[:, : recon_ref.shape[1]].astype(f32)
    recon = sum_ref[...] + partner + bias_ref[...].astype(f32)
    recon_ref[...] = recon
    scale_in = lax.rsqrt(mean_of(recon * recon) + epsilon)
    send_to_all(out_ref, (recon * scale_in * gain_ref[...].astype(f32)).astype(bf16))


def output_kernel(token_count, pieces_ref, recon_ref, target_ref, gain_ref, out_ref, grad_ref):
    gain = gain_ref[...].astype(f32)
    output = total_of(pieces_ref, recon_ref.shape[1])
    scale_out = lax.rsqrt(mean_of(output * output) + epsilon)
    normed_out = output * scale_out
    result = recon_ref[...] + normed_out * gain
    grad_result = 2.0 * (result - target_ref[...].astype(f32)) / token_count
    grad_ref[...] = grad_result
    grad_normed = grad_result * gain
    inner = mean_of(grad_normed * normed_out)
    send_to_all(out_ref, (scale_out * (grad_normed - normed_out * inner)).astype(bf16))


def input_kernel(pieces_ref, recon_ref, grad_ref, gain_ref, out_ref):
    recon = recon_ref[...]
    scale_in = lax.rsqrt(mean_of(recon * recon) + epsilon)
    unit = recon * scale_in
    grad_unit = total_of(pieces_ref, recon_ref.shape[1]) * gain_ref[...].astype(f32)
    inner = mean_of(grad_unit * unit)
    send_to_all(out_ref, (grad_ref[...] + scale_in * (grad_unit - unit * inner)).astype(bf16))


def local(body, outs, args, kept=0):
    stay = len(args) - kept
    args = [*args[:stay], *(in_hbm(a) for a in args[stay:])]
    return call(body, outs, 0, args, in_specs=[WHOLE] * stay + [pl.BlockSpec()] * kept)


def fetches(refs, weights_ref, sems, order):
    *own, near, far = refs
    units, more = own[0].shape[0], near.shape[1]
    copies = []
    for k in order:
        rows = weights_ref.at[k]
        pairs = [(own[k], rows.at[pl.ds(0, units)])]
        pairs += [(near.at[k], rows.at[pl.ds(units, more)])]
        pairs += [(far.at[k], rows.at[pl.ds(units + more, more)])]
        copies.append([pltpu.make_async_copy(*p, sems.at[k, i]) for i, p in enumerate(pairs)])
    for copy in sum(copies, []):
        copy.start()
    return copies


def arrive(copies):
    for copy in copies:
        copy.wait()


def forward_kernel(rows_ref, *refs):
    out_ref, gelu_ref, slope_ref, weights_ref, sems = refs[5:]
    root = 0.7978845608028654
    cube = 0.044715
    gate, up, down = fetches(refs[:5], weights_ref, sems, (0, 1, 2))
    rows = rows_ref[...]
    arrive(gate)
    gate_value = product_t(rows, weights_ref[0])
    arrive(up)
    up_value = product_t(rows, weights_ref[1])
    square = gate_value * gate_value
    curve = jnp.tanh(root * gate_value * (1.0 + cube * square))
    half = 0.5 * (1.0 + curve)
    gelu_value = gate_value * half
    rise = 0.5 * gate_value * (1.0 - curve * curve) * root * (1.0 + 3.0 * cube * square)
    gelu_ref[...] = gelu_value
    slope_ref[...] = up_value * (half + rise)
    hidden = (gelu_value * up_value).astype(bf16)
    arrive(down)
    for at in range(0, out_ref.shape[1], 512):
        span = slice(at, at + 512)
        out_ref[:, span] = product(hidden, weights_ref[2, :, span]).astype(bf16)


def backward_kernel(rows_ref, *refs):
    gelu_ref, slope_ref, out_ref, weights_ref, sems = refs[5:]
    down, gate, up = fetches(refs[:5], weights_ref, sems, (2, 0, 1))
    arrive(down)
    grad_hidden = product_t(rows_ref[...], weights_ref[2])
    grad_gate = (grad_hidden * slope_ref[...]).astype(bf16)
    grad_up = (grad_hidden * gelu_ref[...]).astype(bf16)
    grads = jnp.concatenate([grad_gate, grad_up], axis=1)
    arrive(gate)
    arrive(up)
    for at in range(0, out_ref.shape[1], 512):
        span = slice(at, at + 512)
        part = jnp.concatenate([weights_ref[0, :, span], weights_ref[1, :, span]], axis=0)
        out_ref[:, span] = product(grads, part).astype(bf16)


def with_weights(body, outs, rows, weights, near, far, saved=()):
    anywhere = pl.BlockSpec(memory_space=pl.ANY)
    units, width = weights[0].shape
    units += 2 * near.shape[1]
    return call(
        body,
        outs,
        6 * rows.shape[0] * width * units,
        [rows, *map(in_hbm, weights), in_hbm(near), far, *map(in_hbm, saved)],
        in_specs=[WHOLE] + [anywhere] * 5 + [pl.BlockSpec()] * len(saved),
        scratch_shapes=[pltpu.VMEM((3, units, width), bf16), pltpu.SemaphoreType.DMA((3, 3))],
    )


def latent_kernel(rows_ref, weight_ref, latents_ref, out_ref):
    grad_latent = product_t(rows_ref[...], weight_ref[...])
    out_ref[...] = jnp.where(latents_ref[...].astype(f32) > 0, grad_latent, 0.0).astype(bf16)


def grad_of_preact(rows, weight, latents, tile):
    tokens, width = rows.shape
    count = weight.shape[0]
    return call(
        latent_kernel,
        array((tokens, count)),
        2 * tokens * width * count,
        [rows, weight, latents],
        grid=(count // tile,),
        in_specs=[
            WHOLE,
            pl.BlockSpec((tile, width), lambda j: (j, 0)),
            pl.BlockSpec((tokens, tile), lambda j: (0, j)),
        ],
        out_specs=pl.BlockSpec((tokens, tile), lambda j: (0, j)),
    )


def products_kernel(tile, count, *refs):
    out_ref = refs[-1]
    left = jnp.concatenate([ref[...] for ref in refs[:count]], axis=1)
    first = pl.program_id(1) * tile
    for at in range(0, tile, 256):
        size = min(256, tile - at)
        columns = pl.ds(pl.multiple_of(first + at, 128), size)
        span = slice(at, at + size)
        right = jnp.concatenate([ref[:, columns] for ref in refs[count : 2 * count]], axis=0)
        total = product(left, right)
        if len(refs) > 2 * count + 1:
            rows = out_ref.shape[0]
            start = pl.multiple_of(pl.program_id(0) * rows, rows)
            total += refs[2 * count][pl.ds(start, rows), span]
        out_ref[:, span] = total.astype(out_ref.dtype)


def sum_of_products(left, right, tile, rows_tile=None, start=None, kind=bf16):
    rows, depth = left[0].shape
    columns = right[0].shape[1]
    rows_tile = rows_tile or rows
    count = len(left)
    out_spec = pl.BlockSpec((rows_tile, tile), lambda i, j: (i, j))
    return call(
        functools.partial(products_kernel, tile, count),
        array((rows, columns), kind),
        2 * rows * depth * columns * count,
        [*map(in_hbm, left), *right, *([] if start is None else [start])],
        grid=(rows // rows_tile, columns // tile),
        in_specs=[pl.BlockSpec((rows_tile, depth), lambda i, j: (i, 0))] * count
        + [WHOLE] * count
        + ([] if start is None else [WHOLE]),
        out_specs=out_spec,
    )


def per_device(
    residual,
    target,
    encoder_weight,
    encoder_bias,
    decoder_weight,
    decoder_bias,
    first_gain,
    second_gain,
    gate_weight,
    up_weight,
    down_weight,
):
    tokens, share_width = residual.shape
    shards = lax.axis_size(SHARDS)
    copies = lax.axis_size(BATCH)
    width = share_width * shards
    block = width // copies
    own_tokens = tokens // shards
    token_count = tokens * copies
    offset = lax.axis_index(SHARDS) * share_width
    bias, gain_in, gain_out = (a.reshape(1, width) for a in (decoder_bias, first_gain, second_gain))
    gate, up = gate_weight.T, up_weight.T
    everyone = array((shards, own_tokens, width))
    half = lax.axis_size(HALF)
    half_of_them = hbm_array((half, own_tokens, width))
    own_rows = array((own_tokens, width), f32)

    def to_owners(partial, axes):
        return exchange(partial.reshape(lax.axis_size(axes), own_tokens, -1), axes)

    def all_tokens(pieces, axes):
        return exchange(pieces, axes).reshape(-1, width)

    units = gate.shape[0] // 2
    at = lax.axis_index(BATCH[1]) * units
    weights = [gate, up, down_weight]

    bias_share = lax.dynamic_slice_in_dim(decoder_bias.astype(f32), offset, share_width)
    centered_share = (residual.astype(f32) - bias_share).astype(bf16).T
    pieces = jnp.broadcast_to(centered_share, (shards, share_width, tokens))
    pieces, weights_then = lax.optimization_barrier((pieces, weights))
    sent = rows_of_each(weights_then, at, units)
    near = swap(sent, OTHER_HALF)
    centered = exchange(pieces, SHARDS).reshape(width, tokens)

    latents, turned_latents = encode(centered, encoder_weight, encoder_bias, 512)
    partial_recon = decode(latents, decoder_weight, target.T, 128)

    partial_recon, centered, turned_latents = lax.optimization_barrier(
        (partial_recon, centered, turned_latents)
    )
    far_latents = swap(turned_latents, BATCH[0])
    centered_blocks = blocks_of_all(
        lambda b: lax.dynamic_slice_in_dim(centered, b * block, block, axis=0)
    )
    pieces = exchange(partial_recon.reshape(half, 2 * own_tokens, -1), HALF)
    side = lax.axis_index(SHARDS[1]).reshape(1)
    own_sum, own_targets, sent = call(
        halves_kernel,
        [
            array((own_tokens, width), f32),
            hbm_array((half, own_tokens, 128)),
            array((own_tokens, width + half * 128)),
        ],
        0,
        [side, pieces],
        in_specs=[pl.BlockSpec(memory_space=pltpu.SMEM), WHOLE],
    )
    sent, far_latents, centered_blocks[3] = lax.optimization_barrier(
        (sent, far_latents, centered_blocks[3])
    )
    partner = swap(sent, SHARDS[1])
    pieces, recon = local(
        recon_kernel, [half_of_them, own_rows], [own_sum, partner, bias, gain_in]
    )
    partner_targets = partner[:, width:].reshape(own_tokens, half, 128)
    targets = jnp.stack([jnp.moveaxis(own_targets, 0, 1), partner_targets], axis=2)
    targets = jnp.where(side[0] == 0, targets, jnp.flip(targets, 2))[..., :share_width]
    targets = targets.reshape(own_tokens, *(lax.axis_size(a) for a in OWNERS), share_width)
    own_target = jnp.swapaxes(targets, 2, 3).reshape(own_tokens, width)

    pieces, near = lax.optimization_barrier((pieces, near))
    far = swap(near, BATCH[1])
    normed_input = all_tokens(pieces, HALF)
    rows = half * own_tokens
    hidden = gate.shape[0] + 2 * units
    partial_out, *saved = with_weights(
        forward_kernel,
        [hbm_array((rows, width))] + [hbm_array((rows, hidden), f32)] * 2,
        normed_input,
        weights,
        near,
        far,
    )
    partial_out, centered_blocks[2] = lax.optimization_barrier((partial_out, centered_blocks[2]))

    pieces, grad_result = local(
        functools.partial(output_kernel, token_count),
        [half_of_them, own_rows],
        [to_owners(partial_out, HALF), recon, own_target, gain_out],
    )
    latent_blocks = [turned_latents, swap(turned_latents, BATCH[1])]
    latent_blocks += [far_latents, swap(far_latents, BATCH[1])]
    pieces, latent_blocks, centered_blocks[1] = lax.optimization_barrier(
        (pieces, latent_blocks, centered_blocks[1])
    )
    grad_output = all_tokens(pieces, HALF)
    partial_input = with_weights(
        backward_kernel, array((rows, width)), grad_output, weights, near, in_hbm(far), saved
    )
    (pieces,) = local(
        input_kernel, [everyone], [to_owners(partial_input, HALF), recon, grad_result, gain_in]
    )
    grad_recon = all_tokens(pieces, OWNERS)

    own = lax.axis_index(BATCH)
    recon_blocks = [
        lax.dynamic_slice_in_dim(grad_recon, (own ^ step) * block, block, axis=1)
        for step in range(copies)
    ]
    recon_blocks[2] = swap(recon_blocks[2], BATCH[0])
    recon_blocks[3] = swap(recon_blocks[3], BATCH)
    grad_preact = grad_of_preact(grad_recon, decoder_weight, latents, 512)
    far = swap(grad_preact, BATCH[0])
    far, near, recon_blocks[1] = lax.optimization_barrier((far, grad_preact, recon_blocks[1]))
    recon_blocks[1] = swap(recon_blocks[1], BATCH[1])
    preact_blocks = [grad_preact, swap(near, BATCH[1]), far, swap(far, BATCH[1])]
    part = sum_of_products(latent_blocks[:3], recon_blocks[:3], block, kind=f32)
    encoder_grad = sum_of_products(centered_blocks, preact_blocks, 512)
    part, encoder_grad = lax.optimization_barrier((part, encoder_grad))
    decoder_grad = sum_of_products(latent_blocks[3:], recon_blocks[3:], block, 512, part)
    return encoder_grad, decoder_grad


def solution(mesh):
    batch, latent = mesh.shape["batch"], mesh.shape["latent"]
    split = Mesh(
        mesh.devices.reshape(2, batch // 2, mesh.shape["tensor"] // 2, 2, latent),
        BATCH + SHARDS,
    )
    in_specs = (
        P(BATCH, SHARDS),
        P(BATCH, SHARDS),
        P(None, SHARDS),
        P(SHARDS),
        P(SHARDS, None),
        P(),
        P(),
        P(),
        P(None, SHARDS),
        P(None, SHARDS),
        P(SHARDS, None),
    )
    out_specs = (P(BATCH, SHARDS), P(SHARDS, BATCH))
    return jax.shard_map(
        per_device, mesh=split, in_specs=in_specs, out_specs=out_specs, check_vma=False
    )
```

```python
import functools
import math

import jax
import jax.numpy as jnp
from jax import lax
from jax.experimental import pallas as pl
from jax.experimental.pallas import tpu as pltpu
from jax.sharding import Mesh
from jax.sharding import PartitionSpec as P

SHARDS = ("tensor_0", "tensor_1", "latent")
BATCH = ("batch_0", "batch_1")
HALF = ("tensor_0", "latent")
OWNERS = ("tensor_0", "latent", "tensor_1")
OTHER_HALF = ("batch_0", "tensor_1")

epsilon = 1e-06

f32 = jnp.float32
bf16 = jnp.bfloat16
LAST = (((1,), (1,)), ((), ()))
WHOLE = pl.BlockSpec(memory_space=pltpu.VMEM)
LIMIT = 24 * 1024 * 1024


def exchange(pieces, axes):
    return lax.all_to_all(pieces, axes, split_axis=0, concat_axis=0, tiled=True)


def swap(block, axes):
    for_all = lax.axis_size(axes)
    return lax.ppermute(block, axes, [(i, for_all - 1 - i) for i in range(for_all)])


def copies_of_all(block):
    near = swap(block, BATCH[1])
    far = swap(block, BATCH[0])
    return [block, near, far, swap(far, BATCH[1])]


def blocks_of_all(block_at):
    own = lax.axis_index(BATCH)
    steps = ((1, BATCH[1]), (2, BATCH[0]), (3, BATCH))
    return [block_at(own)] + [swap(block_at(own ^ step), axes) for step, axes in steps]


def call(body, outs, flops, args, **more):
    arrays = [*args, *jax.tree.leaves(outs)]
    moved = sum(math.prod(a.shape) * jnp.dtype(a.dtype).itemsize for a in arrays)
    cost = pl.CostEstimate(flops=flops, bytes_accessed=moved, transcendentals=0)
    return pl.pallas_call(
        body,
        out_shape=outs,
        cost_estimate=cost,
        compiler_params=pltpu.CompilerParams(vmem_limit_bytes=LIMIT),
        **more,
    )(*args)


def array(shape, dtype=bf16):
    return jax.ShapeDtypeStruct(shape, dtype)


def hbm_array(shape, dtype=bf16):
    return pltpu.HBM(shape, dtype)


def in_hbm(value):
    return pltpu.with_memory_space_constraint(value, pltpu.HBM)


def product(left, right):
    return jnp.dot(left, right, preferred_element_type=f32)


def product_t(left, right):
    return lax.dot_general(left, right, LAST, preferred_element_type=f32)


def encode_kernel(centered_ref, weight_ref, bias_ref, latents_ref, turned_ref, rows_ref):
    width = centered_ref.shape[0]

    def finish(total):
        latents = jnp.maximum(total + bias_ref[...].astype(f32), 0.0).astype(bf16)
        latents_ref[...] = latents
        turned_ref[...] = latents.T

    @pl.when(pl.program_id(0) == 0)
    def _():
        total = None
        for at in range(0, width, 256):
            chunk = centered_ref[at : at + 256, :].T
            rows_ref[:, at : at + 256] = chunk
            term = product(chunk, weight_ref[at : at + 256, :])
            total = term if total is None else total + term
        finish(total)

    @pl.when(pl.program_id(0) > 0)
    def _():
        finish(product(rows_ref[...], weight_ref[...]))


def encode(centered, weight, bias, tile):
    width, tokens = centered.shape
    count = weight.shape[1]
    return call(
        encode_kernel,
        [array((tokens, count)), hbm_array((count, tokens))],
        2 * tokens * width * count,
        [centered, in_hbm(weight), bias.reshape(1, count)],
        grid=(count // tile,),
        in_specs=[
            pl.BlockSpec((width, tokens), lambda j: (0, 0)),
            pl.BlockSpec((width, tile), lambda j: (0, j)),
            pl.BlockSpec((1, tile), lambda j: (0, j)),
        ],
        out_specs=[
            pl.BlockSpec((tokens, tile), lambda j: (0, j)),
            pl.BlockSpec((tile, tokens), lambda j: (j, 0)),
        ],
        scratch_shapes=[pltpu.VMEM((tokens, width), bf16)],
    )


def gather_kernel(at_ref, *refs):
    *weights, out_ref, sems = refs
    count = out_ref.shape[1]
    at = pl.multiple_of(at_ref[0], count)
    copies = [
        pltpu.make_async_copy(w.at[pl.ds(at, count)], out_ref.at[k], sems.at[k])
        for k, w in enumerate(weights)
    ]
    for copy in copies:
        copy.start()
    arrive(copies)


def rows_of_each(weights, at, count):
    anywhere = pl.BlockSpec(memory_space=pl.ANY)
    return call(
        gather_kernel,
        hbm_array((len(weights), count, weights[0].shape[1])),
        0,
        [at.reshape(1), *map(in_hbm, weights)],
        in_specs=[pl.BlockSpec(memory_space=pltpu.SMEM)] + [anywhere] * len(weights),
        scratch_shapes=[pltpu.SemaphoreType.DMA((len(weights),))],
    )


def decode_kernel(latents_ref, weight_ref, target_ref, out_ref, held_ref, sems):
    tile = weight_ref.shape[1]
    step = pl.program_id(0)
    last = pl.num_programs(0) - 1
    rows, tokens = target_ref.shape
    spare = -rows % 128
    width = out_ref.shape[1] - rows - spare

    def to_out(at, size, k):
        span = pl.ds(at, size)
        return pltpu.make_async_copy(held_ref.at[:, span], out_ref.at[:, span], sems.at[k])

    @pl.when(step == 0)
    def _():
        padded = jnp.concatenate([target_ref[...], jnp.zeros((spare, tokens), bf16)], axis=0)
        held_ref[:, width:] = padded.T
        to_out(width, rows + spare, width // tile).start()

    at = pl.multiple_of(step * tile, tile)
    held_ref[:, pl.ds(at, tile)] = product(latents_ref[...], weight_ref[...]).astype(bf16)
    to_out(at, tile, step).start()

    @pl.when(step == last)
    def _():
        for k in range(width // tile):
            to_out(k * tile, tile, k).wait()
        to_out(width, rows + spare, width // tile).wait()


def decode(latents, weight, turned_target, room):
    tokens, count = latents.shape
    width = weight.shape[1]
    tile = width // 4
    return call(
        decode_kernel,
        hbm_array((tokens, width + room)),
        2 * tokens * width * count,
        [latents, weight, turned_target],
        grid=(width // tile,),
        in_specs=[WHOLE, pl.BlockSpec((count, tile), lambda j: (0, j)), WHOLE],
        out_specs=pl.BlockSpec(memory_space=pl.ANY),
        scratch_shapes=[
            pltpu.VMEM((tokens, width + room), bf16),
            pltpu.SemaphoreType.DMA((width // tile + 1,)),
        ],
    )


def total_of(pieces_ref, width):
    total = pieces_ref[0, :, :width].astype(f32)
    for k in range(1, pieces_ref.shape[0]):
        total += pieces_ref[k, :, :width].astype(f32)
    return total


def send_to_all(out_ref, rows):
    for k in range(out_ref.shape[0]):
        out_ref[k] = rows


def mean_of(values):
    return jnp.sum(values, axis=1, keepdims=True) / values.shape[1]


def halves_kernel(side_ref, pieces_ref, sum_ref, target_ref, sent_ref):
    rows, width = sum_ref.shape
    count = pieces_ref.shape[0]
    first = side_ref[0] == 0
    total = total_of(pieces_ref, width)
    sum_ref[...] = jnp.where(first, total[:rows], total[rows:])
    sent_ref[:, :width] = jnp.where(first, total[rows:], total[:rows]).astype(bf16)
    for k in range(count):
        piece = pieces_ref[k, :, width:].astype(f32)
        target_ref[k] = jnp.where(first, piece[:rows], piece[rows:]).astype(bf16)
        other = jnp.where(first, piece[rows:], piece[:rows]).astype(bf16)
        sent_ref[:, width + 128 * k : width + 128 * (k + 1)] = other


def recon_kernel(sum_ref, partner_ref, bias_ref, gain_ref, out_ref, recon_ref):
    partner = partner_ref[:, : recon_ref.shape[1]].astype(f32)
    recon = sum_ref[...] + partner + bias_ref[...].astype(f32)
    recon_ref[...] = recon
    scale_in = lax.rsqrt(mean_of(recon * recon) + epsilon)
    send_to_all(out_ref, (recon * scale_in * gain_ref[...].astype(f32)).astype(bf16))


def output_kernel(token_count, pieces_ref, recon_ref, target_ref, gain_ref, out_ref, grad_ref):
    gain = gain_ref[...].astype(f32)
    output = total_of(pieces_ref, recon_ref.shape[1])
    scale_out = lax.rsqrt(mean_of(output * output) + epsilon)
    normed_out = output * scale_out
    result = recon_ref[...] + normed_out * gain
    grad_result = 2.0 * (result - target_ref[...].astype(f32)) / token_count
    grad_ref[...] = grad_result
    grad_normed = grad_result * gain
    inner = mean_of(grad_normed * normed_out)
    send_to_all(out_ref, (scale_out * (grad_normed - normed_out * inner)).astype(bf16))


def input_kernel(pieces_ref, recon_ref, grad_ref, gain_ref, out_ref):
    recon = recon_ref[...]
    scale_in = lax.rsqrt(mean_of(recon * recon) + epsilon)
    unit = recon * scale_in
    grad_unit = total_of(pieces_ref, recon_ref.shape[1]) * gain_ref[...].astype(f32)
    inner = mean_of(grad_unit * unit)
    send_to_all(out_ref, (grad_ref[...] + scale_in * (grad_unit - unit * inner)).astype(bf16))


def local(body, outs, args, kept=0):
    stay = len(args) - kept
    args = [*args[:stay], *(in_hbm(a) for a in args[stay:])]
    return call(body, outs, 0, args, in_specs=[WHOLE] * stay + [pl.BlockSpec()] * kept)


def fetches(refs, weights_ref, sems, order):
    own, near, far = refs[:3], refs[3], refs[4:]
    units, more = own[0].shape[0], near.shape[1]
    copies = []
    for k in order:
        rows = weights_ref.at[k]
        pairs = [(own[k], rows.at[pl.ds(0, units)])]
        pairs += [(near.at[k], rows.at[pl.ds(units, more)])]
        pairs += [(far[k], rows.at[pl.ds(units + more, more)])]
        copies.append([pltpu.make_async_copy(*p, sems.at[k, i]) for i, p in enumerate(pairs)])
    for copy in sum(copies, []):
        copy.start()
    return copies


def arrive(copies):
    for copy in copies:
        copy.wait()


def forward_kernel(rows_ref, *refs):
    out_ref, gelu_ref, slope_ref, weights_ref, sems = refs[7:]
    root = 0.7978845608028654
    cube = 0.044715
    gate, up, down = fetches(refs[:7], weights_ref, sems, (0, 1, 2))
    rows = rows_ref[...]
    arrive(gate)
    gate_value = product_t(rows, weights_ref[0])
    arrive(up)
    up_value = product_t(rows, weights_ref[1])
    square = gate_value * gate_value
    curve = jnp.tanh(root * gate_value * (1.0 + cube * square))
    half = 0.5 * (1.0 + curve)
    gelu_value = gate_value * half
    rise = 0.5 * gate_value * (1.0 - curve * curve) * root * (1.0 + 3.0 * cube * square)
    gelu_ref[...] = gelu_value
    slope_ref[...] = up_value * (half + rise)
    hidden = (gelu_value * up_value).astype(bf16)
    arrive(down)
    for at in range(0, out_ref.shape[1], 512):
        span = slice(at, at + 512)
        out_ref[:, span] = product(hidden, weights_ref[2, :, span]).astype(bf16)


def backward_kernel(rows_ref, *refs):
    gelu_ref, slope_ref, out_ref, weights_ref, sems = refs[7:]
    down, gate, up = fetches(refs[:7], weights_ref, sems, (2, 0, 1))
    arrive(down)
    grad_hidden = product_t(rows_ref[...], weights_ref[2])
    grad_gate = (grad_hidden * slope_ref[...]).astype(bf16)
    grad_up = (grad_hidden * gelu_ref[...]).astype(bf16)
    grads = jnp.concatenate([grad_gate, grad_up], axis=1)
    arrive(gate)
    arrive(up)
    for at in range(0, out_ref.shape[1], 512):
        span = slice(at, at + 512)
        part = jnp.concatenate([weights_ref[0, :, span], weights_ref[1, :, span]], axis=0)
        out_ref[:, span] = product(grads, part).astype(bf16)


def with_weights(body, outs, rows, weights, near, far, saved=()):
    anywhere = pl.BlockSpec(memory_space=pl.ANY)
    units, width = weights[0].shape
    units += 2 * near.shape[1]
    return call(
        body,
        outs,
        6 * rows.shape[0] * width * units,
        [rows, *map(in_hbm, weights), in_hbm(near), *far, *map(in_hbm, saved)],
        in_specs=[WHOLE] + [anywhere] * 7 + [pl.BlockSpec()] * len(saved),
        scratch_shapes=[pltpu.VMEM((3, units, width), bf16), pltpu.SemaphoreType.DMA((3, 3))],
    )


def latent_kernel(rows_ref, weight_ref, latents_ref, out_ref):
    grad_latent = product_t(rows_ref[...], weight_ref[...])
    out_ref[...] = jnp.where(latents_ref[...].astype(f32) > 0, grad_latent, 0.0).astype(bf16)


def grad_of_preact(rows, weight, latents, tile):
    tokens, width = rows.shape
    count = weight.shape[0]
    return call(
        latent_kernel,
        array((tokens, count)),
        2 * tokens * width * count,
        [rows, weight, latents],
        grid=(count // tile,),
        in_specs=[
            WHOLE,
            pl.BlockSpec((tile, width), lambda j: (j, 0)),
            pl.BlockSpec((tokens, tile), lambda j: (0, j)),
        ],
        out_specs=pl.BlockSpec((tokens, tile), lambda j: (0, j)),
    )


def products_kernel(tile, count, *refs):
    out_ref = refs[-1]
    left = jnp.concatenate([ref[...] for ref in refs[:count]], axis=1)
    first = pl.program_id(1) * tile
    for at in range(0, tile, 256):
        size = min(256, tile - at)
        columns = pl.ds(pl.multiple_of(first + at, 128), size)
        span = slice(at, at + size)
        right = jnp.concatenate([ref[:, columns] for ref in refs[count : 2 * count]], axis=0)
        total = product(left, right)
        if len(refs) > 2 * count + 1:
            rows = out_ref.shape[0]
            start = pl.multiple_of(pl.program_id(0) * rows, rows)
            total += refs[2 * count][pl.ds(start, rows), span]
        out_ref[:, span] = total.astype(out_ref.dtype)


def sum_of_products(left, right, tile, rows_tile=None, start=None, kind=bf16):
    rows, depth = left[0].shape
    columns = right[0].shape[1]
    rows_tile = rows_tile or rows
    count = len(left)
    out_spec = pl.BlockSpec((rows_tile, tile), lambda i, j: (i, j))
    return call(
        functools.partial(products_kernel, tile, count),
        array((rows, columns), kind),
        2 * rows * depth * columns * count,
        [*map(in_hbm, left), *right, *([] if start is None else [start])],
        grid=(rows // rows_tile, columns // tile),
        in_specs=[pl.BlockSpec((rows_tile, depth), lambda i, j: (i, 0))] * count
        + [WHOLE] * count
        + ([] if start is None else [WHOLE]),
        out_specs=out_spec,
    )


def per_device(
    residual,
    target,
    encoder_weight,
    encoder_bias,
    decoder_weight,
    decoder_bias,
    first_gain,
    second_gain,
    gate_weight,
    up_weight,
    down_weight,
):
    tokens, share_width = residual.shape
    shards = lax.axis_size(SHARDS)
    copies = lax.axis_size(BATCH)
    width = share_width * shards
    block = width // copies
    own_tokens = tokens // shards
    token_count = tokens * copies
    offset = lax.axis_index(SHARDS) * share_width
    bias, gain_in, gain_out = (a.reshape(1, width) for a in (decoder_bias, first_gain, second_gain))
    gate, up = gate_weight.T, up_weight.T
    everyone = array((shards, own_tokens, width))
    half = lax.axis_size(HALF)
    half_of_them = hbm_array((half, own_tokens, width))
    own_rows = array((own_tokens, width), f32)

    def to_owners(partial, axes):
        return exchange(partial.reshape(lax.axis_size(axes), own_tokens, -1), axes)

    def all_tokens(pieces, axes):
        return exchange(pieces, axes).reshape(-1, width)

    units = gate.shape[0] // 2
    at = lax.axis_index(BATCH[1]) * units
    weights = [gate, up, down_weight]

    bias_share = lax.dynamic_slice_in_dim(decoder_bias.astype(f32), offset, share_width)
    centered_share = (residual.astype(f32) - bias_share).astype(bf16).T
    pieces = jnp.broadcast_to(centered_share, (shards, share_width, tokens))
    pieces, weights_then = lax.optimization_barrier((pieces, weights))
    sent = rows_of_each(weights_then, at, units)
    near = swap(sent, OTHER_HALF)
    centered = exchange(pieces, SHARDS).reshape(width, tokens)

    latents, turned_latents = encode(centered, encoder_weight, encoder_bias, 512)
    partial_recon = decode(latents, decoder_weight, target.T, 128)

    partial_recon, centered, turned_latents = lax.optimization_barrier(
        (partial_recon, centered, turned_latents)
    )
    far_latents = swap(turned_latents, BATCH[0])
    centered_blocks = blocks_of_all(
        lambda b: lax.dynamic_slice_in_dim(centered, b * block, block, axis=0)
    )
    pieces = exchange(partial_recon.reshape(half, 2 * own_tokens, -1), HALF)
    side = lax.axis_index(SHARDS[1]).reshape(1)
    own_sum, own_targets, sent = call(
        halves_kernel,
        [
            array((own_tokens, width), f32),
            hbm_array((half, own_tokens, 128)),
            array((own_tokens, width + half * 128)),
        ],
        0,
        [side, pieces],
        in_specs=[pl.BlockSpec(memory_space=pltpu.SMEM), WHOLE],
    )
    sent, far_latents, centered_blocks[3] = lax.optimization_barrier(
        (sent, far_latents, centered_blocks[3])
    )
    partner = swap(sent, SHARDS[1])
    pieces, recon = local(
        recon_kernel, [half_of_them, own_rows], [own_sum, partner, bias, gain_in]
    )
    partner_targets = partner[:, width:].reshape(own_tokens, half, 128)
    targets = jnp.stack([jnp.moveaxis(own_targets, 0, 1), partner_targets], axis=2)
    targets = jnp.where(side[0] == 0, targets, jnp.flip(targets, 2))[..., :share_width]
    targets = targets.reshape(own_tokens, *(lax.axis_size(a) for a in OWNERS), share_width)
    own_target = jnp.swapaxes(targets, 2, 3).reshape(own_tokens, width)

    _, near = lax.optimization_barrier((pieces, near))
    far = [swap(near[k], BATCH[1]) for k in range(len(weights))]
    normed_input = all_tokens(pieces, HALF)
    rows = half * own_tokens
    hidden = gate.shape[0] + 2 * units
    partial_out, *saved = with_weights(
        forward_kernel,
        [hbm_array((rows, width))] + [hbm_array((rows, hidden), f32)] * 2,
        normed_input,
        weights,
        near,
        far,
    )
    partial_out, centered_blocks[2] = lax.optimization_barrier((partial_out, centered_blocks[2]))

    pieces, grad_result = local(
        functools.partial(output_kernel, token_count),
        [half_of_them, own_rows],
        [to_owners(partial_out, HALF), recon, own_target, gain_out],
    )
    latent_blocks = [turned_latents, swap(turned_latents, BATCH[1])]
    latent_blocks += [far_latents, swap(far_latents, BATCH[1])]
    pieces, latent_blocks, centered_blocks[1] = lax.optimization_barrier(
        (pieces, latent_blocks, centered_blocks[1])
    )
    grad_output = all_tokens(pieces, HALF)
    partial_input = with_weights(
        backward_kernel, array((rows, width)), grad_output, weights, near, far, saved
    )
    (pieces,) = local(
        input_kernel, [everyone], [to_owners(partial_input, HALF), recon, grad_result, gain_in]
    )
    grad_recon = all_tokens(pieces, OWNERS)

    own = lax.axis_index(BATCH)
    recon_blocks = [
        lax.dynamic_slice_in_dim(grad_recon, (own ^ step) * block, block, axis=1)
        for step in range(copies)
    ]
    recon_blocks[2] = swap(recon_blocks[2], BATCH[0])
    recon_blocks[3] = swap(recon_blocks[3], BATCH)
    grad_preact = grad_of_preact(grad_recon, decoder_weight, latents, 512)
    far = swap(grad_preact, BATCH[0])
    far, near, recon_blocks[1] = lax.optimization_barrier((far, grad_preact, recon_blocks[1]))
    recon_blocks[1] = swap(recon_blocks[1], BATCH[1])
    preact_blocks = [grad_preact, swap(near, BATCH[1]), far, swap(far, BATCH[1])]
    part = sum_of_products(latent_blocks[:3], recon_blocks[:3], block, kind=f32)
    encoder_grad = sum_of_products(centered_blocks, preact_blocks, 512)
    part, encoder_grad = lax.optimization_barrier((part, encoder_grad))
    decoder_grad = sum_of_products(latent_blocks[3:], recon_blocks[3:], block, 512, part)
    return encoder_grad, decoder_grad


def solution(mesh):
    batch, latent = mesh.shape["batch"], mesh.shape["latent"]
    split = Mesh(
        mesh.devices.reshape(2, batch // 2, mesh.shape["tensor"] // 2, 2, latent),
        BATCH + SHARDS,
    )
    in_specs = (
        P(BATCH, SHARDS),
        P(BATCH, SHARDS),
        P(None, SHARDS),
        P(SHARDS),
        P(SHARDS, None),
        P(),
        P(),
        P(),
        P(None, SHARDS),
        P(None, SHARDS),
        P(SHARDS, None),
    )
    out_specs = (P(BATCH, SHARDS), P(SHARDS, BATCH))
    return jax.shard_map(
        per_device, mesh=split, in_specs=in_specs, out_specs=out_specs, check_vma=False
    )
```

```python
import functools
import math

import jax
import jax.numpy as jnp
from jax import lax
from jax.experimental import pallas as pl
from jax.experimental.pallas import tpu as pltpu
from jax.sharding import Mesh
from jax.sharding import PartitionSpec as P

SHARDS = ("tensor_0", "tensor_1", "latent")
BATCH = ("batch_0", "batch_1")
HALF = ("tensor_0", "latent")
OWNERS = ("tensor_0", "latent", "tensor_1")
OTHER_HALF = ("batch_0", "tensor_1")

epsilon = 1e-06

f32 = jnp.float32
bf16 = jnp.bfloat16
LAST = (((1,), (1,)), ((), ()))
WHOLE = pl.BlockSpec(memory_space=pltpu.VMEM)
LIMIT = 24 * 1024 * 1024


def exchange(pieces, axes):
    return lax.all_to_all(pieces, axes, split_axis=0, concat_axis=0, tiled=True)


def swap(block, axes):
    for_all = lax.axis_size(axes)
    return lax.ppermute(block, axes, [(i, for_all - 1 - i) for i in range(for_all)])


def copies_of_all(block):
    near = swap(block, BATCH[1])
    far = swap(block, BATCH[0])
    return [block, near, far, swap(far, BATCH[1])]


def blocks_of_all(block_at):
    own = lax.axis_index(BATCH)
    steps = ((1, BATCH[1]), (2, BATCH[0]), (3, BATCH))
    return [block_at(own)] + [swap(block_at(own ^ step), axes) for step, axes in steps]


def call(body, outs, flops, args, **more):
    arrays = [*args, *jax.tree.leaves(outs)]
    moved = sum(math.prod(a.shape) * jnp.dtype(a.dtype).itemsize for a in arrays)
    cost = pl.CostEstimate(flops=flops, bytes_accessed=moved, transcendentals=0)
    return pl.pallas_call(
        body,
        out_shape=outs,
        cost_estimate=cost,
        compiler_params=pltpu.CompilerParams(vmem_limit_bytes=LIMIT),
        **more,
    )(*args)


def array(shape, dtype=bf16):
    return jax.ShapeDtypeStruct(shape, dtype)


def hbm_array(shape, dtype=bf16):
    return pltpu.HBM(shape, dtype)


def in_hbm(value):
    return pltpu.with_memory_space_constraint(value, pltpu.HBM)


def product(left, right):
    return jnp.dot(left, right, preferred_element_type=f32)


def product_t(left, right):
    return lax.dot_general(left, right, LAST, preferred_element_type=f32)


def encode_kernel(centered_ref, weight_ref, bias_ref, latents_ref, turned_ref, rows_ref):
    width = centered_ref.shape[0]

    def finish(total):
        latents = jnp.maximum(total + bias_ref[...].astype(f32), 0.0).astype(bf16)
        latents_ref[...] = latents
        turned_ref[...] = latents.T

    @pl.when(pl.program_id(0) == 0)
    def _():
        total = None
        for at in range(0, width, 256):
            chunk = centered_ref[at : at + 256, :].T
            rows_ref[:, at : at + 256] = chunk
            term = product(chunk, weight_ref[at : at + 256, :])
            total = term if total is None else total + term
        finish(total)

    @pl.when(pl.program_id(0) > 0)
    def _():
        finish(product(rows_ref[...], weight_ref[...]))


def encode(centered, weight, bias, tile):
    width, tokens = centered.shape
    count = weight.shape[1]
    return call(
        encode_kernel,
        [array((tokens, count)), hbm_array((count, tokens))],
        2 * tokens * width * count,
        [centered, in_hbm(weight), bias.reshape(1, count)],
        grid=(count // tile,),
        in_specs=[
            pl.BlockSpec((width, tokens), lambda j: (0, 0)),
            pl.BlockSpec((width, tile), lambda j: (0, j)),
            pl.BlockSpec((1, tile), lambda j: (0, j)),
        ],
        out_specs=[
            pl.BlockSpec((tokens, tile), lambda j: (0, j)),
            pl.BlockSpec((tile, tokens), lambda j: (j, 0)),
        ],
        scratch_shapes=[pltpu.VMEM((tokens, width), bf16)],
    )


def gather_kernel(at_ref, *refs):
    *weights, out_ref, sems = refs
    count = out_ref.shape[1]
    at = pl.multiple_of(at_ref[0], count)
    copies = [
        pltpu.make_async_copy(w.at[pl.ds(at, count)], out_ref.at[k], sems.at[k])
        for k, w in enumerate(weights)
    ]
    for copy in copies:
        copy.start()
    arrive(copies)


def rows_of_each(weights, at, count):
    anywhere = pl.BlockSpec(memory_space=pl.ANY)
    return call(
        gather_kernel,
        hbm_array((len(weights), count, weights[0].shape[1])),
        0,
        [at.reshape(1), *map(in_hbm, weights)],
        in_specs=[pl.BlockSpec(memory_space=pltpu.SMEM)] + [anywhere] * len(weights),
        scratch_shapes=[pltpu.SemaphoreType.DMA((len(weights),))],
    )


def decode_kernel(latents_ref, weight_ref, target_ref, out_ref, held_ref, sems):
    tile = weight_ref.shape[1]
    step = pl.program_id(0)
    last = pl.num_programs(0) - 1
    rows, tokens = target_ref.shape
    spare = -rows % 128
    width = out_ref.shape[1] - rows - spare

    def to_out(at, size, k):
        span = pl.ds(at, size)
        return pltpu.make_async_copy(held_ref.at[:, span], out_ref.at[:, span], sems.at[k])

    @pl.when(step == 0)
    def _():
        padded = jnp.concatenate([target_ref[...], jnp.zeros((spare, tokens), bf16)], axis=0)
        held_ref[:, width:] = padded.T
        to_out(width, rows + spare, width // tile).start()

    at = pl.multiple_of(step * tile, tile)
    held_ref[:, pl.ds(at, tile)] = product(latents_ref[...], weight_ref[...]).astype(bf16)
    to_out(at, tile, step).start()

    @pl.when(step == last)
    def _():
        for k in range(width // tile):
            to_out(k * tile, tile, k).wait()
        to_out(width, rows + spare, width // tile).wait()


def decode(latents, weight, turned_target, room):
    tokens, count = latents.shape
    width = weight.shape[1]
    tile = width // 4
    return call(
        decode_kernel,
        hbm_array((tokens, width + room)),
        2 * tokens * width * count,
        [latents, weight, turned_target],
        grid=(width // tile,),
        in_specs=[WHOLE, pl.BlockSpec((count, tile), lambda j: (0, j)), WHOLE],
        out_specs=pl.BlockSpec(memory_space=pl.ANY),
        scratch_shapes=[
            pltpu.VMEM((tokens, width + room), bf16),
            pltpu.SemaphoreType.DMA((width // tile + 1,)),
        ],
    )


def total_of(pieces_ref, width):
    total = pieces_ref[0, :, :width].astype(f32)
    for k in range(1, pieces_ref.shape[0]):
        total += pieces_ref[k, :, :width].astype(f32)
    return total


def send_to_all(out_ref, rows):
    for k in range(out_ref.shape[0]):
        out_ref[k] = rows


def mean_of(values):
    return jnp.sum(values, axis=1, keepdims=True) / values.shape[1]


def halves_kernel(side_ref, pieces_ref, sum_ref, target_ref, sent_ref):
    rows, width = sum_ref.shape
    count = pieces_ref.shape[0]
    first = side_ref[0] == 0
    total = total_of(pieces_ref, width)
    sum_ref[...] = jnp.where(first, total[:rows], total[rows:])
    sent_ref[:, :width] = jnp.where(first, total[rows:], total[:rows]).astype(bf16)
    for k in range(count):
        piece = pieces_ref[k, :, width:].astype(f32)
        target_ref[k] = jnp.where(first, piece[:rows], piece[rows:]).astype(bf16)
        other = jnp.where(first, piece[rows:], piece[:rows]).astype(bf16)
        sent_ref[:, width + 128 * k : width + 128 * (k + 1)] = other


def recon_kernel(sum_ref, partner_ref, bias_ref, gain_ref, out_ref, recon_ref):
    partner = partner_ref[:, : recon_ref.shape[1]].astype(f32)
    recon = sum_ref[...] + partner + bias_ref[...].astype(f32)
    recon_ref[...] = recon
    scale_in = lax.rsqrt(mean_of(recon * recon) + epsilon)
    send_to_all(out_ref, (recon * scale_in * gain_ref[...].astype(f32)).astype(bf16))


def output_kernel(token_count, pieces_ref, recon_ref, target_ref, gain_ref, out_ref, grad_ref):
    gain = gain_ref[...].astype(f32)
    output = total_of(pieces_ref, recon_ref.shape[1])
    scale_out = lax.rsqrt(mean_of(output * output) + epsilon)
    normed_out = output * scale_out
    result = recon_ref[...] + normed_out * gain
    grad_result = 2.0 * (result - target_ref[...].astype(f32)) / token_count
    grad_ref[...] = grad_result
    grad_normed = grad_result * gain
    inner = mean_of(grad_normed * normed_out)
    send_to_all(out_ref, (scale_out * (grad_normed - normed_out * inner)).astype(bf16))


def input_kernel(pieces_ref, recon_ref, grad_ref, gain_ref, out_ref):
    recon = recon_ref[...]
    scale_in = lax.rsqrt(mean_of(recon * recon) + epsilon)
    unit = recon * scale_in
    grad_unit = total_of(pieces_ref, recon_ref.shape[1]) * gain_ref[...].astype(f32)
    inner = mean_of(grad_unit * unit)
    send_to_all(out_ref, (grad_ref[...] + scale_in * (grad_unit - unit * inner)).astype(bf16))


def local(body, outs, args, kept=0):
    stay = len(args) - kept
    args = [*args[:stay], *(in_hbm(a) for a in args[stay:])]
    return call(body, outs, 0, args, in_specs=[WHOLE] * stay + [pl.BlockSpec()] * kept)


def fetches(refs, weights_ref, sems, order):
    own, near, far = refs[:3], refs[3], refs[4:]
    units, more = own[0].shape[0], near.shape[1]
    copies = []
    for k in order:
        rows = weights_ref.at[k]
        pairs = [(own[k], rows.at[pl.ds(0, units)])]
        pairs += [(near.at[k], rows.at[pl.ds(units, more)])]
        pairs += [(far[k], rows.at[pl.ds(units + more, more)])]
        copies.append([pltpu.make_async_copy(*p, sems.at[k, i]) for i, p in enumerate(pairs)])
    for copy in sum(copies, []):
        copy.start()
    return copies


def arrive(copies):
    for copy in copies:
        copy.wait()


def forward_kernel(rows_ref, *refs):
    out_ref, gelu_ref, slope_ref, weights_ref, sems = refs[7:]
    root = 0.7978845608028654
    cube = 0.044715
    gate, up, down = fetches(refs[:7], weights_ref, sems, (0, 1, 2))
    rows = rows_ref[...]
    arrive(gate)
    gate_value = product_t(rows, weights_ref[0])
    arrive(up)
    up_value = product_t(rows, weights_ref[1])
    square = gate_value * gate_value
    curve = jnp.tanh(root * gate_value * (1.0 + cube * square))
    half = 0.5 * (1.0 + curve)
    gelu_value = gate_value * half
    rise = 0.5 * gate_value * (1.0 - curve * curve) * root * (1.0 + 3.0 * cube * square)
    gelu_ref[...] = gelu_value
    slope_ref[...] = up_value * (half + rise)
    hidden = (gelu_value * up_value).astype(bf16)
    arrive(down)
    for at in range(0, out_ref.shape[1], 512):
        span = slice(at, at + 512)
        out_ref[:, span] = product(hidden, weights_ref[2, :, span]).astype(bf16)


def backward_kernel(rows_ref, *refs):
    gelu_ref, slope_ref, out_ref, weights_ref, sems = refs[7:]
    down, gate, up = fetches(refs[:7], weights_ref, sems, (2, 0, 1))
    arrive(down)
    grad_hidden = product_t(rows_ref[...], weights_ref[2])
    grad_gate = (grad_hidden * slope_ref[...]).astype(bf16)
    grad_up = (grad_hidden * gelu_ref[...]).astype(bf16)
    grads = jnp.concatenate([grad_gate, grad_up], axis=1)
    arrive(gate)
    arrive(up)
    for at in range(0, out_ref.shape[1], 512):
        span = slice(at, at + 512)
        part = jnp.concatenate([weights_ref[0, :, span], weights_ref[1, :, span]], axis=0)
        out_ref[:, span] = product(grads, part).astype(bf16)


def with_weights(body, outs, rows, weights, near, far, saved=()):
    anywhere = pl.BlockSpec(memory_space=pl.ANY)
    units, width = weights[0].shape
    units += 2 * near.shape[1]
    return call(
        body,
        outs,
        6 * rows.shape[0] * width * units,
        [rows, *map(in_hbm, weights), in_hbm(near), *far, *map(in_hbm, saved)],
        in_specs=[WHOLE] + [anywhere] * 7 + [pl.BlockSpec()] * len(saved),
        scratch_shapes=[pltpu.VMEM((3, units, width), bf16), pltpu.SemaphoreType.DMA((3, 3))],
    )


def latent_kernel(rows_ref, weight_ref, latents_ref, out_ref):
    grad_latent = product_t(rows_ref[...], weight_ref[...])
    out_ref[...] = jnp.where(latents_ref[...].astype(f32) > 0, grad_latent, 0.0).astype(bf16)


def grad_of_preact(rows, weight, latents, tile):
    tokens, width = rows.shape
    count = weight.shape[0]
    return call(
        latent_kernel,
        array((tokens, count)),
        2 * tokens * width * count,
        [rows, weight, latents],
        grid=(count // tile,),
        in_specs=[
            WHOLE,
            pl.BlockSpec((tile, width), lambda j: (j, 0)),
            pl.BlockSpec((tokens, tile), lambda j: (0, j)),
        ],
        out_specs=pl.BlockSpec((tokens, tile), lambda j: (0, j)),
    )


def products_kernel(tile, count, *refs):
    out_ref = refs[-1]
    left = jnp.concatenate([ref[...] for ref in refs[:count]], axis=1)
    first = pl.program_id(1) * tile
    for at in range(0, tile, 256):
        size = min(256, tile - at)
        columns = pl.ds(pl.multiple_of(first + at, 128), size)
        span = slice(at, at + size)
        right = jnp.concatenate([ref[:, columns] for ref in refs[count : 2 * count]], axis=0)
        total = product(left, right)
        if len(refs) > 2 * count + 1:
            rows = out_ref.shape[0]
            start = pl.multiple_of(pl.program_id(0) * rows, rows)
            total += refs[2 * count][pl.ds(start, rows), span]
        out_ref[:, span] = total.astype(out_ref.dtype)


def sum_of_products(left, right, tile, rows_tile=None, start=None, kind=bf16):
    rows, depth = left[0].shape
    columns = right[0].shape[1]
    rows_tile = rows_tile or rows
    count = len(left)
    out_spec = pl.BlockSpec((rows_tile, tile), lambda i, j: (i, j))
    return call(
        functools.partial(products_kernel, tile, count),
        array((rows, columns), kind),
        2 * rows * depth * columns * count,
        [*map(in_hbm, left), *right, *([] if start is None else [start])],
        grid=(rows // rows_tile, columns // tile),
        in_specs=[pl.BlockSpec((rows_tile, depth), lambda i, j: (i, 0))] * count
        + [WHOLE] * count
        + ([] if start is None else [WHOLE]),
        out_specs=out_spec,
    )


def per_device(
    residual,
    target,
    encoder_weight,
    encoder_bias,
    decoder_weight,
    decoder_bias,
    first_gain,
    second_gain,
    gate_weight,
    up_weight,
    down_weight,
):
    tokens, share_width = residual.shape
    shards = lax.axis_size(SHARDS)
    copies = lax.axis_size(BATCH)
    width = share_width * shards
    block = width // copies
    own_tokens = tokens // shards
    token_count = tokens * copies
    offset = lax.axis_index(SHARDS) * share_width
    bias, gain_in, gain_out = (a.reshape(1, width) for a in (decoder_bias, first_gain, second_gain))
    gate, up = gate_weight.T, up_weight.T
    everyone = array((shards, own_tokens, width))
    half = lax.axis_size(HALF)
    half_of_them = hbm_array((half, own_tokens, width))
    own_rows = array((own_tokens, width), f32)

    def to_owners(partial, axes):
        return exchange(partial.reshape(lax.axis_size(axes), own_tokens, -1), axes)

    def all_tokens(pieces, axes):
        return exchange(pieces, axes).reshape(-1, width)

    units = gate.shape[0] // 2
    at = lax.axis_index(BATCH[1]) * units
    weights = [gate, up, down_weight]

    bias_share = lax.dynamic_slice_in_dim(decoder_bias.astype(f32), offset, share_width)
    centered_share = (residual.astype(f32) - bias_share).astype(bf16).T
    pieces = jnp.broadcast_to(centered_share, (shards, share_width, tokens))
    pieces, weights_then = lax.optimization_barrier((pieces, weights))
    sent = rows_of_each(weights_then, at, units)
    near = swap(sent, OTHER_HALF)
    centered = exchange(pieces, SHARDS).reshape(width, tokens)

    latents, turned_latents = encode(centered, encoder_weight, encoder_bias, 512)
    partial_recon = decode(latents, decoder_weight, target.T, 128)

    partial_recon, centered, turned_latents = lax.optimization_barrier(
        (partial_recon, centered, turned_latents)
    )
    far_latents = swap(turned_latents, BATCH[0])
    centered_blocks = blocks_of_all(
        lambda b: lax.dynamic_slice_in_dim(centered, b * block, block, axis=0)
    )
    pieces = exchange(partial_recon.reshape(half, 2 * own_tokens, -1), HALF)
    side = lax.axis_index(SHARDS[1]).reshape(1)
    own_sum, own_targets, sent = call(
        halves_kernel,
        [
            array((own_tokens, width), f32),
            hbm_array((half, own_tokens, 128)),
            array((own_tokens, width + half * 128)),
        ],
        0,
        [side, pieces],
        in_specs=[pl.BlockSpec(memory_space=pltpu.SMEM), WHOLE],
    )
    sent, far_latents = lax.optimization_barrier((sent, far_latents))
    partner = swap(sent, SHARDS[1])
    pieces, recon = local(
        recon_kernel, [half_of_them, own_rows], [own_sum, partner, bias, gain_in]
    )
    partner_targets = partner[:, width:].reshape(own_tokens, half, 128)
    targets = jnp.stack([jnp.moveaxis(own_targets, 0, 1), partner_targets], axis=2)
    targets = jnp.where(side[0] == 0, targets, jnp.flip(targets, 2))[..., :share_width]
    targets = targets.reshape(own_tokens, *(lax.axis_size(a) for a in OWNERS), share_width)
    own_target = jnp.swapaxes(targets, 2, 3).reshape(own_tokens, width)

    _, near = lax.optimization_barrier((pieces, near))
    far = [swap(near[k], BATCH[1]) for k in range(len(weights))]
    normed_input = all_tokens(pieces, HALF)
    rows = half * own_tokens
    hidden = gate.shape[0] + 2 * units
    partial_out, *saved = with_weights(
        forward_kernel,
        [hbm_array((rows, width))] + [hbm_array((rows, hidden), f32)] * 2,
        normed_input,
        weights,
        near,
        far,
    )
    partial_out, centered_blocks[2] = lax.optimization_barrier((partial_out, centered_blocks[2]))

    pieces, grad_result = local(
        functools.partial(output_kernel, token_count),
        [half_of_them, own_rows],
        [to_owners(partial_out, HALF), recon, own_target, gain_out],
    )
    latent_blocks = [turned_latents, swap(turned_latents, BATCH[1])]
    latent_blocks += [far_latents, swap(far_latents, BATCH[1])]
    pieces, latent_blocks, centered_blocks[1::2] = lax.optimization_barrier(
        (pieces, latent_blocks, centered_blocks[1::2])
    )
    grad_output = all_tokens(pieces, HALF)
    partial_input = with_weights(
        backward_kernel, array((rows, width)), grad_output, weights, near, far, saved
    )
    (pieces,) = local(
        input_kernel, [everyone], [to_owners(partial_input, HALF), recon, grad_result, gain_in]
    )
    grad_recon = all_tokens(pieces, OWNERS)

    own = lax.axis_index(BATCH)
    recon_blocks = [
        lax.dynamic_slice_in_dim(grad_recon, (own ^ step) * block, block, axis=1)
        for step in range(copies)
    ]
    recon_blocks[2] = swap(recon_blocks[2], BATCH[0])
    recon_blocks[3] = swap(recon_blocks[3], BATCH)
    grad_preact = grad_of_preact(grad_recon, decoder_weight, latents, 512)
    far = swap(grad_preact, BATCH[0])
    far, near, recon_blocks[1] = lax.optimization_barrier((far, grad_preact, recon_blocks[1]))
    recon_blocks[1] = swap(recon_blocks[1], BATCH[1])
    preact_blocks = [grad_preact, swap(near, BATCH[1]), far, swap(far, BATCH[1])]
    part = sum_of_products(latent_blocks[:3], recon_blocks[:3], block, kind=f32)
    encoder_grad = sum_of_products(centered_blocks, preact_blocks, 512)
    part, encoder_grad = lax.optimization_barrier((part, encoder_grad))
    decoder_grad = sum_of_products(latent_blocks[3:], recon_blocks[3:], block, 512, part)
    return encoder_grad, decoder_grad


def solution(mesh):
    batch, latent = mesh.shape["batch"], mesh.shape["latent"]
    split = Mesh(
        mesh.devices.reshape(2, batch // 2, mesh.shape["tensor"] // 2, 2, latent),
        BATCH + SHARDS,
    )
    in_specs = (
        P(BATCH, SHARDS),
        P(BATCH, SHARDS),
        P(None, SHARDS),
        P(SHARDS),
        P(SHARDS, None),
        P(),
        P(),
        P(),
        P(None, SHARDS),
        P(None, SHARDS),
        P(SHARDS, None),
    )
    out_specs = (P(BATCH, SHARDS), P(SHARDS, BATCH))
    return jax.shard_map(
        per_device, mesh=split, in_specs=in_specs, out_specs=out_specs, check_vma=False
    )
```

```python
import functools
import math

import jax
import jax.numpy as jnp
from jax import lax
from jax.experimental import pallas as pl
from jax.experimental.pallas import tpu as pltpu
from jax.sharding import Mesh
from jax.sharding import PartitionSpec as P

SHARDS = ("tensor_0", "tensor_1", "latent")
BATCH = ("batch_0", "batch_1")
HALF = ("tensor_0", "latent")
OWNERS = ("tensor_0", "latent", "tensor_1")
OTHER_HALF = ("batch_0", "tensor_1")

epsilon = 1e-06

f32 = jnp.float32
bf16 = jnp.bfloat16
LAST = (((1,), (1,)), ((), ()))
WHOLE = pl.BlockSpec(memory_space=pltpu.VMEM)
LIMIT = 24 * 1024 * 1024


def exchange(pieces, axes):
    return lax.all_to_all(pieces, axes, split_axis=0, concat_axis=0, tiled=True)


def swap(block, axes):
    for_all = lax.axis_size(axes)
    return lax.ppermute(block, axes, [(i, for_all - 1 - i) for i in range(for_all)])


def copies_of_all(block):
    near = swap(block, BATCH[1])
    far = swap(block, BATCH[0])
    return [block, near, far, swap(far, BATCH[1])]


def blocks_of_all(block_at):
    own = lax.axis_index(BATCH)
    steps = ((1, BATCH[1]), (2, BATCH[0]), (3, BATCH))
    return [block_at(own)] + [swap(block_at(own ^ step), axes) for step, axes in steps]


def call(body, outs, flops, args, **more):
    arrays = [*args, *jax.tree.leaves(outs)]
    moved = sum(math.prod(a.shape) * jnp.dtype(a.dtype).itemsize for a in arrays)
    cost = pl.CostEstimate(flops=flops, bytes_accessed=moved, transcendentals=0)
    return pl.pallas_call(
        body,
        out_shape=outs,
        cost_estimate=cost,
        compiler_params=pltpu.CompilerParams(vmem_limit_bytes=LIMIT),
        **more,
    )(*args)


def array(shape, dtype=bf16):
    return jax.ShapeDtypeStruct(shape, dtype)


def hbm_array(shape, dtype=bf16):
    return pltpu.HBM(shape, dtype)


def in_hbm(value):
    return pltpu.with_memory_space_constraint(value, pltpu.HBM)


def product(left, right):
    return jnp.dot(left, right, preferred_element_type=f32)


def product_t(left, right):
    return lax.dot_general(left, right, LAST, preferred_element_type=f32)


def encode_kernel(centered_ref, weight_ref, bias_ref, latents_ref, turned_ref, rows_ref):
    width = centered_ref.shape[0]

    def finish(total):
        latents = jnp.maximum(total + bias_ref[...].astype(f32), 0.0).astype(bf16)
        latents_ref[...] = latents
        turned_ref[...] = latents.T

    @pl.when(pl.program_id(0) == 0)
    def _():
        total = None
        for at in range(0, width, 256):
            chunk = centered_ref[at : at + 256, :].T
            rows_ref[:, at : at + 256] = chunk
            term = product(chunk, weight_ref[at : at + 256, :])
            total = term if total is None else total + term
        finish(total)

    @pl.when(pl.program_id(0) > 0)
    def _():
        finish(product(rows_ref[...], weight_ref[...]))


def encode(centered, weight, bias, tile):
    width, tokens = centered.shape
    count = weight.shape[1]
    return call(
        encode_kernel,
        [array((tokens, count)), hbm_array((count, tokens))],
        2 * tokens * width * count,
        [centered, in_hbm(weight), bias.reshape(1, count)],
        grid=(count // tile,),
        in_specs=[
            pl.BlockSpec((width, tokens), lambda j: (0, 0)),
            pl.BlockSpec((width, tile), lambda j: (0, j)),
            pl.BlockSpec((1, tile), lambda j: (0, j)),
        ],
        out_specs=[
            pl.BlockSpec((tokens, tile), lambda j: (0, j)),
            pl.BlockSpec((tile, tokens), lambda j: (j, 0)),
        ],
        scratch_shapes=[pltpu.VMEM((tokens, width), bf16)],
    )


def gather_kernel(at_ref, *refs):
    *weights, out_ref, sems = refs
    count = out_ref.shape[1]
    at = pl.multiple_of(at_ref[0], count)
    copies = [
        pltpu.make_async_copy(w.at[pl.ds(at, count)], out_ref.at[k], sems.at[k])
        for k, w in enumerate(weights)
    ]
    for copy in copies:
        copy.start()
    arrive(copies)


def rows_of_each(weights, at, count):
    anywhere = pl.BlockSpec(memory_space=pl.ANY)
    return call(
        gather_kernel,
        hbm_array((len(weights), count, weights[0].shape[1])),
        0,
        [at.reshape(1), *map(in_hbm, weights)],
        in_specs=[pl.BlockSpec(memory_space=pltpu.SMEM)] + [anywhere] * len(weights),
        scratch_shapes=[pltpu.SemaphoreType.DMA((len(weights),))],
    )


def decode_kernel(latents_ref, weight_ref, target_ref, out_ref, held_ref, sems):
    tile = weight_ref.shape[1]
    step = pl.program_id(0)
    last = pl.num_programs(0) - 1
    rows, tokens = target_ref.shape
    spare = -rows % 128
    width = out_ref.shape[1] - rows - spare

    def to_out(at, size, k):
        span = pl.ds(at, size)
        return pltpu.make_async_copy(held_ref.at[:, span], out_ref.at[:, span], sems.at[k])

    @pl.when(step == 0)
    def _():
        padded = jnp.concatenate([target_ref[...], jnp.zeros((spare, tokens), bf16)], axis=0)
        held_ref[:, width:] = padded.T
        to_out(width, rows + spare, width // tile).start()

    at = pl.multiple_of(step * tile, tile)
    held_ref[:, pl.ds(at, tile)] = product(latents_ref[...], weight_ref[...]).astype(bf16)
    to_out(at, tile, step).start()

    @pl.when(step == last)
    def _():
        for k in range(width // tile):
            to_out(k * tile, tile, k).wait()
        to_out(width, rows + spare, width // tile).wait()


def decode(latents, weight, turned_target, room):
    tokens, count = latents.shape
    width = weight.shape[1]
    tile = width // 4
    return call(
        decode_kernel,
        hbm_array((tokens, width + room)),
        2 * tokens * width * count,
        [latents, weight, turned_target],
        grid=(width // tile,),
        in_specs=[WHOLE, pl.BlockSpec((count, tile), lambda j: (0, j)), WHOLE],
        out_specs=pl.BlockSpec(memory_space=pl.ANY),
        scratch_shapes=[
            pltpu.VMEM((tokens, width + room), bf16),
            pltpu.SemaphoreType.DMA((width // tile + 1,)),
        ],
    )


def total_of(pieces_ref, width):
    total = pieces_ref[0, :, :width].astype(f32)
    for k in range(1, pieces_ref.shape[0]):
        total += pieces_ref[k, :, :width].astype(f32)
    return total


def send_to_all(out_ref, rows):
    for k in range(out_ref.shape[0]):
        out_ref[k] = rows


def mean_of(values):
    return jnp.sum(values, axis=1, keepdims=True) / values.shape[1]


def halves_kernel(side_ref, pieces_ref, sum_ref, target_ref, sent_ref):
    rows, width = sum_ref.shape
    count = pieces_ref.shape[0]
    first = side_ref[0] == 0
    total = total_of(pieces_ref, width)
    sum_ref[...] = jnp.where(first, total[:rows], total[rows:])
    sent_ref[:, :width] = jnp.where(first, total[rows:], total[:rows]).astype(bf16)
    for k in range(count):
        piece = pieces_ref[k, :, width:].astype(f32)
        target_ref[k] = jnp.where(first, piece[:rows], piece[rows:]).astype(bf16)
        other = jnp.where(first, piece[rows:], piece[:rows]).astype(bf16)
        sent_ref[:, width + 128 * k : width + 128 * (k + 1)] = other


def recon_kernel(sum_ref, partner_ref, bias_ref, gain_ref, out_ref, recon_ref):
    partner = partner_ref[:, : recon_ref.shape[1]].astype(f32)
    recon = sum_ref[...] + partner + bias_ref[...].astype(f32)
    recon_ref[...] = recon
    scale_in = lax.rsqrt(mean_of(recon * recon) + epsilon)
    send_to_all(out_ref, (recon * scale_in * gain_ref[...].astype(f32)).astype(bf16))


def output_kernel(token_count, pieces_ref, recon_ref, target_ref, gain_ref, out_ref, grad_ref):
    gain = gain_ref[...].astype(f32)
    output = total_of(pieces_ref, recon_ref.shape[1])
    scale_out = lax.rsqrt(mean_of(output * output) + epsilon)
    normed_out = output * scale_out
    result = recon_ref[...] + normed_out * gain
    grad_result = 2.0 * (result - target_ref[...].astype(f32)) / token_count
    grad_ref[...] = grad_result
    grad_normed = grad_result * gain
    inner = mean_of(grad_normed * normed_out)
    send_to_all(out_ref, (scale_out * (grad_normed - normed_out * inner)).astype(bf16))


def input_kernel(pieces_ref, recon_ref, grad_ref, gain_ref, out_ref):
    recon = recon_ref[...]
    scale_in = lax.rsqrt(mean_of(recon * recon) + epsilon)
    unit = recon * scale_in
    grad_unit = total_of(pieces_ref, recon_ref.shape[1]) * gain_ref[...].astype(f32)
    inner = mean_of(grad_unit * unit)
    send_to_all(out_ref, (grad_ref[...] + scale_in * (grad_unit - unit * inner)).astype(bf16))


def local(body, outs, args, kept=0):
    stay = len(args) - kept
    args = [*args[:stay], *(in_hbm(a) for a in args[stay:])]
    return call(body, outs, 0, args, in_specs=[WHOLE] * stay + [pl.BlockSpec()] * kept)


def fetches(refs, weights_ref, sems, order):
    own, near, far = refs[:3], refs[3], refs[4:]
    units, more = own[0].shape[0], near.shape[1]
    copies = []
    for k in order:
        rows = weights_ref.at[k]
        pairs = [(own[k], rows.at[pl.ds(0, units)])]
        pairs += [(near.at[k], rows.at[pl.ds(units, more)])]
        pairs += [(far[k], rows.at[pl.ds(units + more, more)])]
        copies.append([pltpu.make_async_copy(*p, sems.at[k, i]) for i, p in enumerate(pairs)])
    for copy in sum(copies, []):
        copy.start()
    return copies


def arrive(copies):
    for copy in copies:
        copy.wait()


def forward_kernel(rows_ref, *refs):
    out_ref, gelu_ref, slope_ref, weights_ref, sems = refs[7:]
    root = 0.7978845608028654
    cube = 0.044715
    gate, up, down = fetches(refs[:7], weights_ref, sems, (0, 1, 2))
    rows = rows_ref[...]
    arrive(gate)
    gate_value = product_t(rows, weights_ref[0])
    arrive(up)
    up_value = product_t(rows, weights_ref[1])
    square = gate_value * gate_value
    curve = jnp.tanh(root * gate_value * (1.0 + cube * square))
    half = 0.5 * (1.0 + curve)
    gelu_value = gate_value * half
    rise = 0.5 * gate_value * (1.0 - curve * curve) * root * (1.0 + 3.0 * cube * square)
    gelu_ref[...] = gelu_value
    slope_ref[...] = up_value * (half + rise)
    hidden = (gelu_value * up_value).astype(bf16)
    arrive(down)
    for at in range(0, out_ref.shape[1], 512):
        span = slice(at, at + 512)
        out_ref[:, span] = product(hidden, weights_ref[2, :, span]).astype(bf16)


def backward_kernel(rows_ref, *refs):
    gelu_ref, slope_ref, out_ref, weights_ref, sems = refs[7:]
    down, gate, up = fetches(refs[:7], weights_ref, sems, (2, 0, 1))
    arrive(down)
    grad_hidden = product_t(rows_ref[...], weights_ref[2])
    grad_gate = (grad_hidden * slope_ref[...]).astype(bf16)
    grad_up = (grad_hidden * gelu_ref[...]).astype(bf16)
    grads = jnp.concatenate([grad_gate, grad_up], axis=1)
    arrive(gate)
    arrive(up)
    for at in range(0, out_ref.shape[1], 512):
        span = slice(at, at + 512)
        part = jnp.concatenate([weights_ref[0, :, span], weights_ref[1, :, span]], axis=0)
        out_ref[:, span] = product(grads, part).astype(bf16)


def with_weights(body, outs, rows, weights, near, far, saved=()):
    anywhere = pl.BlockSpec(memory_space=pl.ANY)
    units, width = weights[0].shape
    units += 2 * near.shape[1]
    return call(
        body,
        outs,
        6 * rows.shape[0] * width * units,
        [rows, *map(in_hbm, weights), in_hbm(near), *far, *map(in_hbm, saved)],
        in_specs=[WHOLE] + [anywhere] * 7 + [pl.BlockSpec()] * len(saved),
        scratch_shapes=[pltpu.VMEM((3, units, width), bf16), pltpu.SemaphoreType.DMA((3, 3))],
    )


def latent_kernel(rows_ref, weight_ref, latents_ref, out_ref):
    grad_latent = product_t(rows_ref[...], weight_ref[...])
    out_ref[...] = jnp.where(latents_ref[...].astype(f32) > 0, grad_latent, 0.0).astype(bf16)


def grad_of_preact(rows, weight, latents, tile):
    tokens, width = rows.shape
    count = weight.shape[0]
    return call(
        latent_kernel,
        array((tokens, count)),
        2 * tokens * width * count,
        [rows, weight, latents],
        grid=(count // tile,),
        in_specs=[
            WHOLE,
            pl.BlockSpec((tile, width), lambda j: (j, 0)),
            pl.BlockSpec((tokens, tile), lambda j: (0, j)),
        ],
        out_specs=pl.BlockSpec((tokens, tile), lambda j: (0, j)),
    )


def products_kernel(tile, count, *refs):
    out_ref = refs[-1]
    left = jnp.concatenate([ref[...] for ref in refs[:count]], axis=1)
    first = pl.program_id(1) * tile
    for at in range(0, tile, 256):
        size = min(256, tile - at)
        columns = pl.ds(pl.multiple_of(first + at, 128), size)
        span = slice(at, at + size)
        right = jnp.concatenate([ref[:, columns] for ref in refs[count : 2 * count]], axis=0)
        total = product(left, right)
        if len(refs) > 2 * count + 1:
            rows = out_ref.shape[0]
            start = pl.multiple_of(pl.program_id(0) * rows, rows)
            total += refs[2 * count][pl.ds(start, rows), span]
        out_ref[:, span] = total.astype(out_ref.dtype)


def sum_of_products(left, right, tile, rows_tile=None, start=None, kind=bf16):
    rows, depth = left[0].shape
    columns = right[0].shape[1]
    rows_tile = rows_tile or rows
    count = len(left)
    out_spec = pl.BlockSpec((rows_tile, tile), lambda i, j: (i, j))
    return call(
        functools.partial(products_kernel, tile, count),
        array((rows, columns), kind),
        2 * rows * depth * columns * count,
        [*map(in_hbm, left), *right, *([] if start is None else [start])],
        grid=(rows // rows_tile, columns // tile),
        in_specs=[pl.BlockSpec((rows_tile, depth), lambda i, j: (i, 0))] * count
        + [WHOLE] * count
        + ([] if start is None else [WHOLE]),
        out_specs=out_spec,
    )


def per_device(
    residual,
    target,
    encoder_weight,
    encoder_bias,
    decoder_weight,
    decoder_bias,
    first_gain,
    second_gain,
    gate_weight,
    up_weight,
    down_weight,
):
    tokens, share_width = residual.shape
    shards = lax.axis_size(SHARDS)
    copies = lax.axis_size(BATCH)
    width = share_width * shards
    block = width // copies
    own_tokens = tokens // shards
    token_count = tokens * copies
    offset = lax.axis_index(SHARDS) * share_width
    bias, gain_in, gain_out = (a.reshape(1, width) for a in (decoder_bias, first_gain, second_gain))
    gate, up = gate_weight.T, up_weight.T
    everyone = array((shards, own_tokens, width))
    half = lax.axis_size(HALF)
    half_of_them = hbm_array((half, own_tokens, width))
    own_rows = array((own_tokens, width), f32)

    def to_owners(partial, axes):
        return exchange(partial.reshape(lax.axis_size(axes), own_tokens, -1), axes)

    def all_tokens(pieces, axes):
        return exchange(pieces, axes).reshape(-1, width)

    units = gate.shape[0] // 2
    at = lax.axis_index(BATCH[1]) * units
    weights = [gate, up, down_weight]

    bias_share = lax.dynamic_slice_in_dim(decoder_bias.astype(f32), offset, share_width)
    centered_share = (residual.astype(f32) - bias_share).astype(bf16).T
    pieces = jnp.broadcast_to(centered_share, (shards, share_width, tokens))
    pieces, weights_then = lax.optimization_barrier((pieces, weights))
    sent = rows_of_each(weights_then, at, units)
    near = swap(sent, OTHER_HALF)
    centered = exchange(pieces, SHARDS).reshape(width, tokens)

    latents, turned_latents = encode(centered, encoder_weight, encoder_bias, 512)
    partial_recon = decode(latents, decoder_weight, target.T, 128)

    partial_recon, centered, turned_latents = lax.optimization_barrier(
        (partial_recon, centered, turned_latents)
    )
    far_latents = swap(turned_latents, BATCH[0])
    centered_blocks = blocks_of_all(
        lambda b: lax.dynamic_slice_in_dim(centered, b * block, block, axis=0)
    )
    pieces = exchange(partial_recon.reshape(half, 2 * own_tokens, -1), HALF)
    side = lax.axis_index(SHARDS[1]).reshape(1)
    own_sum, own_targets, sent = call(
        halves_kernel,
        [
            array((own_tokens, width), f32),
            hbm_array((half, own_tokens, 128)),
            array((own_tokens, width + half * 128)),
        ],
        0,
        [side, pieces],
        in_specs=[pl.BlockSpec(memory_space=pltpu.SMEM), WHOLE],
    )
    sent, far_latents = lax.optimization_barrier((sent, far_latents))
    partner = swap(sent, SHARDS[1])
    partner, centered_blocks[3] = lax.optimization_barrier((partner, centered_blocks[3]))
    pieces, recon = local(
        recon_kernel, [half_of_them, own_rows], [own_sum, partner, bias, gain_in]
    )
    partner_targets = partner[:, width:].reshape(own_tokens, half, 128)
    targets = jnp.stack([jnp.moveaxis(own_targets, 0, 1), partner_targets], axis=2)
    targets = jnp.where(side[0] == 0, targets, jnp.flip(targets, 2))[..., :share_width]
    targets = targets.reshape(own_tokens, *(lax.axis_size(a) for a in OWNERS), share_width)
    own_target = jnp.swapaxes(targets, 2, 3).reshape(own_tokens, width)

    _, near = lax.optimization_barrier((pieces, near))
    far = [swap(near[k], BATCH[1]) for k in range(len(weights))]
    normed_input = all_tokens(pieces, HALF)
    rows = half * own_tokens
    hidden = gate.shape[0] + 2 * units
    partial_out, *saved = with_weights(
        forward_kernel,
        [hbm_array((rows, width))] + [hbm_array((rows, hidden), f32)] * 2,
        normed_input,
        weights,
        near,
        far,
    )
    partial_out, centered_blocks[2] = lax.optimization_barrier((partial_out, centered_blocks[2]))

    pieces, grad_result = local(
        functools.partial(output_kernel, token_count),
        [half_of_them, own_rows],
        [to_owners(partial_out, HALF), recon, own_target, gain_out],
    )
    latent_blocks = [turned_latents, swap(turned_latents, BATCH[1])]
    latent_blocks += [far_latents, swap(far_latents, BATCH[1])]
    pieces, latent_blocks, centered_blocks[1] = lax.optimization_barrier(
        (pieces, latent_blocks, centered_blocks[1])
    )
    grad_output = all_tokens(pieces, HALF)
    partial_input = with_weights(
        backward_kernel, array((rows, width)), grad_output, weights, near, far, saved
    )
    (pieces,) = local(
        input_kernel, [everyone], [to_owners(partial_input, HALF), recon, grad_result, gain_in]
    )
    grad_recon = all_tokens(pieces, OWNERS)

    own = lax.axis_index(BATCH)
    recon_blocks = [
        lax.dynamic_slice_in_dim(grad_recon, (own ^ step) * block, block, axis=1)
        for step in range(copies)
    ]
    recon_blocks[2] = swap(recon_blocks[2], BATCH[0])
    recon_blocks[3] = swap(recon_blocks[3], BATCH)
    grad_preact = grad_of_preact(grad_recon, decoder_weight, latents, 512)
    far = swap(grad_preact, BATCH[0])
    far, near, recon_blocks[1] = lax.optimization_barrier((far, grad_preact, recon_blocks[1]))
    recon_blocks[1] = swap(recon_blocks[1], BATCH[1])
    preact_blocks = [grad_preact, swap(near, BATCH[1]), far, swap(far, BATCH[1])]
    part = sum_of_products(latent_blocks[:3], recon_blocks[:3], block, kind=f32)
    encoder_grad = sum_of_products(centered_blocks, preact_blocks, 512)
    part, encoder_grad = lax.optimization_barrier((part, encoder_grad))
    decoder_grad = sum_of_products(latent_blocks[3:], recon_blocks[3:], block, 512, part)
    return encoder_grad, decoder_grad


def solution(mesh):
    batch, latent = mesh.shape["batch"], mesh.shape["latent"]
    split = Mesh(
        mesh.devices.reshape(2, batch // 2, mesh.shape["tensor"] // 2, 2, latent),
        BATCH + SHARDS,
    )
    in_specs = (
        P(BATCH, SHARDS),
        P(BATCH, SHARDS),
        P(None, SHARDS),
        P(SHARDS),
        P(SHARDS, None),
        P(),
        P(),
        P(),
        P(None, SHARDS),
        P(None, SHARDS),
        P(SHARDS, None),
    )
    out_specs = (P(BATCH, SHARDS), P(SHARDS, BATCH))
    return jax.shard_map(
        per_device, mesh=split, in_specs=in_specs, out_specs=out_specs, check_vma=False
    )
```
